32 devices in a mesh: fsdp: 8 (over z, y), rep: 4 (over x, core).
Axes of the slice: x: 2, y: 2, z: 4, core: 2. Of those that a mesh axis runs over, the one named last changes fastest.
Arguments:
- layer_input: bfloat16 [64, 512, 768], P(('fsdp', 'rep')), may hold values from -6 to 6
- segment_ids: int32 [64, 512], P(('fsdp', 'rep')), may hold values from 0 to 511, as said below
- joint_weight: bfloat16 [768, 2304], P('fsdp'), may hold values from -0.21875 to 0.21875
- query_bias: bfloat16 [768], replicated, may hold values from -3 to 3
- value_bias: bfloat16 [768], replicated, may hold values from -3 to 3
- close_weight: bfloat16 [768, 768], P('fsdp'), may hold values from -0.875 to 0.875
- close_bias: bfloat16 [768], replicated, may hold values from -3 to 3
- first_gain: bfloat16 [768], replicated, may hold values from 0.099609375 to 1.8984375
- first_shift: bfloat16 [768], replicated, may hold values from -3 to 3
- expand_weight: bfloat16 [768, 3072], P('fsdp'), may hold values from -0.21875 to 0.21875
- expand_bias: bfloat16 [3072], replicated, may hold values from -3 to 3
- shrink_weight: bfloat16 [3072, 768], P('fsdp'), may hold values from -0.109375 to 0.109375
- shrink_bias: bfloat16 [768], replicated, may hold values from -3 to 3
- second_gain: bfloat16 [768], replicated, may hold values from 0.099609375 to 1.8984375
- second_shift: bfloat16 [768], replicated, may hold values from -3 to 3
- cotangent: bfloat16 [64, 512, 768], P(('fsdp', 'rep')), may hold values from -6 to 6
Outputs:
- layer_output: bfloat16 [64, 512, 768], P(('fsdp', 'rep'))
- input_grad: float32 [64, 512, 768], P(('fsdp', 'rep'))
- joint_grad: float32 [768, 2304], P('fsdp')
- query_bias_grad: float32 [768], replicated
- value_bias_grad: float32 [768], replicated
- close_grad: float32 [768, 768], P('fsdp')
- close_bias_grad: float32 [768], replicated
- first_gain_grad: float32 [768], replicated
- first_shift_grad: float32 [768], replicated
- expand_grad: float32 [768, 3072], P('fsdp')
- expand_bias_grad: float32 [3072], replicated
- shrink_grad: float32 [3072, 768], P('fsdp')
- shrink_bias_grad: float32 [768], replicated
- second_gain_grad: float32 [768], replicated
- second_shift_grad: float32 [768], replicated
The draws below stay inside these ranges and needn't reach their ends.
Inputs may be any that keep to these rules, and one draw needn't show every extreme that they name: `segment_ids`: along each packed row of 512 positions the document numbers start at 0, never fall and rise by at most one from a position to the next; every position belongs to a document. Some row holds 512 documents of one position.
All inputs are finite; a program needn't handle non-finite values.
Results may differ from the reference program's by a relative error of at most 0.015.
Values may be sent and summed in bfloat16 or wider, within the bound.
No kernel may reach another device: no remote copies, remote signals or barrier semaphores. Data moves between devices by JAX's collectives and lax.ppermute only.
A program may use at most 192 MiB of HBM per device.

```python
import math
import jax
import jax.numpy as jnp
from jax import lax

D = 768
HEADS = 12
HEAD = 64
FF = 3072
SEQ = 512
ROWS = 64


def draw_segment_ids(key, part):
    key_rate, key_cut = jax.random.split(jax.random.fold_in(key, 17))
    power = jax.random.randint(key_rate, (ROWS, 1), 1, 9)
    first_row = jnp.arange(ROWS, dtype=jnp.int32)[:, None] == 0
    power = jnp.where(first_row, jnp.zeros_like(power), power)
    period = jnp.left_shift(jnp.ones_like(power), power)
    ticket = jax.random.randint(key_cut, (ROWS, SEQ), 0, 1048576)
    position = jnp.arange(SEQ, dtype=jnp.int32)[None, :]
    boundary = jnp.logical_and(ticket % period == 0, position > 0)
    return jnp.cumsum(boundary.astype(jnp.int32), axis=1).astype(jnp.int32)


def block_scale(stream_key, shape, pieces, smallest, high):
    level = 1.0
    for dim, shards_of in pieces:
        heights = jax.random.uniform(jax.random.fold_in(jax.random.fold_in(stream_key, 6), dim), (shards_of,), jnp.float32, smallest / len(pieces), high / len(pieces))
        level = level * jnp.repeat(jnp.exp(heights), shape[dim] // shards_of).reshape((-1,) + (1,) * (len(shape) - 1 - dim))
    return level


def normal_values(key, dims, width, most, shards=(), kind=jnp.bfloat16):
    level = block_scale(key, dims, shards, -0.22, 0.18) if shards else 1.0
    array = jax.random.normal(key, dims, jnp.float32) * width * level
    return jnp.minimum(jnp.maximum(array, -most), most).astype(kind)


def setup_inputs(seed: int = 0) -> dict:
    splits = jax.random.split(jax.random.key(seed), 17)
    return {
        "layer_input": normal_values(splits[0], (ROWS, SEQ, D), 1.0, 6.0, ((0, 32),)),
        "segment_ids": draw_segment_ids(jax.random.fold_in(splits[16], 71), 0),
        "joint_weight": normal_values(splits[2], (D, 3 * D), D ** -0.5, 0.21875, ((0, 8),)),
        "query_bias": normal_values(splits[3], (D,), 0.5, 3.0),
        "value_bias": normal_values(splits[4], (D,), 0.5, 3.0),
        "close_weight": normal_values(splits[5], (D, D), (D // 16) ** -0.5, 0.875, ((0, 8),)),
        "close_bias": normal_values(splits[6], (D,), 0.5, 3.0),
        "first_gain": jnp.clip(1.0 + 0.18 * jax.random.normal(splits[7], (D,), jnp.float32), 0.099609375, 1.8984375).astype(jnp.bfloat16),
        "first_shift": normal_values(splits[8], (D,), 0.5, 3.0),
        "expand_weight": normal_values(splits[9], (D, FF), D ** -0.5, 0.21875, ((0, 8),)),
        "expand_bias": normal_values(splits[10], (FF,), 0.5, 3.0),
        "shrink_weight": normal_values(splits[11], (FF, D), FF ** -0.5, 0.109375, ((0, 8),)),
        "shrink_bias": normal_values(splits[12], (D,), 0.5, 3.0),
        "second_gain": jnp.clip(1.0 + 0.18 * jax.random.normal(splits[13], (D,), jnp.float32), 0.099609375, 1.8984375).astype(jnp.bfloat16),
        "second_shift": normal_values(splits[14], (D,), 0.5, 3.0),
        "cotangent": normal_values(splits[15], (ROWS, SEQ, D), 1.0, 6.0, ((0, 32),)),
    }


EPS = 1e-12
HIGH = lax.Precision.HIGHEST

@jax.custom_vjp
def low(v):
    return lax.optimization_barrier(v.astype(jnp.bfloat16)).astype(jnp.float32)

@jax.custom_vjp
def low_back(v):
    return v

def low_keep(v):
    return (low(v), None)

def low_pass(kept, grad):
    return (grad,)

def back_keep(v):
    return (v, None)

def back_low(kept, grad):
    return (low(grad),)
low.defvjp(low_keep, low_pass)
low_back.defvjp(back_keep, back_low)

def both_ways(values):
    return low(low_back(values))

def layer_norm(values, gain, shift):
    average = lax.optimization_barrier(jnp.mean(values, axis=-1, keepdims=True))
    centred = values - average
    variance = lax.optimization_barrier(jnp.mean(centred * centred, axis=-1, keepdims=True))
    return centred * lax.rsqrt(variance + EPS) * gain + shift

def reference(layer_input, segment_ids, joint_weight, query_bias, value_bias, close_weight, close_bias, first_gain, first_shift, expand_weight, expand_bias, shrink_weight, shrink_bias, second_gain, second_shift, cotangent):
    group = math.gcd(ROWS, 8)
    blocks = ROWS // group
    score_scale = 1.0 / math.sqrt(HEAD)
    seg_blocks = segment_ids.reshape(blocks, group, SEQ)

    def forward(inputs, joint, qbias, vbias, close, cbias, gain_one, shift_one, expand, ebias, shrink, sbias, gain_two, shift_two):
        joint_bias = jnp.concatenate([qbias, jnp.zeros_like(qbias), vbias])

        def block(packet):
            rows_in, segments = packet
            mixed = both_ways(jnp.einsum('rsd,de->rse', rows_in, joint, precision=HIGH) + joint_bias)
            queries = mixed[..., :D].reshape(group, SEQ, HEADS, HEAD)
            keys_part = mixed[..., D:2 * D].reshape(group, SEQ, HEADS, HEAD)
            values_part = mixed[..., 2 * D:].reshape(group, SEQ, HEADS, HEAD)
            scores = low_back(score_scale * jnp.einsum('rqhd,rkhd->rhqk', queries, keys_part, precision=HIGH))
            same_doc = segments[:, None, :, None] == segments[:, None, None, :]
            scores = jnp.where(same_doc, scores, -jnp.inf)
            attn_low = low(jax.nn.softmax(scores, axis=-1))
            context = jnp.einsum('rhqk,rkhd->rqhd', attn_low, values_part, precision=HIGH).reshape(group, SEQ, D)
            context = both_ways(context)
            branch = low_back(jnp.einsum('rsd,de->rse', context, close, precision=HIGH) + cbias)
            hidden = layer_norm(rows_in + branch, gain_one, shift_one)
            inner = low_back(jnp.einsum('rsd,df->rsf', low(hidden), expand, precision=HIGH) + ebias)
            active = low(jax.nn.gelu(inner, approximate=False))
            ffn_out = low_back(jnp.einsum('rsf,fd->rsd', active, shrink, precision=HIGH) + sbias)
            return layer_norm(hidden + ffn_out, gain_two, shift_two)
        outputs = lax.map(jax.checkpoint(block), (inputs.reshape(blocks, group, SEQ, D), seg_blocks))
        return outputs.reshape(ROWS, SEQ, D)
    floats = [item_value.astype(jnp.float32) for item_value in (layer_input, joint_weight, query_bias, value_bias, close_weight, close_bias, first_gain, first_shift, expand_weight, expand_bias, shrink_weight, shrink_bias, second_gain, second_shift)]
    output, pull = jax.vjp(forward, *floats)
    grads = pull(cotangent.astype(jnp.float32))
    return (output.astype(jnp.bfloat16), grads[0], grads[1], grads[2], grads[3], grads[4], grads[5], grads[6], grads[7], grads[8], grads[9], grads[10], grads[11], grads[12], grads[13])
```

```python
import functools
import math

import jax
import jax.numpy as jnp
from jax import lax
from jax.experimental import pallas as pl
from jax.experimental.pallas import tpu as pltpu
from jax.sharding import PartitionSpec as P

HEADS = 12


EPS = 1e-12


def layer_norm(values, gain, shift):
    average = jnp.mean(values, axis=-1, keepdims=True)
    centred = values - average
    variance = jnp.mean(centred * centred, axis=-1, keepdims=True)
    return centred * lax.rsqrt(variance + EPS) * gain + shift


def gelu_exact(values):
    return jax.nn.gelu(values, approximate=False)


def split_heads(packed):
    pos_count = packed.shape[0]
    model_width = packed.shape[1] // 3
    head_size = model_width // HEADS
    queries = packed[:, :model_width].reshape(pos_count, HEADS, head_size)
    keys_part = packed[:, model_width : 2 * model_width].reshape(pos_count, HEADS, head_size)
    values_part = packed[:, 2 * model_width :].reshape(pos_count, HEADS, head_size)
    return (queries, keys_part, values_part, 1.0 / math.sqrt(head_size))


def masked_scores(queries, keys_part, segments, score_scale):
    scores = (
        jnp.einsum("qhd,khd->hqk", queries, keys_part, preferred_element_type=jnp.float32)
        * score_scale
    )
    same_doc = segments[:, None] == segments[None, :]
    return jnp.where(same_doc[None], scores, -jnp.inf)


def attend_row(packed, segments):
    queries, keys_part, values_part, score_scale = split_heads(packed)
    scores = masked_scores(queries, keys_part, segments, score_scale)
    top_score = jnp.max(scores, axis=-1, keepdims=True)
    raised = jnp.exp(scores - top_score)
    denominator = jnp.sum(raised, axis=-1, keepdims=True)
    attn_low = (raised / denominator).astype(jnp.bfloat16)
    context = jnp.einsum("hqk,khd->qhd", attn_low, values_part, preferred_element_type=jnp.float32)
    return (
        context.reshape(packed.shape[0], packed.shape[1] // 3),
        top_score + jnp.log(denominator),
    )


def attend_back(packed, segments, log_total, grad_context):
    pos_count = packed.shape[0]
    model_width = packed.shape[1] // 3
    queries, keys_part, values_part, score_scale = split_heads(packed)
    scores = masked_scores(queries, keys_part, segments, score_scale)
    attn_weights = jnp.exp(scores - log_total)
    grad_heads = grad_context.reshape(pos_count, HEADS, model_width // HEADS)
    grad_attn = jnp.einsum(
        "qhd,khd->hqk", grad_heads, values_part, preferred_element_type=jnp.float32
    )
    inner_sum = jnp.sum(grad_attn * attn_weights, axis=-1, keepdims=True)
    grad_scores = (attn_weights * (grad_attn - inner_sum)).astype(jnp.bfloat16)
    grad_queries = (
        jnp.einsum("hqk,khd->qhd", grad_scores, keys_part, preferred_element_type=jnp.float32)
        * score_scale
    )
    grad_keys = (
        jnp.einsum("hqk,qhd->khd", grad_scores, queries, preferred_element_type=jnp.float32)
        * score_scale
    )
    grad_values = jnp.einsum(
        "hqk,qhd->khd",
        attn_weights.astype(jnp.bfloat16),
        grad_heads,
        preferred_element_type=jnp.float32,
    )
    return jnp.concatenate(
        [
            grad_queries.reshape(pos_count, model_width),
            grad_keys.reshape(pos_count, model_width),
            grad_values.reshape(pos_count, model_width),
        ],
        axis=1,
    )


AXES = ("fsdp", "rep")
WIDE = 768
HALF = 384


def swap(value, mask, total):
    return lax.ppermute(value, AXES, [(i, i ^ mask) for i in range(total)])


def pick(flag, first, second):
    return jnp.where(flag, second, first)


def assemble_kernel(meta_ref, *refs):
    out_ref = refs[-1]
    fsdp_count, piece_rows = refs[0].shape[0], refs[0].shape[1]
    for place in range(4):
        x_here = meta_ref[1] ^ (place & 1)
        c_here = meta_ref[2] ^ (place >> 1)
        row = pl.multiple_of(x_here * piece_rows, piece_rows)
        col = pl.multiple_of(c_here * HALF, 128)
        for j in range(fsdp_count):
            out_ref[meta_ref[0] ^ rel_shard(j, fsdp_count), pl.ds(row, piece_rows), pl.ds(col, HALF)] = refs[place][j]


def rel_shard(j, fsdp_count):
    bits = fsdp_count.bit_length() - 1
    return sum(((j >> b) & 1) << (bits - 1 - b) for b in range(bits))


def assemble(pieces, meta, by_rows):
    fsdp_count, planes, piece_rows, _ = pieces[0].shape
    shard_rows = 2 * piece_rows
    if by_rows:
        shape = (fsdp_count, planes * shard_rows, WIDE)
        out_spec = pl.BlockSpec((fsdp_count, shard_rows, WIDE), lambda p, m: (0, p, 0))
    else:
        shape = (fsdp_count, shard_rows, planes * WIDE)
        out_spec = pl.BlockSpec((fsdp_count, shard_rows, WIDE), lambda p, m: (0, 0, p))
    full = pl.pallas_call(
        assemble_kernel,
        out_shape=jax.ShapeDtypeStruct(shape, jnp.bfloat16),
        grid_spec=pltpu.PrefetchScalarGridSpec(
            num_scalar_prefetch=1,
            grid=(planes,),
            in_specs=[
                pl.BlockSpec((fsdp_count, pl.Squeezed(), piece_rows, HALF), lambda p, m: (0, p, 0, 0))
            ]
            * 4,
            out_specs=out_spec,
        ),
        cost_estimate=pl.CostEstimate(
            flops=0, bytes_accessed=4 * math.prod(shape), transcendentals=0
        ),
        name="assemble",
    )(meta, *pieces)
    return full.reshape(-1, shape[2])


def assemble_plain(pieces, meta, by_rows):
    fsdp_count, planes, piece_rows, _ = pieces[0].shape
    order = meta[0] ^ jnp.array([rel_shard(j, fsdp_count) for j in range(fsdp_count)])
    place = jnp.zeros_like(order).at[order].set(jnp.arange(fsdp_count))
    ordered = [jnp.take(p, place, axis=0) for p in pieces]
    halves = []
    for c in range(2):
        near = [pick(meta[2] != c, ordered[0], ordered[2]), pick(meta[2] != c, ordered[1], ordered[3])]
        halves.append(
            jnp.concatenate(
                [pick(meta[1] == 1, near[0], near[1]), pick(meta[1] == 1, near[1], near[0])], axis=2
            )
        )
    full = jnp.concatenate(halves, axis=3)
    if by_rows:
        return full.reshape(fsdp_count * planes * 2 * piece_rows, WIDE)
    return full.transpose(0, 2, 1, 3).reshape(fsdp_count * 2 * piece_rows, planes * WIDE)


def own_piece(shard, meta, by_rows):
    if by_rows:
        planes = D_SPLIT
        rows = shard.shape[0] // planes
        blocks = [shard[p * rows : (p + 1) * rows] for p in range(planes)]
    else:
        planes = shard.shape[1] // WIDE
        rows = shard.shape[0]
        blocks = [shard[:, p * WIDE : (p + 1) * WIDE] for p in range(planes)]
    half = rows // 2
    out = []
    for b in blocks:
        b = pick(meta[2] == 1, b[:, :HALF], b[:, HALF:])
        out.append(pick(meta[1] == 1, b[:half], b[half:]))
    return jnp.stack(out)


D_SPLIT = 4


def gather_pieces(piece, fsdp_count):
    total = 4 * fsdp_count
    held = piece[None]
    mask = total // 2
    while mask >= 4:
        held = jnp.concatenate([held, swap(held, mask, total)], axis=0)
        mask //= 2
    over_x = swap(held, 2, total)
    return [held, over_x, swap(held, 1, total), swap(over_x, 1, total)]


def gather_weights(shards, meta, fsdp_count):
    parts = [own_piece(s, meta, r) for s, r in shards]
    counts = [p.shape[0] for p in parts]
    pieces = gather_pieces(jnp.concatenate(parts, axis=0), fsdp_count)
    out, start = [], 0
    build = assemble if pieces[0].shape[2] % 16 == 0 else assemble_plain
    for (_, by_rows), n in zip(shards, counts):
        out.append(build([p[:, start : start + n] for p in pieces], meta, by_rows))
        start += n
    return out


def reduce_grads(grads, meta, fsdp_count):
    total = 4 * fsdp_count
    planes, shapes = [], []
    for g, by_rows in grads:
        if by_rows:
            rows = g.shape[0] // fsdp_count // D_SPLIT
            g = g.reshape(fsdp_count, D_SPLIT, rows, WIDE)
            planes += [g[:, p] for p in range(D_SPLIT)]
            shapes.append((D_SPLIT, rows, True))
        else:
            n = g.shape[1] // WIDE
            rows = g.shape[0] // fsdp_count
            g = g.reshape(fsdp_count, rows, g.shape[1])
            planes += [g[:, :, p * WIDE : (p + 1) * WIDE] for p in range(n)]
            shapes.append((n, rows, False))
    core = meta[2] == 1
    keep = jnp.stack([pick(core, p[..., :HALF], p[..., HALF:]) for p in planes], axis=1)
    send = jnp.stack(
        [pick(core, p[..., HALF:], p[..., :HALF]).astype(jnp.bfloat16) for p in planes], axis=1
    )
    held = (keep + swap(send, 1, total)).astype(jnp.bfloat16)
    half = held.shape[2] // 2
    flag = meta[1] == 1
    send = pick(flag, held[:, :, half:], held[:, :, :half])
    keep = pick(flag, held[:, :, :half], held[:, :, half:])
    held = (keep.astype(jnp.float32) + swap(send, 2, total)).astype(jnp.bfloat16)
    bit = 1
    while bit < fsdp_count:
        held = held.reshape((held.shape[0] // 2, 2) + held.shape[1:])
        flag = (meta[0] & bit) != 0
        send = pick(flag, held[:, 1], held[:, 0])
        keep = pick(flag, held[:, 0], held[:, 1])
        held = (keep.astype(jnp.float32) + swap(send, bit * 4, total)).astype(jnp.bfloat16)
        bit *= 2
    mine = held[0]
    other = swap(mine, 2, total)
    near = jnp.concatenate([pick(meta[1] == 1, mine, other), pick(meta[1] == 1, other, mine)], axis=1)
    far = swap(near, 1, total)
    whole = jnp.concatenate(
        [pick(core, near, far), pick(core, far, near)], axis=2
    ).astype(jnp.float32)
    out, start = [], 0
    for n, rows, by_rows in shapes:
        block = whole[start : start + n]
        if by_rows:
            out.append(block.reshape(n * rows, WIDE))
        else:
            out.append(jnp.concatenate([block[p] for p in range(n)], axis=1))
        start += n
    return out


def reduce_vector(vector, fsdp_count):
    total = 4 * fsdp_count
    mask = 1
    while mask < total:
        vector = vector + swap(vector, mask, total)
        mask *= 2
    return vector


def body(
    fsdp_count,
    layer_input,
    segment_ids,
    joint_weight,
    query_bias,
    value_bias,
    close_weight,
    close_bias,
    first_gain,
    first_shift,
    expand_weight,
    expand_bias,
    shrink_weight,
    shrink_bias,
    second_gain,
    second_shift,
    cotangent,
):
    row_count, pos_count, model_width = layer_input.shape
    tok_count = row_count * pos_count
    flat_input = layer_input.reshape(tok_count, model_width)
    rep_index = lax.axis_index("rep")
    meta = jnp.stack([lax.axis_index("fsdp"), rep_index >> 1, rep_index & 1]).astype(jnp.int32)
    (joint_full,) = gather_weights([(joint_weight, False)], meta, fsdp_count)
    close_full, expand_full = gather_weights(
        [(close_weight, False), (expand_weight, False)], meta, fsdp_count
    )
    (shrink_full,) = gather_weights([(shrink_weight, True)], meta, fsdp_count)
    joint_bias = jnp.concatenate([query_bias, jnp.zeros_like(query_bias), value_bias]).astype(
        jnp.float32
    )
    mixed = jnp.dot(flat_input, joint_full, preferred_element_type=jnp.float32) + joint_bias
    joint_low = mixed.astype(jnp.bfloat16).reshape(row_count, pos_count, 3 * model_width)
    context, log_total = lax.map(
        lambda packet: attend_row(packet[0], packet[1]), (joint_low, segment_ids)
    )
    context_low = context.reshape(tok_count, model_width).astype(jnp.bfloat16)
    branch = jnp.dot(
        context_low, close_full, preferred_element_type=jnp.float32
    ) + close_bias.astype(jnp.float32)
    first_sum = flat_input.astype(jnp.float32) + branch
    hidden, first_pull = jax.vjp(
        layer_norm, first_sum, first_gain.astype(jnp.float32), first_shift.astype(jnp.float32)
    )
    hidden_low = hidden.astype(jnp.bfloat16)
    inner = jnp.dot(
        hidden_low, expand_full, preferred_element_type=jnp.float32
    ) + expand_bias.astype(jnp.float32)
    active, gelu_pull = jax.vjp(gelu_exact, inner)
    active_low = active.astype(jnp.bfloat16)
    ffn_out = jnp.dot(
        active_low, shrink_full, preferred_element_type=jnp.float32
    ) + shrink_bias.astype(jnp.float32)
    output, second_pull = jax.vjp(
        layer_norm,
        hidden + ffn_out,
        second_gain.astype(jnp.float32),
        second_shift.astype(jnp.float32),
    )
    layer_output = output.astype(jnp.bfloat16).reshape(row_count, pos_count, model_width)
    grad_second, second_gain_part, second_shift_part = second_pull(
        cotangent.reshape(tok_count, model_width).astype(jnp.float32)
    )
    grad_ffn = grad_second.astype(jnp.bfloat16)
    shrink_term = jnp.einsum("tf,td->fd", active_low, grad_ffn, preferred_element_type=jnp.float32)
    grad_active = jnp.einsum("td,fd->tf", grad_ffn, shrink_full, preferred_element_type=jnp.float32)
    grad_inner = gelu_pull(grad_active)[0].astype(jnp.bfloat16)
    expand_term = jnp.einsum(
        "td,tf->df", hidden_low, grad_inner, preferred_element_type=jnp.float32
    )
    grad_hidden = grad_second + jnp.einsum(
        "tf,df->td", grad_inner, expand_full, preferred_element_type=jnp.float32
    )
    (shrink_grad,) = reduce_grads([(shrink_term, True)], meta, fsdp_count)
    grad_first, first_gain_part, first_shift_part = first_pull(grad_hidden)
    grad_branch = grad_first.astype(jnp.bfloat16)
    close_term = jnp.einsum(
        "td,te->de", context_low, grad_branch, preferred_element_type=jnp.float32
    )
    grad_context = jnp.einsum(
        "te,de->td", grad_branch, close_full, preferred_element_type=jnp.float32
    ).astype(jnp.bfloat16)
    grad_mixed = lax.map(
        lambda packet: attend_back(packet[0], packet[1], packet[2], packet[3]),
        (
            joint_low,
            segment_ids,
            log_total,
            grad_context.reshape(row_count, pos_count, model_width),
        ),
    )
    grad_mixed_low = grad_mixed.reshape(tok_count, 3 * model_width).astype(jnp.bfloat16)
    joint_term = jnp.einsum(
        "td,te->de", flat_input, grad_mixed_low, preferred_element_type=jnp.float32
    )
    input_grad = grad_first + jnp.einsum(
        "te,de->td", grad_mixed_low, joint_full, preferred_element_type=jnp.float32
    )
    close_grad, expand_grad = reduce_grads(
        [(close_term, False), (expand_term, False)], meta, fsdp_count
    )
    (joint_grad,) = reduce_grads([(joint_term, False)], meta, fsdp_count)
    grad_mixed_wide = grad_mixed_low.astype(jnp.float32)
    early = reduce_vector(
        jnp.concatenate(
            [
                jnp.sum(grad_branch.astype(jnp.float32), axis=0),
                first_gain_part,
                first_shift_part,
                jnp.sum(grad_inner.astype(jnp.float32), axis=0),
                jnp.sum(grad_ffn.astype(jnp.float32), axis=0),
                second_gain_part,
                second_shift_part,
            ]
        ),
        fsdp_count,
    )
    hidden_units = expand_bias.shape[0]
    cuts, place = [], 0
    for size in (model_width,) * 3 + (hidden_units,) + (model_width,) * 3:
        cuts.append(early[place : place + size])
        place += size
    (
        close_bias_grad,
        first_gain_grad,
        first_shift_grad,
        expand_bias_grad,
        shrink_bias_grad,
        second_gain_grad,
        second_shift_grad,
    ) = cuts
    late = reduce_vector(
        jnp.concatenate(
            [
                jnp.sum(grad_mixed_wide[:, :model_width], axis=0),
                jnp.sum(grad_mixed_wide[:, 2 * model_width :], axis=0),
            ]
        ),
        fsdp_count,
    )
    query_bias_grad, value_bias_grad = late[:model_width], late[model_width:]
    return (
        layer_output,
        input_grad.reshape(row_count, pos_count, model_width),
        joint_grad,
        query_bias_grad,
        value_bias_grad,
        close_grad,
        close_bias_grad,
        first_gain_grad,
        first_shift_grad,
        expand_grad,
        expand_bias_grad,
        shrink_grad,
        shrink_bias_grad,
        second_gain_grad,
        second_shift_grad,
    )


def solution(mesh):
    placed = (
        P(("fsdp", "rep"), None, None),
        P(("fsdp", "rep"), None),
        P("fsdp", None),
        P(),
        P(),
        P("fsdp", None),
        P(),
        P(),
        P(),
        P("fsdp", None),
        P(),
        P("fsdp", None),
        P(),
        P(),
        P(),
        P(("fsdp", "rep"), None, None),
    )
    return jax.shard_map(
        functools.partial(body, mesh.shape["fsdp"]),
        mesh=mesh,
        in_specs=placed,
        out_specs=(
            P(("fsdp", "rep"), None, None),
            P(("fsdp", "rep"), None, None),
            P("fsdp", None),
            P(),
            P(),
            P("fsdp", None),
            P(),
            P(),
            P(),
            P("fsdp", None),
            P(),
            P("fsdp", None),
            P(),
            P(),
            P(),
        ),
        check_vma=False,
    )
```

```python
import functools
import math

import jax
import jax.numpy as jnp
from jax import lax
from jax.experimental import pallas as pl
from jax.experimental.pallas import tpu as pltpu
from jax.sharding import PartitionSpec as P

HEADS = 12
EPS = 1e-12
AXES = ("fsdp", "rep")
LANES = 128
NT = (((1,), (1,)), ((), ()))
NN = (((1,), (0,)), ((), ()))
LOW = jnp.bfloat16
WIDE = jnp.float32


def layer_norm(values, gain, shift):
    average = jnp.mean(values, axis=-1, keepdims=True)
    centred = values - average
    variance = jnp.mean(centred * centred, axis=-1, keepdims=True)
    return centred * lax.rsqrt(variance + EPS) * gain + shift


def attend_kernel(mixed_ref, seg_col_ref, seg_row_ref, *refs):
    context_ref, weights_ref, inverse_ref = refs[-3:]
    pos = mixed_ref.shape[0]
    head = mixed_ref.shape[1] // 6
    same = seg_col_ref[...] == seg_row_ref[...]
    values_t = mixed_ref[:, 4 * head : 6 * head].T
    ones = jnp.ones((16, pos), LOW)
    outs, inverses = [], []
    for h in range(2):
        queries = mixed_ref[:, h * head : (h + 1) * head] * LOW(1.0 / math.sqrt(head))
        keys = mixed_ref[:, (2 + h) * head : (3 + h) * head]
        scores = lax.dot_general(keys, queries, NT, preferred_element_type=WIDE)
        scores = jnp.where(same, scores, -jnp.inf)
        raised = jnp.exp(scores - jnp.max(scores, axis=0, keepdims=True)).astype(LOW)
        weights_ref[h] = raised
        extended = jnp.concatenate([values_t[h * head : (h + 1) * head], ones], axis=0)
        out = lax.dot_general(extended, raised, NN, preferred_element_type=WIDE)
        inverse = 1.0 / out[head : head + 1]
        outs.append(out[:head] * inverse)
        inverses.append(jnp.broadcast_to(inverse, (head, pos)))
    context_ref[...] = jnp.concatenate(outs, axis=0).T.astype(LOW)
    inverse_ref[...] = jnp.concatenate(inverses, axis=0).T


def attend_back_kernel(mixed_ref, weights_ref, context_ref, inverse_ref, grad_ref, *refs):
    out_ref, sum_ref = refs[-2:]
    head = mixed_ref.shape[1] // 6
    scale = LOW(1.0 / math.sqrt(head))
    grad = grad_ref[...].astype(WIDE) * inverse_ref[...]
    product = (grad * context_ref[...].astype(WIDE)).astype(LOW)
    grad_low = grad.astype(LOW)
    queries = mixed_ref[:, : 2 * head] * scale
    keys_t = (mixed_ref[:, 2 * head : 4 * head] * scale).T
    ones = jnp.ones((8, head), LOW)
    grad_q, grad_k, grad_v = [], [], []
    for h in range(2):
        cut = slice(h * head, (h + 1) * head)
        values = mixed_ref[:, (4 + h) * head : (5 + h) * head]
        inner = lax.dot_general(ones, product[:, cut], NT, preferred_element_type=WIDE)[0:1]
        raised = weights_ref[h]
        grad_attn = lax.dot_general(values, grad_low[:, cut], NT, preferred_element_type=WIDE)
        grad_scores = raised * (grad_attn - inner).astype(LOW)
        grad_k.append(lax.dot_general(grad_scores, queries[:, cut], NN, preferred_element_type=WIDE))
        grad_v.append(lax.dot_general(raised, grad_low[:, cut], NN, preferred_element_type=WIDE))
        grad_q.append(lax.dot_general(keys_t[cut], grad_scores, NN, preferred_element_type=WIDE))
    out = jnp.concatenate([jnp.concatenate(grad_q, axis=0).T] + grad_k + grad_v, axis=1).astype(LOW)
    out_ref[...] = out
    sum_ref[...] = jnp.broadcast_to(
        jnp.sum(out.astype(WIDE), axis=0, keepdims=True), sum_ref.shape
    )


class Chunk:
    def __init__(self, first, count, half):
        self.first, self.count, self.half = first, count, half
        self.pairs = [c * half + first + i for c in range(2) for i in range(count)]

    def block(self, place):
        return (place // self.count) * self.half + self.first + place % self.count


def attend(mixed, segments, chunk, context=None, behind=()):
    rows, pos, width = mixed.shape
    group = width // len(chunk.pairs)
    pair = group // 3
    count = len(chunk.pairs)
    total = 2 * chunk.half
    in_specs = [
        pl.BlockSpec((None, pos, group), lambda r, p: (r, 0, p)),
        pl.BlockSpec((None, pos, 1), lambda r, p: (r, 0, 0)),
        pl.BlockSpec((None, 1, pos), lambda r, p: (r, 0, 0)),
    ]
    operands = [mixed, segments[:, :, None], segments[:, None, :]]
    aliases = {}
    if context is not None:
        in_specs.append(pl.BlockSpec(memory_space=pl.ANY))
        operands.append(context)
        aliases = {3: 0}
    in_specs += [pl.BlockSpec(memory_space=pl.ANY)] * len(behind)
    operands += behind
    return pl.pallas_call(
        attend_kernel,
        grid=(rows, count),
        in_specs=in_specs,
        out_specs=[
            pl.BlockSpec((None, pos, pair), lambda r, p: (r, 0, chunk.block(p))),
            pl.BlockSpec((None, None, 2, pos, pos), lambda r, p: (r, p, 0, 0, 0)),
            pl.BlockSpec((None, pos, pair), lambda r, p: (r, 0, p)),
        ],
        out_shape=[
            jax.ShapeDtypeStruct((rows, pos, total * pair), LOW),
            jax.ShapeDtypeStruct((rows, count, 2, pos, pos), LOW),
            jax.ShapeDtypeStruct((rows, pos, count * pair), WIDE),
        ],
        input_output_aliases=aliases,
        cost_estimate=pl.CostEstimate(
            flops=rows * count * pos * pos * pair * 16,
            bytes_accessed=rows * count * pos * pos * 8,
            transcendentals=rows * count * pos * pos * 2,
        ),
        name="attend",
    )(*operands)


def attend_back(mixed, weights, context, inverse, grad, chunk, behind=()):
    rows, pos, width = mixed.shape
    count = len(chunk.pairs)
    group = width // count
    pair = group // 3
    natural = pl.BlockSpec((None, pos, pair), lambda r, p: (r, 0, chunk.block(p)))
    return pl.pallas_call(
        attend_back_kernel,
        grid=(rows, count),
        in_specs=[
            pl.BlockSpec((None, pos, group), lambda r, p: (r, 0, p)),
            pl.BlockSpec((None, None, 2, pos, pos), lambda r, p: (r, p, 0, 0, 0)),
            natural,
            pl.BlockSpec((None, pos, pair), lambda r, p: (r, 0, p)),
            natural,
        ]
        + [pl.BlockSpec(memory_space=pl.ANY)] * len(behind),
        out_specs=[
            pl.BlockSpec((None, pos, group), lambda r, p: (r, 0, p)),
            pl.BlockSpec((None, None, 8, group), lambda r, p: (r, p, 0, 0)),
        ],
        out_shape=[
            jax.ShapeDtypeStruct((rows, pos, count * group), LOW),
            jax.ShapeDtypeStruct((rows, count, 8, group), WIDE),
        ],
        cost_estimate=pl.CostEstimate(
            flops=rows * count * pos * pos * pair * 32,
            bytes_accessed=rows * count * pos * pos * 8,
            transcendentals=0,
        ),
        name="attend_back",
    )(mixed, weights, context, inverse, grad, *behind)


def expand_kernel(hidden_ref, weight_ref, bias_ref, active_ref, slope_ref, *, chunks):
    step = hidden_ref.shape[0] // chunks
    for i in range(chunks):
        cut = slice(i * step, (i + 1) * step)
        inner = lax.dot_general(hidden_ref[cut], weight_ref[...], NN, preferred_element_type=WIDE)
        inner = inner + bias_ref[...]
        share = 0.5 + 0.5 * lax.erf(inner * math.sqrt(0.5))
        active_ref[cut] = (inner * share).astype(LOW)
        density = jnp.exp(-0.5 * inner * inner) * (1.0 / math.sqrt(2.0 * math.pi))
        slope_ref[cut] = (share + inner * density).astype(LOW)


def expand_gelu(hidden, weight, bias):
    tokens, model_width = hidden.shape
    units = weight.shape[1]
    tile = 768
    return pl.pallas_call(
        functools.partial(expand_kernel, chunks=8),
        grid=(units // tile,),
        in_specs=[
            pl.BlockSpec((tokens, model_width), lambda j: (0, 0)),
            pl.BlockSpec((model_width, tile), lambda j: (0, j)),
            pl.BlockSpec((1, tile), lambda j: (0, j)),
        ],
        out_specs=[pl.BlockSpec((tokens, tile), lambda j: (0, j))] * 2,
        out_shape=[jax.ShapeDtypeStruct((tokens, units), LOW)] * 2,
        cost_estimate=pl.CostEstimate(
            flops=3 * tokens * model_width * units,
            bytes_accessed=2 * (tokens * units * 2 + model_width * units),
            transcendentals=2 * tokens * units,
        ),
        name="expand_gelu",
    )(hidden, weight, bias)


class Wires:
    def __init__(self, fsdp_count):
        self.fsdp_count = fsdp_count
        self.total = 4 * fsdp_count
        self.shard = lax.axis_index("fsdp")
        rep = lax.axis_index("rep")
        self.x = rep >> 1
        self.core = rep & 1
        self.meta = jnp.stack([self.shard, self.x, self.core]).astype(jnp.int32)

    def swap(self, value, mask):
        return lax.ppermute(value, AXES, [(i, i ^ mask) for i in range(self.total)])

    def own_half(self, low, high):
        return jnp.where(self.core == 1, high, low)

    def other_half(self, low, high):
        return jnp.where(self.core == 1, low, high)

    def own_rows(self, value, axis=0):
        half = value.shape[axis] // 2
        low = lax.slice_in_dim(value, 0, half, axis=axis)
        high = lax.slice_in_dim(value, half, 2 * half, axis=axis)
        return jnp.where(self.x == 1, high, low), jnp.where(self.x == 1, low, high)


    def steps(self):
        masks, mask = [], self.total // 2
        while mask >= 4:
            masks.append(mask)
            mask //= 2
        return masks

    def share(self, near):
        return near + [self.swap(v, 1) for v in near]


    def halve_steps(self, held):
        bit = 1
        while bit < self.fsdp_count:
            held = held.reshape((held.shape[0] // 2, 2) + held.shape[1:])
            flag = (self.shard & bit) != 0
            send = jnp.where(flag, held[:, 0], held[:, 1])
            keep = jnp.where(flag, held[:, 1], held[:, 0])
            held = add_low(keep, self.swap(send, 4 * bit))
            bit *= 2
            yield held if bit < self.fsdp_count else held[0]

    def x_steps(self, keep, got):
        held = add_low(keep, got)
        for held in self.halve_steps(held):
            yield held
        other = self.swap(held, 2)
        flag = self.x == 1
        yield jnp.concatenate([jnp.where(flag, other, held), jnp.where(flag, held, other)], axis=0)

    def all_steps(self, held):
        for held in self.halve_steps(held):
            yield held
        yield add_low(held, self.swap(held, 2))

    def reduce_vector(self, vector):
        mask = 1
        while mask < self.total:
            vector = vector + self.swap(vector, mask)
            mask *= 2
        return vector


def tie(*values):
    return lax.optimization_barrier(values)


def last(steps):
    for value in steps:
        pass
    return value


def row(vector):
    return vector.reshape(1, -1).astype(WIDE)


def add_low(first, second):
    return (first.astype(WIDE) + second.astype(WIDE)).astype(LOW)


def weight_copies(meta_ref, refs, out_ref, sem, parts, half_width):
    count = out_ref.shape[0]
    at = 0
    copies = []
    for width, start, by_x, offset in parts:
        for place in range(4 if by_x else 2):
            piece = refs[at]
            at += 1
            core = meta_ref[2] ^ (place // 2 if by_x else place)
            col = pl.multiple_of(core * half_width + offset, LANES)
            rows = piece.shape[1]
            row = pl.multiple_of((meta_ref[1] ^ (place & 1)) * rows, rows) if by_x else 0
            for j in range(count):
                copies.append(
                    pltpu.make_async_copy(
                        piece.at[j, :, pl.ds(start, width)],
                        out_ref.at[
                            meta_ref[0] ^ from_front(j, count), pl.ds(row, rows), pl.ds(col, width)
                        ],
                        sem,
                    )
                )
    return copies


def assemble_kernel(meta_ref, *refs, parts, half_width):
    copies = weight_copies(meta_ref, refs, refs[-2], refs[-1], parts, half_width)
    for copy in copies:
        copy.start()
    for copy in copies:
        copy.wait()


def project(inputs, weight_ref, query_ref, value_ref, out_ref, pairs):
    group = 3 * LANES
    step = 256
    for i, p in enumerate(pairs):
        cut = slice(i * group, (i + 1) * group)
        weight = weight_ref[..., cut].reshape(inputs.shape[1], group)
        bias = jnp.concatenate(
            [query_ref[p : p + 1], jnp.zeros((1, LANES), WIDE), value_ref[p : p + 1]], axis=1
        )
        for t in range(0, inputs.shape[0], step):
            out = lax.dot_general(inputs[t : t + step], weight, NN, preferred_element_type=WIDE)
            out_ref[t : t + step, cut] = (out + bias).astype(LOW)


def project_kernel(meta_ref, inputs_ref, query_ref, value_ref, *refs, parts, half_width, pairs):
    full_ref, out_ref, sem = refs[-3:]
    copies = weight_copies(meta_ref, refs, full_ref, sem, parts, half_width)
    for copy in copies:
        copy.start()
    for copy in copies:
        copy.wait()
    project(inputs_ref, full_ref, query_ref, value_ref, out_ref, pairs)


def project_whole_kernel(inputs_ref, query_ref, value_ref, full_ref, *refs, pairs):
    project(inputs_ref, full_ref, query_ref, value_ref, refs[-1], pairs)


def joint_project(wires, inputs, pieces, query_bias, value_bias, chunk, shard_rows, behind=()):
    tokens, model_width = inputs.shape
    half_width = chunk.count * 3 * LANES
    out_shape = jax.ShapeDtypeStruct((tokens, 2 * half_width), LOW)
    on_chip = pl.BlockSpec(memory_space=pltpu.VMEM)
    anywhere = pl.BlockSpec(memory_space=pl.ANY)
    cost = pl.CostEstimate(
        flops=4 * tokens * model_width * half_width,
        bytes_accessed=4 * half_width * (tokens + 3 * model_width),
        transcendentals=0,
    )
    if not isinstance(pieces, list):
        out = pl.pallas_call(
            functools.partial(project_whole_kernel, pairs=chunk.pairs),
            out_shape=out_shape,
            in_specs=[on_chip] * 4 + [anywhere] * len(behind),
            out_specs=on_chip,
            cost_estimate=cost,
            name="joint_project",
        )(inputs, query_bias, value_bias, pieces, *behind)
        return pieces, out
    full, out = pl.pallas_call(
        functools.partial(
            project_kernel,
            parts=[(half_width, 0, True, 0)],
            half_width=half_width,
            pairs=chunk.pairs,
        ),
        out_shape=[
            jax.ShapeDtypeStruct((wires.fsdp_count, shard_rows, 2 * half_width), LOW),
            out_shape,
        ],
        in_specs=[pl.BlockSpec(memory_space=pltpu.SMEM)]
        + [on_chip] * 3
        + [anywhere] * (len(pieces) + len(behind)),
        out_specs=[on_chip] * 2,
        scratch_shapes=[pltpu.SemaphoreType.DMA],
        cost_estimate=cost,
        name="joint_project",
    )(wires.meta, inputs, query_bias, value_bias, *pieces, *behind)
    return full.reshape(model_width, 2 * half_width), out


def pack_kernel(*refs, chunks, wide):
    *vector_refs, out_ref = refs
    sum_refs, vector_refs = vector_refs[: len(chunks)], vector_refs[len(chunks) :]
    out_ref[...] = jnp.zeros_like(out_ref)
    for ref, chunk in zip(sum_refs, chunks):
        for i, p in enumerate(chunk.pairs):
            total = ref[0, i, 0:1]
            for r in range(1, ref.shape[0]):
                total = total + ref[r, i, 0:1]
            out_ref[0:1, p * LANES : (p + 1) * LANES] = total[:, :LANES]
            out_ref[1:2, p * LANES : (p + 1) * LANES] = total[:, 2 * LANES :]
    row = 2
    for ref in vector_refs:
        for start in range(0, ref.shape[1], wide):
            out_ref[row : row + 1] = ref[:, start : start + wide]
            row += 1


def pack(sums, chunks, vectors, wide):
    rows = 2 + sum(v.shape[1] // wide for v in vectors)
    return pl.pallas_call(
        functools.partial(pack_kernel, chunks=chunks, wide=wide),
        out_shape=jax.ShapeDtypeStruct(((rows + 7) // 8 * 8, wide), WIDE),
        name="pack",
    )(*sums, *vectors)


def from_front(place, count):
    bits = count.bit_length() - 1
    return sum(((place >> b) & 1) << (bits - 1 - b) for b in range(bits))


def assemble(wires, shard_rows, half_width, parts):
    count = wires.fsdp_count
    operands, plan = [], []
    for pieces, width, start, by_x, offset in parts:
        plan.append((width, start, by_x, offset))
        operands += pieces
    shape = (count, shard_rows, 2 * half_width)
    full = pl.pallas_call(
        functools.partial(assemble_kernel, parts=plan, half_width=half_width),
        out_shape=jax.ShapeDtypeStruct(shape, LOW),
        in_specs=[pl.BlockSpec(memory_space=pltpu.SMEM)]
        + [pl.BlockSpec(memory_space=pl.ANY)] * len(operands),
        out_specs=pl.BlockSpec(memory_space=pltpu.VMEM),
        scratch_shapes=[pltpu.SemaphoreType.DMA],
        cost_estimate=pl.CostEstimate(
            flops=0, bytes_accessed=4 * math.prod(shape), transcendentals=0
        ),
        name="assemble",
    )(wires.meta, *operands)
    return full.reshape(count * shard_rows, 2 * half_width)


def pair_columns(array, pairs, model_width):
    return jnp.concatenate(
        [
            array[..., part * model_width + p * LANES : part * model_width + (p + 1) * LANES]
            for p in pairs
            for part in range(3)
        ],
        axis=-1,
    )


def natural_columns(pieces, chunks):
    where = {}
    for piece, chunk in zip(pieces, chunks):
        for i, p in enumerate(chunk.pairs):
            for part in range(3):
                place = (3 * i + part) * LANES
                where[(part, p)] = piece[..., place : place + LANES]
    return jnp.concatenate([where[key] for key in sorted(where)], axis=-1)


def body(
    fsdp_count,
    layer_input,
    segment_ids,
    joint_weight,
    query_bias,
    value_bias,
    close_weight,
    close_bias,
    first_gain,
    first_shift,
    expand_weight,
    expand_bias,
    shrink_weight,
    shrink_bias,
    second_gain,
    second_shift,
    cotangent,
):
    row_count, pos_count, model_width = layer_input.shape
    hidden_units = expand_bias.shape[0]
    tok_count = row_count * pos_count
    flat_input = layer_input.reshape(tok_count, model_width)
    wires = Wires(fsdp_count)
    half_pairs = model_width // LANES // 2
    small, large = Chunk(0, 1, half_pairs), Chunk(1, half_pairs - 1, half_pairs)
    chunks = (small, large)
    shard_rows = joint_weight.shape[0]

    joint_pieces = []
    for chunk in chunks:
        low, high = (
            pair_columns(joint_weight, chunk.pairs[c * chunk.count : (c + 1) * chunk.count], model_width)
            for c in range(2)
        )
        joint_pieces.append(wires.own_rows(wires.own_half(low, high))[0])
    unit = hidden_units // 4
    expand_half = wires.own_half(expand_weight[:, : 2 * unit], expand_weight[:, 2 * unit :])
    close_half = wires.own_half(
        close_weight[:, : model_width // 2], close_weight[:, model_width // 2 :]
    )
    plain_piece = jnp.concatenate([expand_half[:, :unit], close_half], axis=1)
    split_piece = wires.own_rows(expand_half[:, unit:])[0]
    shrink_piece = wires.own_half(
        shrink_weight[:, : model_width // 2], shrink_weight[:, model_width // 2 :]
    )
    aligned = shard_rows % 32 == 0
    query_rows = query_bias.astype(WIDE).reshape(-1, LANES)
    value_rows = value_bias.astype(WIDE).reshape(-1, LANES)
    half_model = model_width // 2
    behind = ((), (), ())
    if aligned:
        first, second = joint_pieces[0][None], joint_pieces[1][None]
        plain, split, shrink = plain_piece[None], split_piece[None], shrink_piece[None]
        *outer, inner = wires.steps()

        def join(held, got):
            return jnp.concatenate([held, got], axis=0)

        for mask in outer:
            got = wires.swap(first, mask)
            first = join(first, got)
        first, second = tie(first, second)
        got = wires.swap(first, inner)
        second_got = wires.swap(second, outer[0])
        got, second_got = tie(got, second_got)
        first, second = join(first, got), join(second, second_got)
        first_x = wires.swap(first, 2)
        for mask in outer[1:]:
            second = join(second, wires.swap(second, mask))
        first_x, second, plain = tie(first_x, second, plain)
        second_got = wires.swap(second, inner)
        for mask in outer:
            plain = join(plain, wires.swap(plain, mask))
        second = join(second, second_got)
        plain, second, split = tie(plain, second, split)
        second_x = wires.swap(second, 2)
        plain_got = wires.swap(plain, inner)
        for mask in outer:
            split = join(split, wires.swap(split, mask))
        split, shrink, plain_got = tie(split, shrink, plain_got)
        plain = join(plain, plain_got)
        split = join(split, wires.swap(split, inner))
        second_x, split = tie(second_x, split)
        split_x = wires.swap(split, 2)
        for mask in outer:
            shrink = join(shrink, wires.swap(shrink, mask))
        split, shrink = tie(split, shrink)
        shrink = join(shrink, wires.swap(shrink, inner))
        joint_shared = [wires.share([first, first_x]), wires.share([second, second_x])]
        split_shared = wires.share([split, split_x])
        plain_shared = wires.share([plain])
        shrink_shared = wires.share([shrink])
    else:
        joint_shared = [
            lax.all_gather(
                pair_columns(joint_weight, c.pairs, model_width), "fsdp", axis=0, tiled=True
            )
            for c in chunks
        ]

    joint_full, mixed, weights, inverse = [], [], [], []
    context = None
    for shared, chunk in zip(joint_shared, chunks):
        full, part = joint_project(
            wires, flat_input, shared, query_rows, value_rows, chunk, shard_rows
        )
        joint_full.append(full)
        mixed.append(part.reshape(row_count, pos_count, -1))
        context, w, inv = attend(mixed[-1], segment_ids, chunk, context)
        weights.append(w)
        inverse.append(inv)
    context_low = context.reshape(tok_count, model_width)

    if aligned:
        close_full = assemble(
            wires, shard_rows, half_model, [(plain_shared, half_model, unit, False, 0)]
        )
        expand_full = assemble(
            wires,
            shard_rows,
            hidden_units // 2,
            [(plain_shared, unit, 0, False, 0), (split_shared, unit, 0, True, unit)],
        )
        shrink_full = assemble(
            wires, shrink_weight.shape[0], half_model, [(shrink_shared, half_model, 0, False, 0)]
        )
    else:
        close_full, expand_full, shrink_full = (
            lax.all_gather(w, "fsdp", axis=0, tiled=True)
            for w in (close_weight, expand_weight, shrink_weight)
        )

    branch = jnp.dot(context_low, close_full, preferred_element_type=WIDE) + row(close_bias)
    first_sum = flat_input.astype(WIDE) + branch
    hidden, first_pull = jax.vjp(
        layer_norm, first_sum, row(first_gain), row(first_shift)
    )
    hidden_low = hidden.astype(LOW)
    active_low, slope = expand_gelu(hidden_low, expand_full, row(expand_bias))
    ffn_out = jnp.dot(active_low, shrink_full, preferred_element_type=WIDE) + row(shrink_bias)
    output, second_pull = jax.vjp(
        layer_norm, hidden + ffn_out, row(second_gain), row(second_shift)
    )
    layer_output = output.astype(LOW).reshape(row_count, pos_count, model_width)
    grad_second, second_gain_part, second_shift_part = second_pull(
        cotangent.reshape(tok_count, model_width).astype(WIDE)
    )
    grad_ffn = grad_second.astype(LOW)

    def outgoing(left, right):
        half = right.shape[1] // 2
        send = wires.other_half(right[:, :half], right[:, half:])
        return jnp.einsum("tf,td->fd", left, send, preferred_element_type=WIDE).astype(LOW)

    def staying(left, right, got):
        half = right.shape[1] // 2
        keep = wires.own_half(right[:, :half], right[:, half:])
        keep = jnp.einsum("tf,td->fd", left, keep, preferred_element_type=WIDE)
        held = (keep + got.astype(WIDE)).astype(LOW)
        return held.reshape(fsdp_count, held.shape[0] // fsdp_count, half)

    def both_halves(mine):
        other = wires.swap(mine, 1)
        return wires.own_half(mine, other), wires.own_half(other, mine)

    shrink_send = outgoing(active_low, grad_ffn)
    grad_ffn, shrink_send = tie(grad_ffn, shrink_send)
    shrink_got = wires.swap(shrink_send, 1)
    grad_active = jnp.einsum("td,fd->tf", grad_ffn, shrink_full, preferred_element_type=WIDE)
    grad_inner = (grad_active * slope.astype(WIDE)).astype(LOW)
    active_low, grad_inner = tie(active_low, grad_inner)
    shrink_held = staying(active_low, grad_ffn, shrink_got)
    hidden_low, shrink_held = tie(hidden_low, shrink_held)
    shrink_steps = wires.halve_steps(shrink_held)
    expand_send = outgoing(hidden_low, grad_inner)
    grad_inner, expand_send = tie(grad_inner, expand_send)
    expand_got = wires.swap(expand_send, 1)
    grad_hidden = grad_second + jnp.einsum(
        "tf,df->td", grad_inner, expand_full, preferred_element_type=WIDE
    )
    grad_first, first_gain_part, first_shift_part = first_pull(grad_hidden)
    grad_branch = grad_first.astype(LOW)
    hidden_low, grad_branch = tie(hidden_low, grad_branch)
    expand_held = staying(hidden_low, grad_inner, expand_got)
    context_low, expand_held = tie(context_low, expand_held)
    close_send = outgoing(context_low, grad_branch)
    grad_branch, close_send = tie(grad_branch, close_send)
    close_got = wires.swap(close_send, 1)
    grad_context = jnp.einsum(
        "te,de->td", grad_branch, close_full, preferred_element_type=WIDE
    ).astype(LOW)
    context_low, grad_context = tie(context_low, grad_context)
    close_held = staying(context_low, grad_branch, close_got)
    grad_context = grad_context.reshape(row_count, pos_count, model_width)
    second_keep, second_send = wires.own_rows(
        jnp.concatenate([expand_held, close_held], axis=2), axis=1
    )
    second_got = wires.swap(second_send, 2)

    shrink_now = next(shrink_steps)
    grad_mixed, bias_sums = {}, {}
    grad_mixed[1], bias_sums[1] = attend_back(
        mixed[1],
        weights[1],
        context,
        inverse[1],
        grad_context,
        chunks[1],
        [shrink_now, second_send],
    )
    grad_mixed[1] = grad_mixed[1].reshape(tok_count, -1)
    send = outgoing(flat_input, grad_mixed[1])
    flat_input, send = tie(flat_input, send)
    held = staying(flat_input, grad_mixed[1], wires.swap(send, 1))
    large_steps = wires.all_steps(held)
    shrink_now = next(shrink_steps)
    grad_mixed[0], bias_sums[0] = attend_back(
        mixed[0],
        weights[0],
        context,
        inverse[0],
        grad_context,
        chunks[0],
        [shrink_now, held],
    )
    grad_mixed[0] = grad_mixed[0].reshape(tok_count, -1)
    send = outgoing(flat_input, grad_mixed[0])
    flat_input, send = tie(flat_input, send)
    held = staying(flat_input, grad_mixed[0], wires.swap(send, 1))
    grad_mixed[0], grad_mixed[1], held = tie(grad_mixed[0], grad_mixed[1], held)
    small_steps = wires.all_steps(held)
    second_steps = wires.x_steps(second_keep, second_got)
    input_grad = (
        grad_first
        + jnp.einsum("te,de->td", grad_mixed[0], joint_full[0], preferred_element_type=WIDE)
        + jnp.einsum("te,de->td", grad_mixed[1], joint_full[1], preferred_element_type=WIDE)
    )
    for shrink_now in shrink_steps:
        pass
    shrink_mine = add_low(shrink_now, wires.swap(shrink_now, 2))
    second_mine, large_mine, small_mine = (last(v) for v in (second_steps, large_steps, small_steps))
    joint_mine = (small_mine, large_mine)

    def column_sum(value):
        return jnp.sum(value.astype(WIDE), axis=0, keepdims=True)

    packed = pack(
        [bias_sums[0], bias_sums[1]],
        chunks,
        [
            column_sum(grad_branch),
            first_gain_part,
            first_shift_part,
            column_sum(grad_ffn),
            second_gain_part,
            second_shift_part,
            column_sum(grad_inner),
        ],
        model_width,
    )
    summed = wires.reduce_vector(packed)
    (
        query_bias_grad,
        value_bias_grad,
        close_bias_grad,
        first_gain_grad,
        first_shift_grad,
        shrink_bias_grad,
        second_gain_grad,
        second_shift_grad,
    ) = (summed[i] for i in range(8))
    expand_bias_grad = summed[8 : 8 + hidden_units // model_width].reshape(hidden_units)

    shrink_grad = jnp.concatenate(both_halves(shrink_mine), axis=1).astype(WIDE)
    low, high = both_halves(second_mine)
    cut = hidden_units // 2
    expand_grad = jnp.concatenate([low[:, :cut], high[:, :cut]], axis=1).astype(WIDE)
    close_grad = jnp.concatenate([low[:, cut:], high[:, cut:]], axis=1).astype(WIDE)
    joint_grad = natural_columns(
        [jnp.concatenate(both_halves(joint_mine[i]), axis=1) for i in range(2)], chunks
    ).astype(WIDE)
    return (
        layer_output,
        input_grad.reshape(row_count, pos_count, model_width),
        joint_grad,
        query_bias_grad,
        value_bias_grad,
        close_grad,
        close_bias_grad,
        first_gain_grad,
        first_shift_grad,
        expand_grad,
        expand_bias_grad,
        shrink_grad,
        shrink_bias_grad,
        second_gain_grad,
        second_shift_grad,
    )


def solution(mesh):
    rows = P(("fsdp", "rep"), None, None)
    sharded = P("fsdp", None)
    copied = P()
    return jax.shard_map(
        functools.partial(body, mesh.shape["fsdp"]),
        mesh=mesh,
        in_specs=(
            rows,
            P(("fsdp", "rep"), None),
            sharded,
            copied,
            copied,
            sharded,
            copied,
            copied,
            copied,
            sharded,
            copied,
            sharded,
            copied,
            copied,
            copied,
            rows,
        ),
        out_specs=(
            rows,
            rows,
            sharded,
            copied,
            copied,
            sharded,
            copied,
            copied,
            copied,
            sharded,
            copied,
            sharded,
            copied,
            copied,
            copied,
        ),
        check_vma=False,
    )
```

```python
import functools
import math

import jax
import jax.numpy as jnp
from jax import lax
from jax.experimental import pallas as pl
from jax.experimental.pallas import tpu as pltpu
from jax.sharding import PartitionSpec as P

HEADS = 12
EPS = 1e-12
AXES = ("fsdp", "rep")
LANES = 128
NT = (((1,), (1,)), ((), ()))
NN = (((1,), (0,)), ((), ()))
LOW = jnp.bfloat16
WIDE = jnp.float32


def layer_norm(values, gain, shift):
    average = jnp.mean(values, axis=-1, keepdims=True)
    centred = values - average
    variance = jnp.mean(centred * centred, axis=-1, keepdims=True)
    return centred * lax.rsqrt(variance + EPS) * gain + shift


def attend_kernel(mixed_ref, seg_col_ref, seg_row_ref, *refs):
    context_ref, weights_ref, inverse_ref = refs[-3:]
    pos = mixed_ref.shape[0]
    head = mixed_ref.shape[1] // 6
    same = seg_col_ref[...] == seg_row_ref[...]
    values_t = mixed_ref[:, 4 * head : 6 * head].T
    ones = jnp.ones((16, pos), LOW)
    outs, inverses = [], []
    for h in range(2):
        queries = mixed_ref[:, h * head : (h + 1) * head] * LOW(1.0 / math.sqrt(head))
        keys = mixed_ref[:, (2 + h) * head : (3 + h) * head]
        scores = lax.dot_general(keys, queries, NT, preferred_element_type=WIDE)
        scores = jnp.where(same, scores, -jnp.inf)
        raised = jnp.exp(scores - jnp.max(scores, axis=0, keepdims=True)).astype(LOW)
        weights_ref[h] = raised
        extended = jnp.concatenate([values_t[h * head : (h + 1) * head], ones], axis=0)
        out = lax.dot_general(extended, raised, NN, preferred_element_type=WIDE)
        inverse = 1.0 / out[head : head + 1]
        outs.append(out[:head] * inverse)
        inverses.append(jnp.broadcast_to(inverse, (head, pos)))
    context_ref[...] = jnp.concatenate(outs, axis=0).T.astype(LOW)
    inverse_ref[...] = jnp.concatenate(inverses, axis=0).T


def attend_back_kernel(mixed_ref, weights_ref, context_ref, inverse_ref, grad_ref, *refs):
    out_ref, sum_ref = refs[-2:]
    head = mixed_ref.shape[1] // 6
    scale = LOW(1.0 / math.sqrt(head))
    grad = grad_ref[...].astype(WIDE) * inverse_ref[...]
    product = (grad * context_ref[...].astype(WIDE)).astype(LOW)
    grad_low = grad.astype(LOW)
    queries = mixed_ref[:, : 2 * head] * scale
    keys_t = (mixed_ref[:, 2 * head : 4 * head] * scale).T
    ones = jnp.ones((8, head), LOW)
    grad_q, grad_k, grad_v = [], [], []
    for h in range(2):
        cut = slice(h * head, (h + 1) * head)
        values = mixed_ref[:, (4 + h) * head : (5 + h) * head]
        inner = lax.dot_general(ones, product[:, cut], NT, preferred_element_type=WIDE)[0:1]
        raised = weights_ref[h]
        grad_attn = lax.dot_general(values, grad_low[:, cut], NT, preferred_element_type=WIDE)
        grad_scores = raised * (grad_attn - inner).astype(LOW)
        grad_k.append(lax.dot_general(grad_scores, queries[:, cut], NN, preferred_element_type=WIDE))
        grad_v.append(lax.dot_general(raised, grad_low[:, cut], NN, preferred_element_type=WIDE))
        grad_q.append(lax.dot_general(keys_t[cut], grad_scores, NN, preferred_element_type=WIDE))
    out = jnp.concatenate([jnp.concatenate(grad_q, axis=0).T] + grad_k + grad_v, axis=1).astype(LOW)
    out_ref[...] = out
    sum_ref[...] = jnp.broadcast_to(
        jnp.sum(out.astype(WIDE), axis=0, keepdims=True), sum_ref.shape
    )


class Chunk:
    def __init__(self, first, count, half):
        self.first, self.count, self.half = first, count, half
        self.pairs = [c * half + first + i for c in range(2) for i in range(count)]

    def block(self, place):
        return (place // self.count) * self.half + self.first + place % self.count


def attend(mixed, segments, chunk, context=None, behind=()):
    rows, pos, width = mixed.shape
    group = width // len(chunk.pairs)
    pair = group // 3
    count = len(chunk.pairs)
    total = 2 * chunk.half
    in_specs = [
        pl.BlockSpec((None, pos, group), lambda r, p: (r, 0, p)),
        pl.BlockSpec((None, pos, 1), lambda r, p: (r, 0, 0)),
        pl.BlockSpec((None, 1, pos), lambda r, p: (r, 0, 0)),
    ]
    operands = [mixed, segments[:, :, None], segments[:, None, :]]
    aliases = {}
    if context is not None:
        in_specs.append(pl.BlockSpec(memory_space=pl.ANY))
        operands.append(context)
        aliases = {3: 0}
    in_specs += [pl.BlockSpec(memory_space=pl.ANY)] * len(behind)
    operands += behind
    return pl.pallas_call(
        attend_kernel,
        grid=(rows, count),
        in_specs=in_specs,
        out_specs=[
            pl.BlockSpec((None, pos, pair), lambda r, p: (r, 0, chunk.block(p))),
            pl.BlockSpec((None, None, 2, pos, pos), lambda r, p: (r, p, 0, 0, 0)),
            pl.BlockSpec((None, pos, pair), lambda r, p: (r, 0, p)),
        ],
        out_shape=[
            jax.ShapeDtypeStruct((rows, pos, total * pair), LOW),
            jax.ShapeDtypeStruct((rows, count, 2, pos, pos), LOW),
            jax.ShapeDtypeStruct((rows, pos, count * pair), WIDE),
        ],
        input_output_aliases=aliases,
        cost_estimate=pl.CostEstimate(
            flops=rows * count * pos * pos * pair * 16,
            bytes_accessed=rows * count * pos * pos * 8,
            transcendentals=rows * count * pos * pos * 2,
        ),
        name="attend",
    )(*operands)


def attend_back(mixed, weights, context, inverse, grad, chunk, behind=()):
    rows, pos, width = mixed.shape
    count = len(chunk.pairs)
    group = width // count
    pair = group // 3
    natural = pl.BlockSpec((None, pos, pair), lambda r, p: (r, 0, chunk.block(p)))
    return pl.pallas_call(
        attend_back_kernel,
        grid=(rows, count),
        in_specs=[
            pl.BlockSpec((None, pos, group), lambda r, p: (r, 0, p)),
            pl.BlockSpec((None, None, 2, pos, pos), lambda r, p: (r, p, 0, 0, 0)),
            natural,
            pl.BlockSpec((None, pos, pair), lambda r, p: (r, 0, p)),
            natural,
        ]
        + [pl.BlockSpec(memory_space=pl.ANY)] * len(behind),
        out_specs=[
            pl.BlockSpec((None, pos, group), lambda r, p: (r, 0, p)),
            pl.BlockSpec((None, None, 8, group), lambda r, p: (r, p, 0, 0)),
        ],
        out_shape=[
            jax.ShapeDtypeStruct((rows, pos, count * group), LOW),
            jax.ShapeDtypeStruct((rows, count, 8, group), WIDE),
        ],
        cost_estimate=pl.CostEstimate(
            flops=rows * count * pos * pos * pair * 32,
            bytes_accessed=rows * count * pos * pos * 8,
            transcendentals=0,
        ),
        name="attend_back",
    )(mixed, weights, context, inverse, grad, *behind)


def expand_kernel(hidden_ref, weight_ref, bias_ref, active_ref, slope_ref, *, chunks):
    step = hidden_ref.shape[0] // chunks
    for i in range(chunks):
        cut = slice(i * step, (i + 1) * step)
        inner = lax.dot_general(hidden_ref[cut], weight_ref[...], NN, preferred_element_type=WIDE)
        inner = inner + bias_ref[...]
        share = 0.5 + 0.5 * lax.erf(inner * math.sqrt(0.5))
        active_ref[cut] = (inner * share).astype(LOW)
        density = jnp.exp(-0.5 * inner * inner) * (1.0 / math.sqrt(2.0 * math.pi))
        slope_ref[cut] = (share + inner * density).astype(LOW)


def expand_gelu(hidden, weight, bias):
    tokens, model_width = hidden.shape
    units = weight.shape[1]
    tile = 768
    return pl.pallas_call(
        functools.partial(expand_kernel, chunks=8),
        grid=(units // tile,),
        in_specs=[
            pl.BlockSpec((tokens, model_width), lambda j: (0, 0)),
            pl.BlockSpec((model_width, tile), lambda j: (0, j)),
            pl.BlockSpec((1, tile), lambda j: (0, j)),
        ],
        out_specs=[pl.BlockSpec((tokens, tile), lambda j: (0, j))] * 2,
        out_shape=[jax.ShapeDtypeStruct((tokens, units), LOW)] * 2,
        cost_estimate=pl.CostEstimate(
            flops=3 * tokens * model_width * units,
            bytes_accessed=2 * (tokens * units * 2 + model_width * units),
            transcendentals=2 * tokens * units,
        ),
        name="expand_gelu",
    )(hidden, weight, bias)


def inner_grad_kernel(grad_ref, weight_ref, slope_ref, out_ref, sum_ref, *, chunks):
    step = grad_ref.shape[0] // chunks
    total = jnp.zeros((1, weight_ref.shape[0]), WIDE)
    for i in range(chunks):
        cut = slice(i * step, (i + 1) * step)
        grad = lax.dot_general(grad_ref[cut], weight_ref[...], NT, preferred_element_type=WIDE)
        grad = (grad * slope_ref[cut].astype(WIDE)).astype(LOW)
        out_ref[cut] = grad
        total = total + jnp.sum(grad.astype(WIDE), axis=0, keepdims=True)
    sum_ref[...] = total


def inner_grad(grad, weight, slope):
    tokens, model_width = grad.shape
    units = weight.shape[0]
    tile = 768
    return pl.pallas_call(
        functools.partial(inner_grad_kernel, chunks=4),
        grid=(units // tile,),
        in_specs=[
            pl.BlockSpec((tokens, model_width), lambda j: (0, 0)),
            pl.BlockSpec((tile, model_width), lambda j: (j, 0)),
            pl.BlockSpec((tokens, tile), lambda j: (0, j)),
        ],
        out_specs=[
            pl.BlockSpec((tokens, tile), lambda j: (0, j)),
            pl.BlockSpec((1, tile), lambda j: (0, j)),
        ],
        out_shape=[
            jax.ShapeDtypeStruct((tokens, units), LOW),
            jax.ShapeDtypeStruct((1, units), WIDE),
        ],
        cost_estimate=pl.CostEstimate(
            flops=2 * tokens * model_width * units,
            bytes_accessed=4 * tokens * units + 2 * model_width * units,
            transcendentals=0,
        ),
        name="inner_grad",
    )(grad, weight, slope)


class Wires:
    def __init__(self, fsdp_count):
        self.fsdp_count = fsdp_count
        self.total = 4 * fsdp_count
        self.shard = lax.axis_index("fsdp")
        rep = lax.axis_index("rep")
        self.x = rep >> 1
        self.core = rep & 1
        self.meta = jnp.stack([self.shard, self.x, self.core]).astype(jnp.int32)

    def swap(self, value, mask):
        return lax.ppermute(value, AXES, [(i, i ^ mask) for i in range(self.total)])

    def own_half(self, low, high):
        return jnp.where(self.core == 1, high, low)

    def other_half(self, low, high):
        return jnp.where(self.core == 1, low, high)

    def own_rows(self, value, axis=0):
        half = value.shape[axis] // 2
        low = lax.slice_in_dim(value, 0, half, axis=axis)
        high = lax.slice_in_dim(value, half, 2 * half, axis=axis)
        return jnp.where(self.x == 1, high, low), jnp.where(self.x == 1, low, high)

    def near(self, value):
        return [self.swap(value, 8 * k) for k in range(1, self.fsdp_count // 2)]

    def share(self, near):
        return near + [self.swap(v, 1) for v in near]


    def y_halves(self, held):
        held = held.reshape((held.shape[0] // 2, 2) + held.shape[1:])
        flag = (self.shard & 1) != 0
        return jnp.where(flag, held[:, 1], held[:, 0]), jnp.where(flag, held[:, 0], held[:, 1])

    def z_block(self, held, k):
        return lax.dynamic_index_in_dim(held, (self.shard >> 1) ^ k, 0, keepdims=False)

    def z_sends(self, held):
        if held.shape[0] > 4:
            return [held]
        return [self.z_block(held, k) for k in range(1, held.shape[0])]

    def z_swap(self, sends):
        if sends[0].ndim == 2:
            return [self.swap(v, 8 * (k + 1)) for k, v in enumerate(sends)]
        held, bit = sends[0], 2
        while bit < self.fsdp_count:
            held = held.reshape((held.shape[0] // 2, 2) + held.shape[1:])
            flag = (self.shard & bit) != 0
            got = self.swap(jnp.where(flag, held[:, 0], held[:, 1]), 4 * bit)
            held = add_low(jnp.where(flag, held[:, 1], held[:, 0]), got)
            bit *= 2
        return [held[0]]

    def z_sum(self, held, got):
        if held.shape[0] > 4:
            return got[0]
        return add_low(self.z_block(held, 0), *got)

    def by_x(self, own, other):
        return jnp.where(self.x == 1, other, own), jnp.where(self.x == 1, own, other)

    def reduce_vector(self, vector):
        mask = 1
        while mask < self.total:
            vector = vector + self.swap(vector, mask)
            mask *= 2
        return vector


def tie(*values):
    return lax.optimization_barrier(values)


def row(vector):
    return vector.reshape(1, -1).astype(WIDE)


def add_low(first, *others):
    total = first.astype(WIDE)
    for other in others:
        total = total + other.astype(WIDE)
    return total.astype(LOW)


def weight_copies(meta_ref, refs, out_ref, sem, parts, half_width):
    count = out_ref.shape[0]
    at = 0
    copies = []
    for width, start, by_x, offset, row in parts:
        for place in range(4 if by_x else 2):
            piece = refs[at]
            at += 1
            core = meta_ref[2] ^ (place // 2 if by_x else place)
            col = core * half_width + offset
            if by_x:
                col = col + (meta_ref[1] ^ (place & 1)) * width
            col = pl.multiple_of(col, LANES)
            rows = piece.shape[1]
            for j in range(count):
                copies.append(
                    pltpu.make_async_copy(
                        piece.at[j, :, pl.ds(start, width)],
                        out_ref.at[
                            meta_ref[0] ^ relative(j, count), row : row + rows, pl.ds(col, width)
                        ],
                        sem,
                    )
                )
    return copies


def assemble_kernel(meta_ref, *refs, parts, half_width):
    copies = weight_copies(meta_ref, refs, refs[-2], refs[-1], parts, half_width)
    for copy in copies:
        copy.start()
    for copy in copies:
        copy.wait()


def project(inputs, weight_ref, query_ref, value_ref, out_ref, pairs):
    group = 3 * LANES
    step = 256
    for i, p in enumerate(pairs):
        cut = slice(i * group, (i + 1) * group)
        weight = weight_ref[..., cut].reshape(inputs.shape[1], group)
        bias = jnp.concatenate(
            [query_ref[p : p + 1], jnp.zeros((1, LANES), WIDE), value_ref[p : p + 1]], axis=1
        )
        for t in range(0, inputs.shape[0], step):
            out = lax.dot_general(inputs[t : t + step], weight, NN, preferred_element_type=WIDE)
            out_ref[t : t + step, cut] = (out + bias).astype(LOW)


def project_kernel(meta_ref, inputs_ref, query_ref, value_ref, *refs, parts, half_width, pairs):
    full_ref, out_ref, sem = refs[-3:]
    copies = weight_copies(meta_ref, refs, full_ref, sem, parts, half_width)
    for copy in copies:
        copy.start()
    for copy in copies:
        copy.wait()
    project(inputs_ref, full_ref, query_ref, value_ref, out_ref, pairs)


def project_whole_kernel(inputs_ref, query_ref, value_ref, full_ref, *refs, pairs):
    project(inputs_ref, full_ref, query_ref, value_ref, refs[-1], pairs)


def joint_project(wires, inputs, pieces, query_bias, value_bias, chunk, shard_rows, behind=()):
    tokens, model_width = inputs.shape
    half_width = chunk.count * 3 * LANES
    out_shape = jax.ShapeDtypeStruct((tokens, 2 * half_width), LOW)
    on_chip = pl.BlockSpec(memory_space=pltpu.VMEM)
    anywhere = pl.BlockSpec(memory_space=pl.ANY)
    cost = pl.CostEstimate(
        flops=4 * tokens * model_width * half_width,
        bytes_accessed=4 * half_width * (tokens + 3 * model_width),
        transcendentals=0,
    )
    if not isinstance(pieces, list):
        out = pl.pallas_call(
            functools.partial(project_whole_kernel, pairs=chunk.pairs),
            out_shape=out_shape,
            in_specs=[on_chip] * 4 + [anywhere] * len(behind),
            out_specs=on_chip,
            cost_estimate=cost,
            name="joint_project",
        )(inputs, query_bias, value_bias, pieces, *behind)
        return pieces, out
    full, out = pl.pallas_call(
        functools.partial(
            project_kernel,
            parts=[(half_width, 0, False, 0, 0)],
            half_width=half_width,
            pairs=chunk.pairs,
        ),
        out_shape=[
            jax.ShapeDtypeStruct((wires.fsdp_count, shard_rows, 2 * half_width), LOW),
            out_shape,
        ],
        in_specs=[pl.BlockSpec(memory_space=pltpu.SMEM)]
        + [on_chip] * 3
        + [anywhere] * (len(pieces) + len(behind)),
        out_specs=[on_chip] * 2,
        scratch_shapes=[pltpu.SemaphoreType.DMA],
        cost_estimate=cost,
        name="joint_project",
    )(wires.meta, inputs, query_bias, value_bias, *pieces, *behind)
    return full.reshape(model_width, 2 * half_width), out


def pack_kernel(*refs, chunks, wide):
    *vector_refs, out_ref = refs
    sum_refs, vector_refs = vector_refs[: len(chunks)], vector_refs[len(chunks) :]
    out_ref[...] = jnp.zeros_like(out_ref)
    for ref, chunk in zip(sum_refs, chunks):
        for i, p in enumerate(chunk.pairs):
            total = ref[0, i, 0:1]
            for r in range(1, ref.shape[0]):
                total = total + ref[r, i, 0:1]
            out_ref[0:1, p * LANES : (p + 1) * LANES] = total[:, :LANES]
            out_ref[1:2, p * LANES : (p + 1) * LANES] = total[:, 2 * LANES :]
    row = 2
    for ref in vector_refs:
        for start in range(0, ref.shape[1], wide):
            out_ref[row : row + 1] = ref[:, start : start + wide]
            row += 1


def pack(sums, chunks, vectors, wide):
    rows = 2 + sum(v.shape[1] // wide for v in vectors)
    return pl.pallas_call(
        functools.partial(pack_kernel, chunks=chunks, wide=wide),
        out_shape=jax.ShapeDtypeStruct(((rows + 7) // 8 * 8, wide), WIDE),
        name="pack",
    )(*sums, *vectors)


def relative(place, count):
    half = count // 2
    return (place % half) * 2 + place // half


def assemble(wires, shard_rows, half_width, parts):
    count = wires.fsdp_count
    operands, plan = [], []
    for pieces, *where in parts:
        plan.append(where)
        operands += pieces
    shape = (count, shard_rows, 2 * half_width)
    full = pl.pallas_call(
        functools.partial(assemble_kernel, parts=plan, half_width=half_width),
        out_shape=jax.ShapeDtypeStruct(shape, LOW),
        in_specs=[pl.BlockSpec(memory_space=pltpu.SMEM)]
        + [pl.BlockSpec(memory_space=pl.ANY)] * len(operands),
        out_specs=pl.BlockSpec(memory_space=pltpu.VMEM),
        scratch_shapes=[pltpu.SemaphoreType.DMA],
        cost_estimate=pl.CostEstimate(
            flops=0, bytes_accessed=4 * math.prod(shape), transcendentals=0
        ),
        name="assemble",
    )(wires.meta, *operands)
    return full.reshape(count * shard_rows, 2 * half_width)


def pair_columns(array, pairs, model_width):
    return jnp.concatenate(
        [
            array[..., part * model_width + p * LANES : part * model_width + (p + 1) * LANES]
            for p in pairs
            for part in range(3)
        ],
        axis=-1,
    )


def natural_columns(pieces, chunks):
    where = {}
    for piece, chunk in zip(pieces, chunks):
        for i, p in enumerate(chunk.pairs):
            for part in range(3):
                place = (3 * i + part) * LANES
                where[(part, p)] = piece[..., place : place + LANES]
    return jnp.concatenate([where[key] for key in sorted(where)], axis=-1)


def body(
    fsdp_count,
    layer_input,
    segment_ids,
    joint_weight,
    query_bias,
    value_bias,
    close_weight,
    close_bias,
    first_gain,
    first_shift,
    expand_weight,
    expand_bias,
    shrink_weight,
    shrink_bias,
    second_gain,
    second_shift,
    cotangent,
):
    row_count, pos_count, model_width = layer_input.shape
    hidden_units = expand_bias.shape[0]
    tok_count = row_count * pos_count
    flat_input = layer_input.reshape(tok_count, model_width)
    wires = Wires(fsdp_count)
    half_pairs = model_width // LANES // 2
    small, large = Chunk(0, 1, half_pairs), Chunk(1, half_pairs - 1, half_pairs)
    chunks = (small, large)
    shard_rows = joint_weight.shape[0]

    joint_pieces = []
    for chunk in chunks:
        low, high = (
            pair_columns(joint_weight, chunk.pairs[c * chunk.count : (c + 1) * chunk.count], model_width)
            for c in range(2)
        )
        joint_pieces.append(wires.own_half(low, high))
    half_model, half_hidden = model_width // 2, hidden_units // 2
    unit = half_hidden // 3
    expand_half = wires.own_half(expand_weight[:, :half_hidden], expand_weight[:, half_hidden:])
    close_half = wires.own_half(close_weight[:, :half_model], close_weight[:, half_model:])
    shrink_half = wires.own_half(shrink_weight[:, :half_model], shrink_weight[:, half_model:])
    aligned = fsdp_count == 8 and shard_rows % 32 == 0
    query_rows = query_bias.astype(WIDE).reshape(-1, LANES)
    value_rows = value_bias.astype(WIDE).reshape(-1, LANES)

    def join(*parts):
        return jnp.concatenate(parts, axis=0)

    def project_and_attend(place, shared, context):
        full, part = joint_project(
            wires, flat_input, shared, query_rows, value_rows, chunks[place], shard_rows
        )
        return full, part.reshape(row_count, pos_count, -1)

    if aligned:
        first, second = joint_pieces[0][None], joint_pieces[1][None]
        mixed_piece = jnp.concatenate([expand_half[:, :unit], close_half], axis=1)[None]
        split = wires.by_x(expand_half[:, unit : 2 * unit], expand_half[:, 2 * unit :])[0][None]
        shrink_rows = shrink_half.shape[0] // 2
        top, bottom = shrink_half[None, :shrink_rows], shrink_half[None, shrink_rows:]
        first_near = wires.near(first)
        first = join(first, *first_near)
        first, second = tie(first, second)
        first_y = wires.swap(first, 4)
        second_near = wires.near(second)
        first = join(first, first_y)
        first_core = wires.swap(first, 1)
        first_core, split, second, *second_near = tie(first_core, split, second, *second_near)
        second = join(second, *second_near)
        second_y = wires.swap(second, 4)
        split_near = wires.near(split)
        full, part = project_and_attend(0, [first, first_core], None)
        joint_full, mixed = [full], [part]
        mixed[0], mixed_piece = tie(mixed[0], mixed_piece)
        piece_near = wires.near(mixed_piece)
        context, w, inv = attend(mixed[0], segment_ids, chunks[0])
        weights, inverse = [w], [inv]
        context, second, second_y, split, *split_near = tie(
            context, second, second_y, split, *split_near
        )
        second = join(second, second_y)
        second_core = wires.swap(second, 1)
        split = join(split, *split_near)
        split_y = wires.swap(split, 4)
        full, part = project_and_attend(1, [second, second_core], context)
        joint_full.append(full)
        part, split, split_y, mixed_piece, top, *piece_near = tie(
            part, split, split_y, mixed_piece, top, *piece_near
        )
        mixed.append(part)
        split = join(split, split_y)
        split_x = wires.swap(split, 2)
        mixed_piece = join(mixed_piece, *piece_near)
        piece_y = wires.swap(mixed_piece, 4)
        top_near = wires.near(top)
        context, w, inv = attend(mixed[1], segment_ids, chunks[1], context)
        weights.append(w)
        inverse.append(inv)
        context, split, split_x, mixed_piece, piece_y, top, bottom, *top_near = tie(
            context, split, split_x, mixed_piece, piece_y, top, bottom, *top_near
        )
        plain_shared = wires.share([join(mixed_piece, piece_y)])
        split_shared = wires.share([split, split_x])
        top = join(top, *top_near)
        top_y = wires.swap(top, 4)
        bottom_near = wires.near(bottom)
        close_full = assemble(
            wires, shard_rows, half_model, [(plain_shared, half_model, unit, False, 0, 0)]
        )
        expand_full = assemble(
            wires,
            shard_rows,
            half_hidden,
            [(plain_shared, unit, 0, False, 0, 0), (split_shared, unit, 0, True, unit, 0)],
        )
    else:
        joint_full, mixed, weights, inverse = [], [], [], []
        context = None
        for place, chunk in enumerate(chunks):
            shared = lax.all_gather(
                pair_columns(joint_weight, chunk.pairs, model_width), "fsdp", axis=0, tiled=True
            )
            full, part = project_and_attend(place, shared, context)
            joint_full.append(full)
            mixed.append(part)
            context, w, inv = attend(part, segment_ids, chunk, context)
            weights.append(w)
            inverse.append(inv)
        close_full, expand_full, shrink_full = (
            lax.all_gather(w, "fsdp", axis=0, tiled=True)
            for w in (close_weight, expand_weight, shrink_weight)
        )
    context_low = context.reshape(tok_count, model_width)

    branch = jnp.dot(context_low, close_full, preferred_element_type=WIDE) + row(close_bias)
    first_sum = flat_input.astype(WIDE) + branch
    hidden, first_pull = jax.vjp(
        layer_norm, first_sum, row(first_gain), row(first_shift)
    )
    hidden_low = hidden.astype(LOW)
    active_low, slope = expand_gelu(hidden_low, expand_full, row(expand_bias))
    if aligned:
        active_low, top, top_y, bottom, *bottom_near = tie(
            active_low, top, top_y, bottom, *bottom_near
        )
        bottom = join(bottom, *bottom_near)
        bottom_y = wires.swap(bottom, 4)
        top_shared = wires.share([join(top, top_y)])
        bottom_shared = wires.share([join(bottom, bottom_y)])
        shrink_full = assemble(
            wires,
            shrink_weight.shape[0],
            half_model,
            [
                (top_shared, half_model, 0, False, 0, 0),
                (bottom_shared, half_model, 0, False, 0, shrink_rows),
            ],
        )
    ffn_out = jnp.dot(active_low, shrink_full, preferred_element_type=WIDE) + row(shrink_bias)
    output, second_pull = jax.vjp(
        layer_norm, hidden + ffn_out, row(second_gain), row(second_shift)
    )
    layer_output = output.astype(LOW).reshape(row_count, pos_count, model_width)
    grad_second, second_gain_part, second_shift_part = second_pull(
        cotangent.reshape(tok_count, model_width).astype(WIDE)
    )
    grad_ffn = grad_second.astype(LOW)

    def outgoing(left, right):
        half = right.shape[1] // 2
        send = wires.other_half(right[:, :half], right[:, half:])
        return jnp.einsum("tf,td->fd", left, send, preferred_element_type=WIDE).astype(LOW)

    def staying(left, right, got):
        half = right.shape[1] // 2
        keep = wires.own_half(right[:, :half], right[:, half:])
        keep = jnp.einsum("tf,td->fd", left, keep, preferred_element_type=WIDE)
        held = (keep + got.astype(WIDE)).astype(LOW)
        return held.reshape(fsdp_count, held.shape[0] // fsdp_count, half)

    def both_halves(mine):
        other = wires.swap(mine, 1)
        return wires.own_half(mine, other), wires.own_half(other, mine)

    shrink_send = outgoing(active_low, grad_ffn)
    grad_ffn, shrink_send = tie(grad_ffn, shrink_send)
    shrink_got = wires.swap(shrink_send, 1)
    grad_inner, inner_sum = inner_grad(grad_ffn, shrink_full, slope)
    active_low, grad_inner, shrink_got = tie(active_low, grad_inner, shrink_got)
    shrink_keep, shrink_send = wires.y_halves(staying(active_low, grad_ffn, shrink_got))
    hidden_low, shrink_keep, shrink_send = tie(hidden_low, shrink_keep, shrink_send)
    shrink_got = wires.swap(shrink_send, 4)
    expand_send = outgoing(hidden_low, grad_inner)
    grad_inner, expand_send = tie(grad_inner, expand_send)
    expand_got = wires.swap(expand_send, 1)
    grad_hidden = grad_second + jnp.einsum(
        "tf,df->td", grad_inner, expand_full, preferred_element_type=WIDE
    )
    grad_first, first_gain_part, first_shift_part = first_pull(grad_hidden)
    grad_branch = grad_first.astype(LOW)
    hidden_low, grad_branch, expand_got = tie(hidden_low, grad_branch, expand_got)
    expand_held = staying(hidden_low, grad_inner, expand_got)
    expand_keep, expand_send = wires.by_x(
        expand_held[..., : half_hidden // 2], expand_held[..., half_hidden // 2 :]
    )
    context_low, expand_keep, expand_send = tie(context_low, expand_keep, expand_send)
    expand_got = wires.swap(expand_send, 2)
    close_send = outgoing(context_low, grad_branch)
    grad_branch, close_send = tie(grad_branch, close_send)
    close_got = wires.swap(close_send, 1)
    grad_context = jnp.einsum(
        "te,de->td", grad_branch, close_full, preferred_element_type=WIDE
    ).astype(LOW)
    context_low, grad_context, close_got = tie(context_low, grad_context, close_got)
    close_held = staying(context_low, grad_branch, close_got)
    grad_context = grad_context.reshape(row_count, pos_count, model_width)
    grad_context, close_held, shrink_keep, shrink_got = tie(
        grad_context, close_held, shrink_keep, shrink_got
    )
    shrink_held = add_low(shrink_keep, shrink_got)
    grad_context, shrink_held, *shrink_sends = tie(
        grad_context, shrink_held, *wires.z_sends(shrink_held)
    )
    shrink_got = wires.z_swap(shrink_sends)

    grad_mixed, bias_sums = {}, {}
    grad_mixed[1], bias_sums[1] = attend_back(
        mixed[1], weights[1], context, inverse[1], grad_context, chunks[1]
    )
    grad_mixed[1] = grad_mixed[1].reshape(tok_count, -1)
    large_send = outgoing(flat_input, grad_mixed[1])
    grad_mixed[1], large_send, expand_keep, expand_got = tie(
        grad_mixed[1], large_send, expand_keep, expand_got
    )
    large_got = wires.swap(large_send, 1)
    second_keep, second_send = wires.y_halves(
        jnp.concatenate([add_low(expand_keep, expand_got), close_held], axis=2)
    )
    flat_input, second_keep, second_send, large_got = tie(
        flat_input, second_keep, second_send, large_got
    )
    second_got = wires.swap(second_send, 4)
    large_keep, large_send = wires.own_rows(staying(flat_input, grad_mixed[1], large_got), axis=1)
    grad_context, large_keep, large_send, shrink_held, *shrink_got = tie(
        grad_context, large_keep, large_send, shrink_held, *shrink_got
    )
    large_got = wires.swap(large_send, 2)
    shrink_mine = wires.z_sum(shrink_held, shrink_got)
    grad_mixed[0], bias_sums[0] = attend_back(
        mixed[0], weights[0], context, inverse[0], grad_context, chunks[0]
    )
    grad_mixed[0] = grad_mixed[0].reshape(tok_count, -1)
    small_send = outgoing(flat_input, grad_mixed[0])
    grad_mixed[0], small_send, large_keep, large_got, second_keep, second_got = tie(
        grad_mixed[0], small_send, large_keep, large_got, second_keep, second_got
    )
    small_got = wires.swap(small_send, 1)
    large_keep, large_send = wires.y_halves(add_low(large_keep, large_got))
    second_held = add_low(second_keep, second_got)
    flat_input, small_got, large_keep, large_send, second_held, *second_sends = tie(
        flat_input, small_got, large_keep, large_send, second_held, *wires.z_sends(second_held)
    )
    large_got = wires.swap(large_send, 4)
    second_got = wires.z_swap(second_sends)
    small_keep, small_send = wires.own_rows(staying(flat_input, grad_mixed[0], small_got), axis=1)
    grad_mixed[0], grad_mixed[1], small_keep, small_send = tie(
        grad_mixed[0], grad_mixed[1], small_keep, small_send
    )
    small_got = wires.swap(small_send, 2)
    input_grad = (
        grad_first
        + jnp.einsum("te,de->td", grad_mixed[0], joint_full[0], preferred_element_type=WIDE)
        + jnp.einsum("te,de->td", grad_mixed[1], joint_full[1], preferred_element_type=WIDE)
    )
    input_grad, small_keep, small_got, large_keep, large_got = tie(
        input_grad, small_keep, small_got, large_keep, large_got
    )
    small_keep, small_send = wires.y_halves(add_low(small_keep, small_got))
    small_got = wires.swap(small_send, 4)
    large_held = add_low(large_keep, large_got)
    joint_held = jnp.concatenate([add_low(small_keep, small_got), large_held], axis=2)
    joint_mine = wires.z_sum(joint_held, wires.z_swap(wires.z_sends(joint_held)))
    second_mine = wires.z_sum(second_held, second_got)

    shrink_mine = add_low(shrink_mine, wires.swap(shrink_mine, 2))
    second_other = wires.swap(second_mine, 2)
    quarter = half_hidden // 2
    second_mine = jnp.concatenate(
        [
            *wires.by_x(second_mine[:, :quarter], second_other[:, :quarter]),
            add_low(second_mine[:, quarter:], second_other[:, quarter:]),
        ],
        axis=1,
    )
    joint_mine = jnp.concatenate(wires.by_x(joint_mine, wires.swap(joint_mine, 2)), axis=0)

    def column_sum(value):
        return jnp.sum(value.astype(WIDE), axis=0, keepdims=True)

    packed = pack(
        [bias_sums[0], bias_sums[1]],
        chunks,
        [
            column_sum(grad_branch),
            first_gain_part,
            first_shift_part,
            column_sum(grad_ffn),
            second_gain_part,
            second_shift_part,
            inner_sum,
        ],
        model_width,
    )
    summed = wires.reduce_vector(packed)
    (
        query_bias_grad,
        value_bias_grad,
        close_bias_grad,
        first_gain_grad,
        first_shift_grad,
        shrink_bias_grad,
        second_gain_grad,
        second_shift_grad,
    ) = (summed[i] for i in range(8))
    expand_bias_grad = summed[8 : 8 + hidden_units // model_width].reshape(hidden_units)

    shrink_grad = jnp.concatenate(both_halves(shrink_mine), axis=1).astype(WIDE)
    low, high = both_halves(second_mine)
    cut = hidden_units // 2
    expand_grad = jnp.concatenate([low[:, :cut], high[:, :cut]], axis=1).astype(WIDE)
    close_grad = jnp.concatenate([low[:, cut:], high[:, cut:]], axis=1).astype(WIDE)
    low, high = both_halves(joint_mine)
    cut = small.count * 3 * LANES
    joint_grad = natural_columns(
        [
            jnp.concatenate([low[:, :cut], high[:, :cut]], axis=1),
            jnp.concatenate([low[:, cut:], high[:, cut:]], axis=1),
        ],
        chunks,
    ).astype(WIDE)
    return (
        layer_output,
        input_grad.reshape(row_count, pos_count, model_width),
        joint_grad,
        query_bias_grad,
        value_bias_grad,
        close_grad,
        close_bias_grad,
        first_gain_grad,
        first_shift_grad,
        expand_grad,
        expand_bias_grad,
        shrink_grad,
        shrink_bias_grad,
        second_gain_grad,
        second_shift_grad,
    )


def solution(mesh):
    rows = P(("fsdp", "rep"), None, None)
    sharded = P("fsdp", None)
    copied = P()
    return jax.shard_map(
        functools.partial(body, mesh.shape["fsdp"]),
        mesh=mesh,
        in_specs=(
            rows,
            P(("fsdp", "rep"), None),
            sharded,
            copied,
            copied,
            sharded,
            copied,
            copied,
            copied,
            sharded,
            copied,
            sharded,
            copied,
            copied,
            copied,
            rows,
        ),
        out_specs=(
            rows,
            rows,
            sharded,
            copied,
            copied,
            sharded,
            copied,
            copied,
            copied,
            sharded,
            copied,
            sharded,
            copied,
            copied,
            copied,
        ),
        check_vma=False,
    )
```

```python
import functools
import itertools
import math

import jax
import jax.numpy as jnp
from jax import lax
from jax.experimental import pallas as pl
from jax.experimental.pallas import tpu as pltpu
from jax.sharding import PartitionSpec as P

HEADS = 12
EPS = 1e-12
AXES = ("fsdp", "rep")
LANES = 128
NT = (((1,), (1,)), ((), ()))
NN = (((1,), (0,)), ((), ()))
LOW = jnp.bfloat16
WIDE = jnp.float32
BRIEF = pl.CostEstimate(flops=0, bytes_accessed=0, transcendentals=0)


def layer_norm(values, gain, shift):
    average = jnp.mean(values, axis=-1, keepdims=True)
    centred = values - average
    variance = jnp.mean(centred * centred, axis=-1, keepdims=True)
    return centred * lax.rsqrt(variance + EPS) * gain + shift


def attend_kernel(mixed_ref, seg_col_ref, seg_row_ref, *refs):
    context_ref, weights_ref, inverse_ref = refs[-3:]
    pos = mixed_ref.shape[0]
    head = mixed_ref.shape[1] // 6
    same = seg_col_ref[...] == seg_row_ref[...]
    values_t = mixed_ref[:, 4 * head : 6 * head].T
    ones = jnp.ones((16, pos), LOW)
    outs, inverses = [], []
    for h in range(2):
        queries = mixed_ref[:, h * head : (h + 1) * head] * LOW(1.0 / math.sqrt(head))
        keys = mixed_ref[:, (2 + h) * head : (3 + h) * head]
        scores = lax.dot_general(keys, queries, NT, preferred_element_type=WIDE)
        scores = jnp.where(same, scores, -jnp.inf)
        raised = jnp.exp(scores - jnp.max(scores, axis=0, keepdims=True)).astype(LOW)
        weights_ref[h] = raised
        extended = jnp.concatenate([values_t[h * head : (h + 1) * head], ones], axis=0)
        out = lax.dot_general(extended, raised, NN, preferred_element_type=WIDE)
        inverse = 1.0 / out[head : head + 1]
        outs.append(out[:head] * inverse)
        inverses.append(jnp.broadcast_to(inverse, (head, pos)))
    context_ref[...] = jnp.concatenate(outs, axis=0).T.astype(LOW)
    inverse_ref[...] = jnp.concatenate(inverses, axis=0).T


def attend_back_kernel(
    mixed_ref,
    weights_ref,
    context_ref,
    inverse_ref,
    grad_ref,
    inputs_ref,
    out_ref,
    sum_ref,
    joint_ref,
    total_ref,
):
    row = pl.program_id(1)
    head = mixed_ref.shape[1] // 6
    scale = LOW(1.0 / math.sqrt(head))
    grad = grad_ref[...].astype(WIDE) * inverse_ref[...]
    product = (grad * context_ref[...].astype(WIDE)).astype(LOW)
    grad_low = grad.astype(LOW)
    queries = mixed_ref[:, : 2 * head] * scale
    keys_t = (mixed_ref[:, 2 * head : 4 * head] * scale).T
    ones = jnp.ones((8, head), LOW)
    grad_q, grad_k, grad_v = [], [], []
    for h in range(2):
        cut = slice(h * head, (h + 1) * head)
        values = mixed_ref[:, (4 + h) * head : (5 + h) * head]
        inner = lax.dot_general(ones, product[:, cut], NT, preferred_element_type=WIDE)[0:1]
        raised = weights_ref[h]
        grad_attn = lax.dot_general(values, grad_low[:, cut], NT, preferred_element_type=WIDE)
        grad_scores = raised * (grad_attn - inner).astype(LOW)
        grad_k.append(lax.dot_general(grad_scores, queries[:, cut], NN, preferred_element_type=WIDE))
        grad_v.append(lax.dot_general(raised, grad_low[:, cut], NN, preferred_element_type=WIDE))
        grad_q.append(lax.dot_general(keys_t[cut], grad_scores, NN, preferred_element_type=WIDE))
    out = jnp.concatenate([jnp.concatenate(grad_q, axis=0).T] + grad_k + grad_v, axis=1).astype(LOW)
    out_ref[...] = out
    sum_ref[...] = jnp.broadcast_to(
        jnp.sum(out.astype(WIDE), axis=0, keepdims=True), sum_ref.shape
    )
    part = lax.dot_general(inputs_ref[row], out, NN, preferred_element_type=WIDE)

    @pl.when(row == 0)
    def _():
        total_ref[...] = part

    @pl.when(row > 0)
    def _():
        total_ref[...] += part

    @pl.when(row == pl.num_programs(1) - 1)
    def _():
        joint_ref[...] = total_ref[...].astype(LOW)


class Chunk:
    def __init__(self, first, count, half):
        self.first, self.count, self.half = first, count, half
        self.pairs = [c * half + first + i for c in range(2) for i in range(count)]

    def block(self, place):
        return (place // self.count) * self.half + self.first + place % self.count


def attend(mixed, segments, chunk, context=None, behind=()):
    rows, pos, width = mixed.shape
    group = width // len(chunk.pairs)
    pair = group // 3
    count = len(chunk.pairs)
    total = 2 * chunk.half
    in_specs = [
        pl.BlockSpec((None, pos, group), lambda r, p: (r, 0, p)),
        pl.BlockSpec((None, pos, 1), lambda r, p: (r, 0, 0)),
        pl.BlockSpec((None, 1, pos), lambda r, p: (r, 0, 0)),
    ]
    operands = [mixed, *segments]
    aliases = {}
    if context is not None:
        in_specs.append(pl.BlockSpec(memory_space=pl.ANY))
        operands.append(context)
        aliases = {3: 0}
    in_specs += [pl.BlockSpec(memory_space=pl.ANY)] * len(behind)
    operands += behind
    return pl.pallas_call(
        attend_kernel,
        grid=(rows, count),
        in_specs=in_specs,
        out_specs=[
            pl.BlockSpec((None, pos, pair), lambda r, p: (r, 0, chunk.block(p))),
            pl.BlockSpec((None, None, 2, pos, pos), lambda r, p: (r, p, 0, 0, 0)),
            pl.BlockSpec((None, pos, pair), lambda r, p: (r, 0, p)),
        ],
        out_shape=[
            jax.ShapeDtypeStruct((rows, pos, total * pair), LOW),
            jax.ShapeDtypeStruct((rows, count, 2, pos, pos), LOW),
            jax.ShapeDtypeStruct((rows, pos, count * pair), WIDE),
        ],
        input_output_aliases=aliases,
        cost_estimate=BRIEF,
        name="attend",
    )(*operands)


def attend_back(mixed, weights, context, inverse, grad, inputs, chunk):
    rows, pos, width = mixed.shape
    model_width = inputs.shape[1]
    count = len(chunk.pairs)
    group = width // count
    pair = group // 3
    natural = pl.BlockSpec((None, pos, pair), lambda p, r: (r, 0, chunk.block(p)))
    return pl.pallas_call(
        attend_back_kernel,
        grid=(count, rows),
        in_specs=[
            pl.BlockSpec((None, pos, group), lambda p, r: (r, 0, p)),
            pl.BlockSpec((None, None, 2, pos, pos), lambda p, r: (r, p, 0, 0, 0)),
            natural,
            pl.BlockSpec((None, pos, pair), lambda p, r: (r, 0, p)),
            natural,
            pl.BlockSpec((rows, model_width, pos), lambda p, r: (0, 0, 0)),
        ],
        out_specs=[
            pl.BlockSpec((None, pos, group), lambda p, r: (r, 0, p)),
            pl.BlockSpec((None, None, 8, group), lambda p, r: (r, p, 0, 0)),
            pl.BlockSpec(
                (None, model_width, group),
                lambda p, r: (p // chunk.count, 0, p % chunk.count),
            ),
        ],
        out_shape=[
            jax.ShapeDtypeStruct((rows, pos, count * group), LOW),
            jax.ShapeDtypeStruct((rows, count, 8, group), WIDE),
            jax.ShapeDtypeStruct((2, model_width, chunk.count * group), LOW),
        ],
        scratch_shapes=[pltpu.VMEM((model_width, group), WIDE)],
        cost_estimate=BRIEF,
        name="attend_back",
    )(mixed, weights, context, inverse, grad, inputs)


def expand_kernel(hidden_ref, weight_ref, bias_ref, active_ref, slope_ref, *, chunks):
    step = hidden_ref.shape[0] // chunks
    for i in range(chunks):
        cut = slice(i * step, (i + 1) * step)
        inner = lax.dot_general(hidden_ref[cut], weight_ref[...], NN, preferred_element_type=WIDE)
        inner = inner + bias_ref[...]
        share = 0.5 + 0.5 * lax.erf(inner * math.sqrt(0.5))
        active_ref[cut] = (inner * share).astype(LOW)
        density = jnp.exp(-0.5 * inner * inner) * (1.0 / math.sqrt(2.0 * math.pi))
        slope_ref[cut] = (share + inner * density).astype(LOW)


def expand_gelu(hidden, weight, bias):
    tokens, model_width = hidden.shape
    units = weight.shape[1]
    tile = 768
    return pl.pallas_call(
        functools.partial(expand_kernel, chunks=8),
        grid=(units // tile,),
        in_specs=[
            pl.BlockSpec((tokens, model_width), lambda j: (0, 0)),
            pl.BlockSpec((model_width, tile), lambda j: (0, j)),
            pl.BlockSpec((1, tile), lambda j: (0, j)),
        ],
        out_specs=[pl.BlockSpec((tokens, tile), lambda j: (0, j))] * 2,
        out_shape=[jax.ShapeDtypeStruct((tokens, units), LOW)] * 2,
        cost_estimate=BRIEF,
        name="expand_gelu",
    )(hidden, weight, bias)


def inner_grad_kernel(grad_ref, weight_ref, slope_ref, out_ref, sum_ref, *, chunks):
    step = grad_ref.shape[0] // chunks
    total = jnp.zeros((1, weight_ref.shape[0]), WIDE)
    for i in range(chunks):
        cut = slice(i * step, (i + 1) * step)
        grad = lax.dot_general(grad_ref[cut], weight_ref[...], NT, preferred_element_type=WIDE)
        grad = (grad * slope_ref[cut].astype(WIDE)).astype(LOW)
        out_ref[cut] = grad
        total = total + jnp.sum(grad.astype(WIDE), axis=0, keepdims=True)
    sum_ref[...] = total


def inner_grad(grad, weight, slope):
    tokens, model_width = grad.shape
    units = weight.shape[0]
    tile = 768
    return pl.pallas_call(
        functools.partial(inner_grad_kernel, chunks=4),
        grid=(units // tile,),
        in_specs=[
            pl.BlockSpec((tokens, model_width), lambda j: (0, 0)),
            pl.BlockSpec((tile, model_width), lambda j: (j, 0)),
            pl.BlockSpec((tokens, tile), lambda j: (0, j)),
        ],
        out_specs=[
            pl.BlockSpec((tokens, tile), lambda j: (0, j)),
            pl.BlockSpec((1, tile), lambda j: (0, j)),
        ],
        out_shape=[
            jax.ShapeDtypeStruct((tokens, units), LOW),
            jax.ShapeDtypeStruct((1, units), WIDE),
        ],
        cost_estimate=BRIEF,
        name="inner_grad",
    )(grad, weight, slope)


def first_back_kernel(
    inner_ref, weight_ref, second_ref, value_ref, gain_ref, grad_ref, low_ref, sum_ref
):
    grad = second_ref[...] + lax.dot_general(
        inner_ref[...], weight_ref[...], NT, preferred_element_type=WIDE
    )
    value = value_ref[...]
    centred = value - jnp.mean(value, axis=-1, keepdims=True)
    scale = lax.rsqrt(jnp.mean(centred * centred, axis=-1, keepdims=True) + EPS)
    normal = centred * scale
    product = grad * normal
    grad_normal = grad * gain_ref[...]
    total = (
        scale
        * (
            grad_normal
            - jnp.mean(grad_normal, axis=-1, keepdims=True)
            - normal * jnp.mean(grad_normal * normal, axis=-1, keepdims=True)
        )
    )
    low = total.astype(LOW)
    grad_ref[...] = total
    low_ref[...] = low
    sums = jnp.concatenate(
        [jnp.sum(v, axis=0, keepdims=True) for v in (low.astype(WIDE), product, grad)], axis=0
    )
    first = pl.program_id(0) == 0

    @pl.when(first)
    def _():
        sum_ref[...] = sums

    @pl.when(jnp.logical_not(first))
    def _():
        sum_ref[...] += sums


def first_back(grad_inner, weight, grad_second, value, gain):
    tokens, units = grad_inner.shape
    model_width = weight.shape[0]
    tile = 256
    wide = pl.BlockSpec((tile, model_width), lambda i: (i, 0))
    whole = lambda i: (0, 0)
    return pl.pallas_call(
        first_back_kernel,
        grid=(tokens // tile,),
        in_specs=[
            pl.BlockSpec((tile, units), lambda i: (i, 0)),
            pl.BlockSpec((model_width, units), whole),
            wide,
            wide,
            pl.BlockSpec((1, model_width), whole),
        ],
        out_specs=[wide, wide, pl.BlockSpec((3, model_width), whole)],
        out_shape=[
            jax.ShapeDtypeStruct((tokens, model_width), WIDE),
            jax.ShapeDtypeStruct((tokens, model_width), LOW),
            jax.ShapeDtypeStruct((3, model_width), WIDE),
        ],
        cost_estimate=BRIEF,
        name="first_back",
    )(grad_inner, weight, grad_second, value, gain)


class Wires:
    def __init__(self, fsdp_count):
        self.fsdp_count = fsdp_count
        self.total = 4 * fsdp_count
        self.shard = lax.axis_index("fsdp")
        rep = lax.axis_index("rep")
        self.x = rep >> 1
        self.core = rep & 1
        self.meta = jnp.stack([self.shard, self.x, self.core]).astype(jnp.int32)

    def swap(self, value, mask):
        return lax.ppermute(value, AXES, [(i, i ^ mask) for i in range(self.total)])

    def own_half(self, low, high):
        return jnp.where(self.core == 1, high, low)

    def other_half(self, low, high):
        return jnp.where(self.core == 1, low, high)

    def own_rows(self, value, axis=0):
        half = value.shape[axis] // 2
        low = lax.slice_in_dim(value, 0, half, axis=axis)
        high = lax.slice_in_dim(value, half, 2 * half, axis=axis)
        return jnp.where(self.x == 1, high, low), jnp.where(self.x == 1, low, high)

    def near(self, value):
        return [self.swap(value, 8 * k) for k in range(1, self.fsdp_count // 2)]

    def share(self, near):
        return near + [self.swap(v, 1) for v in near]


    def y_halves(self, held):
        held = held.reshape((held.shape[0] // 2, 2) + held.shape[1:])
        flag = (self.shard & 1) != 0
        return jnp.where(flag, held[:, 1], held[:, 0]), jnp.where(flag, held[:, 0], held[:, 1])

    def z_block(self, held, k):
        return lax.dynamic_index_in_dim(held, (self.shard >> 1) ^ k, 0, keepdims=False)

    def z_sends(self, held):
        if held.shape[0] > 4:
            return [held]
        return [self.z_block(held, k) for k in range(1, held.shape[0])]

    def z_swap(self, sends):
        if sends[0].ndim == 2:
            return [self.swap(v, 8 * (k + 1)) for k, v in enumerate(sends)]
        held, bit = sends[0], 2
        while bit < self.fsdp_count:
            held = held.reshape((held.shape[0] // 2, 2) + held.shape[1:])
            flag = (self.shard & bit) != 0
            got = self.swap(jnp.where(flag, held[:, 0], held[:, 1]), 4 * bit)
            held = add_low(jnp.where(flag, held[:, 1], held[:, 0]), got)
            bit *= 2
        return [held[0]]

    def z_sum(self, held, got):
        if held.shape[0] > 4:
            return got[0]
        return add_low(self.z_block(held, 0), *got)

    def by_x(self, own, other):
        return jnp.where(self.x == 1, other, own), jnp.where(self.x == 1, own, other)


def tie(*values):
    return lax.optimization_barrier(values)


def join(*parts):
    return jnp.concatenate(parts, axis=0)


def row(vector):
    return vector.reshape(1, -1).astype(WIDE)


def add_low(first, *others):
    total = first.astype(WIDE)
    for other in others:
        total = total + other.astype(WIDE)
    return total.astype(LOW)


def weight_copies(meta_ref, refs, out_ref, sem, parts, half_width):
    at = 0
    copies = []
    for width, start, by_x, offset, row in parts:
        for core, x, y in itertools.product(range(2), range(2 if by_x else 1), range(2)):
            piece = refs[at]
            at += 1
            col = (meta_ref[2] ^ core) * half_width + offset
            if by_x:
                col = col + (meta_ref[1] ^ x) * width
            col = pl.multiple_of(col, LANES)
            rows = slice(row, row + piece.shape[1])
            for j in range(piece.shape[0]):
                copies.append(
                    pltpu.make_async_copy(
                        piece.at[j, :, pl.ds(start, width)],
                        out_ref.at[meta_ref[0] ^ (2 * j + y), rows, pl.ds(col, width)],
                        sem,
                    )
                )
    return copies


def assemble_kernel(meta_ref, *refs, parts, half_width):
    copies = weight_copies(meta_ref, refs, refs[-2], refs[-1], parts, half_width)
    for copy in copies:
        copy.start()
    for copy in copies:
        copy.wait()


def project(inputs, weight_ref, query_ref, value_ref, out_ref, pairs):
    group = 3 * LANES
    step = 256
    for i, p in enumerate(pairs):
        cut = slice(i * group, (i + 1) * group)
        weight = weight_ref[..., cut].reshape(inputs.shape[1], group)
        bias = jnp.concatenate(
            [query_ref[p : p + 1], jnp.zeros((1, LANES), WIDE), value_ref[p : p + 1]], axis=1
        )
        for t in range(0, inputs.shape[0], step):
            out = lax.dot_general(inputs[t : t + step], weight, NN, preferred_element_type=WIDE)
            out_ref[t : t + step, cut] = (out + bias).astype(LOW)


def project_kernel(meta_ref, inputs_ref, query_ref, value_ref, *refs, parts, half_width, pairs):
    full_ref, out_ref, sem = refs[-3:]
    copies = weight_copies(meta_ref, refs, full_ref, sem, parts, half_width)
    for copy in copies:
        copy.start()
    for copy in copies:
        copy.wait()
    project(inputs_ref, full_ref, query_ref, value_ref, out_ref, pairs)


def project_whole_kernel(inputs_ref, query_ref, value_ref, full_ref, *refs, pairs):
    project(inputs_ref, full_ref, query_ref, value_ref, refs[-1], pairs)


def joint_project(wires, inputs, pieces, query_bias, value_bias, chunk, shard_rows, behind=()):
    tokens, model_width = inputs.shape
    half_width = chunk.count * 3 * LANES
    out_shape = jax.ShapeDtypeStruct((tokens, 2 * half_width), LOW)
    on_chip = pl.BlockSpec(memory_space=pltpu.VMEM)
    anywhere = pl.BlockSpec(memory_space=pl.ANY)
    cost = BRIEF
    if not isinstance(pieces, list):
        out = pl.pallas_call(
            functools.partial(project_whole_kernel, pairs=chunk.pairs),
            out_shape=out_shape,
            in_specs=[on_chip] * 4 + [anywhere] * len(behind),
            out_specs=on_chip,
            cost_estimate=cost,
            name="joint_project",
        )(inputs, query_bias, value_bias, pieces, *behind)
        return pieces, out
    full, out = pl.pallas_call(
        functools.partial(
            project_kernel,
            parts=[(half_width, 0, False, 0, 0)],
            half_width=half_width,
            pairs=chunk.pairs,
        ),
        out_shape=[
            jax.ShapeDtypeStruct((wires.fsdp_count, shard_rows, 2 * half_width), LOW),
            out_shape,
        ],
        in_specs=[pl.BlockSpec(memory_space=pltpu.SMEM)]
        + [on_chip] * 3
        + [anywhere] * (len(pieces) + len(behind)),
        out_specs=[on_chip] * 2,
        scratch_shapes=[pltpu.SemaphoreType.DMA],
        cost_estimate=cost,
        name="joint_project",
    )(wires.meta, inputs, query_bias, value_bias, *pieces, *behind)
    return full.reshape(model_width, 2 * half_width), out


def pack_kernel(*refs, chunks, wide):
    *vector_refs, out_ref = refs
    sum_refs, vector_refs = vector_refs[: len(chunks)], vector_refs[len(chunks) :]
    out_ref[...] = jnp.zeros_like(out_ref)
    for ref, chunk in zip(sum_refs, chunks):
        for i, p in enumerate(chunk.pairs):
            total = ref[0, i, 0:1]
            for r in range(1, ref.shape[0]):
                total = total + ref[r, i, 0:1]
            out_ref[0:1, p * LANES : (p + 1) * LANES] = total[:, :LANES]
            out_ref[1:2, p * LANES : (p + 1) * LANES] = total[:, 2 * LANES :]
    row = 2
    for ref in vector_refs:
        for r, start in itertools.product(range(ref.shape[0]), range(0, ref.shape[1], wide)):
            out_ref[row : row + 1] = ref[r : r + 1, start : start + wide]
            row += 1


def pack(sums, chunks, vectors, wide):
    rows = 2 + sum(v.shape[0] * v.shape[1] // wide for v in vectors)
    return pl.pallas_call(
        functools.partial(pack_kernel, chunks=chunks, wide=wide),
        out_shape=jax.ShapeDtypeStruct(((rows + 7) // 8 * 8, wide), WIDE),
        name="pack",
    )(*sums, *vectors)


def assemble(wires, shard_rows, half_width, parts):
    count = wires.fsdp_count
    operands, plan = [], []
    for pieces, *where in parts:
        plan.append(where)
        operands += pieces
    shape = (count, shard_rows, 2 * half_width)
    full = pl.pallas_call(
        functools.partial(assemble_kernel, parts=plan, half_width=half_width),
        out_shape=jax.ShapeDtypeStruct(shape, LOW),
        in_specs=[pl.BlockSpec(memory_space=pltpu.SMEM)]
        + [pl.BlockSpec(memory_space=pl.ANY)] * len(operands),
        out_specs=pl.BlockSpec(memory_space=pltpu.VMEM),
        scratch_shapes=[pltpu.SemaphoreType.DMA],
        cost_estimate=BRIEF,
        name="assemble",
    )(wires.meta, *operands)
    return full.reshape(count * shard_rows, 2 * half_width)


def pair_columns(array, pairs, model_width):
    return jnp.concatenate(
        [
            array[..., part * model_width + p * LANES : part * model_width + (p + 1) * LANES]
            for p in pairs
            for part in range(3)
        ],
        axis=-1,
    )


def natural_columns(pieces, chunks):
    where = {}
    for piece, chunk in zip(pieces, chunks):
        for i, p in enumerate(chunk.pairs):
            for part in range(3):
                place = (3 * i + part) * LANES
                where[(part, p)] = piece[..., place : place + LANES]
    return jnp.concatenate([where[key] for key in sorted(where)], axis=-1)


def body(
    fsdp_count,
    layer_input,
    segment_ids,
    joint_weight,
    query_bias,
    value_bias,
    close_weight,
    close_bias,
    first_gain,
    first_shift,
    expand_weight,
    expand_bias,
    shrink_weight,
    shrink_bias,
    second_gain,
    second_shift,
    cotangent,
):
    row_count, pos_count, model_width = layer_input.shape
    hidden_units = expand_bias.shape[0]
    tok_count = row_count * pos_count
    flat_input = layer_input.reshape(tok_count, model_width)
    wires = Wires(fsdp_count)
    half_pairs = model_width // LANES // 2
    chunks = (Chunk(0, 1, half_pairs), Chunk(1, half_pairs - 1, half_pairs))
    shard_rows = joint_weight.shape[0]

    joint_pieces = []
    for chunk in chunks:
        low, high = (
            pair_columns(joint_weight, chunk.pairs[c * chunk.count : (c + 1) * chunk.count], model_width)
            for c in range(2)
        )
        joint_pieces.append(wires.own_half(low, high))
    half_model, half_hidden = model_width // 2, hidden_units // 2
    unit = half_hidden // 3
    expand_half = wires.own_half(expand_weight[:, :half_hidden], expand_weight[:, half_hidden:])
    close_half = wires.own_half(close_weight[:, :half_model], close_weight[:, half_model:])
    shrink_half = wires.own_half(shrink_weight[:, :half_model], shrink_weight[:, half_model:])
    shrink_rows = shrink_half.shape[0] // 2
    aligned = fsdp_count == 8 and shard_rows % 32 == 0
    query_rows = query_bias.astype(WIDE).reshape(-1, LANES)
    value_rows = value_bias.astype(WIDE).reshape(-1, LANES)

    inputs_t = jnp.swapaxes(layer_input, 1, 2)
    segments = segment_ids[:, :, None], segment_ids[:, None, :]

    def project_and_attend(place, shared, context):
        full, part = joint_project(
            wires, flat_input, shared, query_rows, value_rows, chunks[place], shard_rows
        )
        return full, part.reshape(row_count, pos_count, -1)

    if aligned:
        first, second = joint_pieces[0][None], joint_pieces[1][None]
        mixed_piece = jnp.concatenate([expand_half[:, :unit], close_half], axis=1)[None]
        split = wires.by_x(expand_half[:, unit : 2 * unit], expand_half[:, 2 * unit :])[0][None]
        top, bottom = shrink_half[None, :shrink_rows], shrink_half[None, shrink_rows:]
        first_near = wires.near(first)
        first = join(first, *first_near)
        first, second, inputs_t, *segments = tie(first, second, inputs_t, *segments)
        first_y = wires.swap(first, 4)
        second_near = wires.near(second)
        first, first_y, second_near[0], second_near[1] = tie(
            first, first_y, second_near[0], second_near[1]
        )
        first_shared = wires.share([first, first_y])
        *first_shared, split, second, second_near[0], second_near[1], second_near[2] = tie(
            *first_shared, split, second, *second_near
        )
        second = join(second, *second_near)
        second_y = wires.swap(second, 4)
        split_near = wires.near(split)
        full, part = project_and_attend(0, first_shared, None)
        joint_full, mixed = [full], [part]
        mixed[0], mixed_piece = tie(mixed[0], mixed_piece)
        piece_near = wires.near(mixed_piece)
        context, w, inv = attend(mixed[0], segments, chunks[0])
        weights, inverse = [w], [inv]
        context, second, second_y, split, *split_near = tie(
            context, second, second_y, split, *split_near
        )
        second_shared = wires.share([second, second_y])
        split = join(split, *split_near)
        split_y = wires.swap(split, 4)
        split_x = wires.swap(split, 2)
        full, part = project_and_attend(1, second_shared, context)
        joint_full.append(full)
        part, split, split_x, split_y, mixed_piece, top, *piece_near = tie(
            part, split, split_x, split_y, mixed_piece, top, *piece_near
        )
        mixed.append(part)
        split_yx = wires.swap(split_y, 2)
        mixed_piece = join(mixed_piece, *piece_near)
        piece_y = wires.swap(mixed_piece, 4)
        top_near = wires.near(top)
        context, w, inv = attend(mixed[1], segments, chunks[1], context)
        weights.append(w)
        inverse.append(inv)
        context, split, split_x, split_y, split_yx, mixed_piece, piece_y, top, bottom, *top_near = tie(
            context, split, split_x, split_y, split_yx, mixed_piece, piece_y, top, bottom, *top_near
        )
        top = join(top, *top_near)
        top_y = wires.swap(top, 4)
        bottom_near = wires.near(bottom)
        plain_shared = wires.share([mixed_piece, piece_y])
        split_shared = wires.share([split, split_y, split_x, split_yx])
        close_full = assemble(
            wires, shard_rows, half_model, [(plain_shared, half_model, unit, False, 0, 0)]
        )
        expand_full = assemble(
            wires,
            shard_rows,
            half_hidden,
            [(plain_shared, unit, 0, False, 0, 0), (split_shared, unit, 0, True, unit, 0)],
        )
    else:
        joint_full, mixed, weights, inverse = [], [], [], []
        context = None
        for place, chunk in enumerate(chunks):
            shared = lax.all_gather(
                pair_columns(joint_weight, chunk.pairs, model_width), "fsdp", axis=0, tiled=True
            )
            full, part = project_and_attend(place, shared, context)
            joint_full.append(full)
            mixed.append(part)
            context, w, inv = attend(part, segments, chunk, context)
            weights.append(w)
            inverse.append(inv)
        close_full, expand_full, shrink_full = (
            lax.all_gather(w, "fsdp", axis=0, tiled=True)
            for w in (close_weight, expand_weight, shrink_weight)
        )
    context_low = context.reshape(tok_count, model_width)

    branch = jnp.dot(context_low, close_full, preferred_element_type=WIDE) + row(close_bias)
    first_sum = flat_input.astype(WIDE) + branch
    hidden = layer_norm(first_sum, row(first_gain), row(first_shift))
    hidden_low = hidden.astype(LOW)
    if aligned:
        hidden_low, expand_full, top, top_y, bottom, *bottom_near = tie(
            hidden_low, expand_full, top, top_y, bottom, *bottom_near
        )
        bottom = join(bottom, *bottom_near)
        bottom_y = wires.swap(bottom, 4)
    active_low, slope = expand_gelu(hidden_low, expand_full, row(expand_bias))
    if aligned:
        active_low, top, top_y, bottom, bottom_y = tie(
            active_low, top, top_y, bottom, bottom_y
        )
        shrink_full = assemble(
            wires,
            shrink_weight.shape[0],
            half_model,
            [
                (wires.share([top, top_y]), half_model, 0, False, 0, 0),
                (wires.share([bottom, bottom_y]), half_model, 0, False, 0, shrink_rows),
            ],
        )
    ffn_out = jnp.dot(active_low, shrink_full, preferred_element_type=WIDE) + row(shrink_bias)
    output, second_pull = jax.vjp(
        layer_norm, hidden + ffn_out, row(second_gain), row(second_shift)
    )
    layer_output = output.astype(LOW).reshape(row_count, pos_count, model_width)
    grad_second, second_gain_part, second_shift_part = second_pull(
        cotangent.reshape(tok_count, model_width).astype(WIDE)
    )
    grad_ffn = grad_second.astype(LOW)

    def outgoing(left, right):
        half = right.shape[1] // 2
        send = wires.other_half(right[:, :half], right[:, half:])
        return jnp.einsum("tf,td->fd", left, send, preferred_element_type=WIDE).astype(LOW)

    def kept(left, right):
        half = right.shape[1] // 2
        keep = wires.own_half(right[:, :half], right[:, half:])
        return jnp.einsum("tf,td->fd", left, keep, preferred_element_type=WIDE)

    def by_shard(held):
        return held.reshape(fsdp_count, held.shape[0] // fsdp_count, held.shape[1])

    def staying(left, right, got):
        return by_shard(add_low(kept(left, right), got))

    def both_halves(mine):
        other = wires.swap(mine, 1)
        return wires.own_half(mine, other), wires.own_half(other, mine)

    shrink_send = outgoing(active_low, grad_ffn)
    active_low, shrink_send = tie(active_low, shrink_send)
    shrink_got = wires.swap(shrink_send, 1)
    shrink_keep = kept(active_low, grad_ffn)
    grad_ffn, shrink_keep, shrink_got = tie(grad_ffn, shrink_keep, shrink_got)
    shrink_held = by_shard(add_low(shrink_keep, shrink_got))
    top_keep, top_send = wires.y_halves(shrink_held[:, :shrink_rows])
    low_keep, low_send = wires.own_rows(shrink_held[:, shrink_rows:], axis=1)
    grad_ffn, top_keep, top_send, low_keep, low_send = tie(
        grad_ffn, top_keep, top_send, low_keep, low_send
    )
    top_got = wires.swap(top_send, 4)
    low_got = wires.swap(low_send, 2)
    grad_inner, inner_sum = inner_grad(grad_ffn, shrink_full, slope)
    grad_inner, top_keep, top_got, low_keep, low_got = tie(
        grad_inner, top_keep, top_got, low_keep, low_got
    )
    low_keep, low_send = wires.y_halves(add_low(low_keep, low_got))
    top_held = add_low(top_keep, top_got)
    hidden_low, low_keep, low_send = tie(hidden_low, low_keep, low_send)
    low_got = wires.swap(low_send, 4)
    expand_send = outgoing(hidden_low, grad_inner)
    hidden_low, expand_send = tie(hidden_low, expand_send)
    expand_got = wires.swap(expand_send, 1)
    expand_keep = kept(hidden_low, grad_inner)
    grad_inner, expand_keep, expand_got = tie(grad_inner, expand_keep, expand_got)
    expand_held = by_shard(add_low(expand_keep, expand_got))
    quarter = half_hidden // 2
    left_keep, left_send = wires.y_halves(expand_held[..., :quarter])
    right_keep, right_send = wires.by_x(
        expand_held[..., quarter : quarter + quarter // 2],
        expand_held[..., quarter + quarter // 2 :],
    )
    (
        grad_inner,
        left_keep,
        left_send,
        right_keep,
        right_send,
        low_keep,
        low_got,
        top_held,
        *top_sends,
    ) = tie(
        grad_inner,
        left_keep,
        left_send,
        right_keep,
        right_send,
        low_keep,
        low_got,
        top_held,
        *wires.z_sends(top_held),
    )
    top_got = wires.z_swap(top_sends)
    left_got = wires.swap(left_send, 4)
    right_got = wires.swap(right_send, 2)
    grad_first, grad_branch, first_sums = first_back(
        grad_inner, expand_full, grad_second, first_sum, row(first_gain)
    )
    grad_branch, left_keep, left_got, right_keep, right_got, top_held, *top_got = tie(
        grad_branch, left_keep, left_got, right_keep, right_got, top_held, *top_got
    )
    right_keep, right_send = wires.y_halves(add_low(right_keep, right_got))
    grad_branch, right_keep, right_send = tie(grad_branch, right_keep, right_send)
    right_got = wires.swap(right_send, 4)
    top_mine = wires.z_sum(top_held, top_got)
    mid_held = jnp.concatenate([add_low(left_keep, left_got), add_low(low_keep, low_got)], axis=2)
    context_low, grad_branch = tie(context_low, grad_branch)
    close_send = outgoing(context_low, grad_branch)
    grad_branch, close_send = tie(grad_branch, close_send)
    close_got = wires.swap(close_send, 1)
    grad_context = jnp.einsum(
        "te,de->td", grad_branch, close_full, preferred_element_type=WIDE
    ).astype(LOW)
    context_low, grad_context, close_got = tie(context_low, grad_context, close_got)
    close_held = staying(context_low, grad_branch, close_got)
    grad_context = grad_context.reshape(row_count, pos_count, model_width)
    close_keep, close_send = wires.y_halves(close_held)
    (
        grad_context,
        close_keep,
        close_send,
        right_keep,
        right_got,
        top_mine,
        mid_held,
        *mid_sends,
    ) = tie(
        grad_context,
        close_keep,
        close_send,
        right_keep,
        right_got,
        top_mine,
        mid_held,
        *wires.z_sends(mid_held),
    )
    top_other = wires.swap(top_mine, 2)
    close_got = wires.swap(close_send, 4)
    mid_got = wires.z_swap(mid_sends)

    grad_mixed, bias_sums, joint_parts = {}, {}, {}
    grad_mixed[1], bias_sums[1], joint_parts[1] = attend_back(
        mixed[1], weights[1], context, inverse[1], grad_context, inputs_t, chunks[1]
    )
    grad_mixed[1] = grad_mixed[1].reshape(tok_count, -1)
    large, close_keep, close_got, top_mine, top_other, mid_held, *mid_got = tie(
        joint_parts[1], close_keep, close_got, top_mine, top_other, mid_held, *mid_got
    )
    large_got = wires.swap(wires.other_half(large[0], large[1]), 1)
    second_held = add_low(
        jnp.concatenate([right_keep, close_keep], axis=2),
        jnp.concatenate([right_got, close_got], axis=2),
    )
    large, large_got, second_held, *second_sends = tie(
        large, large_got, second_held, *wires.z_sends(second_held)
    )
    second_got = wires.z_swap(second_sends)
    large_keep, large_send = wires.own_rows(
        by_shard(add_low(wires.own_half(large[0], large[1]), large_got)), axis=1
    )
    grad_context, large_keep, large_send = tie(grad_context, large_keep, large_send)
    large_got = wires.swap(large_send, 2)
    grad_mixed[0], bias_sums[0], joint_parts[0] = attend_back(
        mixed[0], weights[0], context, inverse[0], grad_context, inputs_t, chunks[0]
    )
    grad_mixed[0] = grad_mixed[0].reshape(tok_count, -1)
    small, large_keep, large_got, second_held, *second_got = tie(
        joint_parts[0], large_keep, large_got, second_held, *second_got
    )
    small_got = wires.swap(wires.other_half(small[0], small[1]), 1)

    def column_sum(value):
        return jnp.sum(value.astype(WIDE), axis=0, keepdims=True)

    packed = pack(
        [bias_sums[0], bias_sums[1]],
        chunks,
        [
            first_sums,
            column_sum(grad_ffn),
            second_gain_part,
            second_shift_part,
            inner_sum,
        ],
        model_width,
    )

    small, small_got, packed = tie(small, small_got, packed)
    vector_got = wires.swap(packed, 1)
    small_keep, small_send = wires.y_halves(
        by_shard(add_low(wires.own_half(small[0], small[1]), small_got))
    )
    small_keep, small_send, large_keep, packed, vector_got = tie(
        small_keep, small_send, large_keep, packed, vector_got
    )
    small_got = wires.swap(small_send, 4)
    large_keep, large_send = wires.y_halves(add_low(large_keep, large_got))
    packed = packed + vector_got
    mine = jnp.concatenate(
        [wires.z_sum(mid_held, mid_got), wires.z_sum(second_held, second_got)], axis=1
    )
    grad_mixed[0], grad_mixed[1], large_keep, large_send, packed, mine = tie(
        grad_mixed[0], grad_mixed[1], large_keep, large_send, packed, mine
    )
    other = wires.swap(mine, 2)
    large_got = wires.swap(large_send, 4)
    vector_got = wires.swap(packed, 2)
    input_grad = grad_first + jnp.einsum(
        "te,de->td", grad_mixed[0], joint_full[0], preferred_element_type=WIDE
    )
    input_grad, packed, vector_got = tie(input_grad, packed, vector_got)
    packed = packed + vector_got
    vector_got = wires.swap(packed, 4)
    input_grad = input_grad + jnp.einsum(
        "te,de->td", grad_mixed[1], joint_full[1], preferred_element_type=WIDE
    )
    input_grad, small_keep, small_got, large_keep, large_got, packed, vector_got, mine, other = tie(
        input_grad, small_keep, small_got, large_keep, large_got, packed, vector_got, mine, other
    )
    small_held = add_low(small_keep, small_got)
    half_rows = small_held.shape[1] // 2
    joint_held = jnp.concatenate(
        [small_held[:, :half_rows], small_held[:, half_rows:], add_low(large_keep, large_got)],
        axis=2,
    )
    packed = packed + vector_got
    packed, joint_held, *joint_sends = tie(packed, joint_held, *wires.z_sends(joint_held))
    joint_got = wires.z_swap(joint_sends)
    vector_got = wires.swap(packed, 8)
    joint_held, packed, vector_got, *joint_got = tie(
        joint_held, packed, vector_got, *joint_got
    )
    joint_mine, packed = tie(wires.z_sum(joint_held, joint_got), packed + vector_got)

    top_mine = add_low(top_mine, top_other)
    total = add_low(mine, other)
    cuts = [quarter, quarter + half_model, quarter + half_model + quarter // 2]
    left, _, _, close = jnp.split(total, cuts, axis=1)
    (_, low, right, _), (_, low_other, right_other, _) = (
        jnp.split(v, cuts, axis=1) for v in (mine, other)
    )
    shrink_mine = jnp.concatenate([top_mine, *wires.by_x(low, low_other)], axis=0)
    second_mine = jnp.concatenate([left, *wires.by_x(right, right_other), close], axis=1)
    joint_other = wires.swap(joint_mine, 2)
    vector_got = wires.swap(packed, 16)
    joint_mine, joint_other, packed, vector_got = tie(
        joint_mine, joint_other, packed, vector_got
    )
    small_width = small_held.shape[2]
    small_mine = add_low(joint_mine[:, : 2 * small_width], joint_other[:, : 2 * small_width])
    joint_mine = jnp.concatenate(
        [
            jnp.concatenate([small_mine[:, :small_width], small_mine[:, small_width:]], axis=0),
            jnp.concatenate(
                wires.by_x(joint_mine[:, 2 * small_width :], joint_other[:, 2 * small_width :]),
                axis=0,
            ),
        ],
        axis=1,
    )

    shrink_grad = jnp.concatenate(both_halves(shrink_mine), axis=1).astype(WIDE)
    low, high = both_halves(second_mine)
    cut = hidden_units // 2
    expand_grad = jnp.concatenate([low[:, :cut], high[:, :cut]], axis=1).astype(WIDE)
    close_grad = jnp.concatenate([low[:, cut:], high[:, cut:]], axis=1).astype(WIDE)
    joint_mine, summed = tie(joint_mine, packed + vector_got)
    low, high = both_halves(joint_mine)
    mask = 32
    while mask < wires.total:
        summed = summed + wires.swap(summed, mask)
        mask *= 2
    cut = chunks[0].count * 3 * LANES
    joint_grad = natural_columns(
        [
            jnp.concatenate([low[:, :cut], high[:, :cut]], axis=1),
            jnp.concatenate([low[:, cut:], high[:, cut:]], axis=1),
        ],
        chunks,
    ).astype(WIDE)
    (
        query_bias_grad,
        value_bias_grad,
        close_bias_grad,
        first_gain_grad,
        first_shift_grad,
        shrink_bias_grad,
        second_gain_grad,
        second_shift_grad,
    ) = (summed[i] for i in range(8))
    expand_bias_grad = summed[8 : 8 + hidden_units // model_width].reshape(hidden_units)
    return (
        layer_output,
        input_grad.reshape(row_count, pos_count, model_width),
        joint_grad,
        query_bias_grad,
        value_bias_grad,
        close_grad,
        close_bias_grad,
        first_gain_grad,
        first_shift_grad,
        expand_grad,
        expand_bias_grad,
        shrink_grad,
        shrink_bias_grad,
        second_gain_grad,
        second_shift_grad,
    )


def solution(mesh):
    rows = P(("fsdp", "rep"), None, None)
    sharded = P("fsdp", None)
    copied = P()
    return jax.shard_map(
        functools.partial(body, mesh.shape["fsdp"]),
        mesh=mesh,
        in_specs=(
            rows,
            P(("fsdp", "rep"), None),
            sharded,
            copied,
            copied,
            sharded,
            copied,
            copied,
            copied,
            sharded,
            copied,
            sharded,
            copied,
            copied,
            copied,
            rows,
        ),
        out_specs=(
            rows,
            rows,
            sharded,
            copied,
            copied,
            sharded,
            copied,
            copied,
            copied,
            sharded,
            copied,
            sharded,
            copied,
            copied,
            copied,
        ),
        check_vma=False,
    )
```

```python
import functools
import itertools
import math

import jax
import jax.numpy as jnp
from jax import lax
from jax.experimental import pallas as pl
from jax.experimental.pallas import tpu as pltpu
from jax.sharding import PartitionSpec as P

HEADS = 12
EPS = 1e-12
AXES = ("fsdp", "rep")
LANES = 128
NT = (((1,), (1,)), ((), ()))
NN = (((1,), (0,)), ((), ()))
LOW = jnp.bfloat16
WIDE = jnp.float32
BRIEF = pl.CostEstimate(flops=0, bytes_accessed=0, transcendentals=0)


def attend_kernel(mixed_ref, seg_col_ref, seg_row_ref, *refs):
    context_ref, weights_ref, inverse_ref = refs[-3:]
    pos = mixed_ref.shape[0]
    head = mixed_ref.shape[1] // 6
    same = seg_col_ref[...] == seg_row_ref[...]
    values_t = mixed_ref[:, 4 * head : 6 * head].T
    ones = jnp.ones((16, pos), LOW)
    outs, inverses = [], []
    for h in range(2):
        queries = mixed_ref[:, h * head : (h + 1) * head] * LOW(1.0 / math.sqrt(head))
        keys = mixed_ref[:, (2 + h) * head : (3 + h) * head]
        scores = lax.dot_general(keys, queries, NT, preferred_element_type=WIDE)
        scores = jnp.where(same, scores, -jnp.inf)
        raised = jnp.exp(scores - jnp.max(scores, axis=0, keepdims=True)).astype(LOW)
        weights_ref[h] = raised
        extended = jnp.concatenate([values_t[h * head : (h + 1) * head], ones], axis=0)
        out = lax.dot_general(extended, raised, NN, preferred_element_type=WIDE)
        inverse = 1.0 / out[head : head + 1]
        outs.append(out[:head] * inverse)
        inverses.append(jnp.broadcast_to(inverse, (head, pos)))
    context_ref[...] = jnp.concatenate(outs, axis=0).T.astype(LOW)
    inverse_ref[...] = jnp.concatenate(inverses, axis=0).T


def attend_back_kernel(
    mixed_ref,
    weights_ref,
    context_ref,
    inverse_ref,
    grad_ref,
    inputs_ref,
    out_ref,
    sum_ref,
    joint_ref,
    total_ref,
):
    row = pl.program_id(1)
    head = mixed_ref.shape[1] // 6
    scale = LOW(1.0 / math.sqrt(head))
    grad = grad_ref[...].astype(WIDE) * inverse_ref[...]
    product = (grad * context_ref[...].astype(WIDE)).astype(LOW)
    grad_low = grad.astype(LOW)
    queries = mixed_ref[:, : 2 * head] * scale
    keys_t = (mixed_ref[:, 2 * head : 4 * head] * scale).T
    ones = jnp.ones((8, head), LOW)
    grad_q, grad_k, grad_v = [], [], []
    for h in range(2):
        cut = slice(h * head, (h + 1) * head)
        values = mixed_ref[:, (4 + h) * head : (5 + h) * head]
        inner = lax.dot_general(ones, product[:, cut], NT, preferred_element_type=WIDE)[0:1]
        raised = weights_ref[h]
        grad_attn = lax.dot_general(values, grad_low[:, cut], NT, preferred_element_type=WIDE)
        grad_scores = raised * (grad_attn - inner).astype(LOW)
        grad_k.append(lax.dot_general(grad_scores, queries[:, cut], NN, preferred_element_type=WIDE))
        grad_v.append(lax.dot_general(raised, grad_low[:, cut], NN, preferred_element_type=WIDE))
        grad_q.append(lax.dot_general(keys_t[cut], grad_scores, NN, preferred_element_type=WIDE))
    out = jnp.concatenate([jnp.concatenate(grad_q, axis=0).T] + grad_k + grad_v, axis=1).astype(LOW)
    out_ref[...] = out
    sum_ref[...] = jnp.broadcast_to(
        jnp.sum(out.astype(WIDE), axis=0, keepdims=True), sum_ref.shape
    )
    part = lax.dot_general(inputs_ref[row], out, NN, preferred_element_type=WIDE)

    @pl.when(row == 0)
    def _():
        total_ref[...] = part

    @pl.when(row > 0)
    def _():
        total_ref[...] += part

    @pl.when(row == pl.num_programs(1) - 1)
    def _():
        joint_ref[...] = total_ref[...].astype(LOW)


class Chunk:
    def __init__(self, first, count, half):
        self.first, self.count, self.half = first, count, half
        self.pairs = [c * half + first + i for c in range(2) for i in range(count)]

    def block(self, place):
        return (place // self.count) * self.half + self.first + place % self.count


def attend(mixed, segments, chunk, context=None, behind=()):
    rows, pos, width = mixed.shape
    group = width // len(chunk.pairs)
    pair = group // 3
    count = len(chunk.pairs)
    total = 2 * chunk.half
    in_specs = [
        pl.BlockSpec((None, pos, group), lambda r, p: (r, 0, p)),
        pl.BlockSpec((None, pos, 1), lambda r, p: (r, 0, 0)),
        pl.BlockSpec((None, 1, pos), lambda r, p: (r, 0, 0)),
    ]
    operands = [mixed, *segments]
    aliases = {}
    if context is not None:
        in_specs.append(pl.BlockSpec(memory_space=pl.ANY))
        operands.append(context)
        aliases = {3: 0}
    in_specs += [pl.BlockSpec(memory_space=pl.ANY)] * len(behind)
    operands += behind
    return pl.pallas_call(
        attend_kernel,
        grid=(rows, count),
        in_specs=in_specs,
        out_specs=[
            pl.BlockSpec((None, pos, pair), lambda r, p: (r, 0, chunk.block(p))),
            pl.BlockSpec((None, None, 2, pos, pos), lambda r, p: (r, p, 0, 0, 0)),
            pl.BlockSpec((None, pos, pair), lambda r, p: (r, 0, p)),
        ],
        out_shape=[
            jax.ShapeDtypeStruct((rows, pos, total * pair), LOW),
            jax.ShapeDtypeStruct((rows, count, 2, pos, pos), LOW),
            jax.ShapeDtypeStruct((rows, pos, count * pair), WIDE),
        ],
        input_output_aliases=aliases,
        cost_estimate=BRIEF,
        name="attend",
    )(*operands)


def attend_back(mixed, weights, context, inverse, grad, inputs, chunk):
    rows, pos, width = mixed.shape
    model_width = inputs.shape[1]
    count = len(chunk.pairs)
    group = width // count
    pair = group // 3
    natural = pl.BlockSpec((None, pos, pair), lambda p, r: (r, 0, chunk.block(p)))
    return pl.pallas_call(
        attend_back_kernel,
        grid=(count, rows),
        in_specs=[
            pl.BlockSpec((None, pos, group), lambda p, r: (r, 0, p)),
            pl.BlockSpec((None, None, 2, pos, pos), lambda p, r: (r, p, 0, 0, 0)),
            natural,
            pl.BlockSpec((None, pos, pair), lambda p, r: (r, 0, p)),
            natural,
            pl.BlockSpec((rows, model_width, pos), lambda p, r: (0, 0, 0)),
        ],
        out_specs=[
            pl.BlockSpec((None, pos, group), lambda p, r: (r, 0, p)),
            pl.BlockSpec((None, None, 8, group), lambda p, r: (r, p, 0, 0)),
            pl.BlockSpec(
                (None, model_width, group),
                lambda p, r: (p // chunk.count, 0, p % chunk.count),
            ),
        ],
        out_shape=[
            jax.ShapeDtypeStruct((rows, pos, count * group), LOW),
            jax.ShapeDtypeStruct((rows, count, 8, group), WIDE),
            jax.ShapeDtypeStruct((2, model_width, chunk.count * group), LOW),
        ],
        scratch_shapes=[pltpu.VMEM((model_width, group), WIDE)],
        cost_estimate=BRIEF,
        name="attend_back",
    )(mixed, weights, context, inverse, grad, inputs)


def expand_kernel(hidden_ref, weight_ref, bias_ref, active_ref, slope_ref, *, chunks):
    step = hidden_ref.shape[0] // chunks
    for i in range(chunks):
        cut = slice(i * step, (i + 1) * step)
        inner = lax.dot_general(hidden_ref[cut], weight_ref[...], NN, preferred_element_type=WIDE)
        inner = inner + bias_ref[...]
        share = 0.5 + 0.5 * lax.erf(inner * math.sqrt(0.5))
        active_ref[cut] = (inner * share).astype(LOW)
        density = jnp.exp(-0.5 * inner * inner) * (1.0 / math.sqrt(2.0 * math.pi))
        slope_ref[cut] = (share + inner * density).astype(LOW)


def expand_gelu(hidden, weight, bias):
    tokens, model_width = hidden.shape
    units = weight.shape[1]
    tile = 768
    return pl.pallas_call(
        functools.partial(expand_kernel, chunks=8),
        grid=(units // tile,),
        in_specs=[
            pl.BlockSpec((tokens, model_width), lambda j: (0, 0)),
            pl.BlockSpec((model_width, tile), lambda j: (0, j)),
            pl.BlockSpec((1, tile), lambda j: (0, j)),
        ],
        out_specs=[pl.BlockSpec((tokens, tile), lambda j: (0, j))] * 2,
        out_shape=[jax.ShapeDtypeStruct((tokens, units), LOW)] * 2,
        cost_estimate=BRIEF,
        name="expand_gelu",
    )(hidden, weight, bias)


def inner_grad_kernel(grad_ref, weight_ref, slope_ref, out_ref, sum_ref, *, chunks):
    step = grad_ref.shape[0] // chunks
    total = jnp.zeros((1, weight_ref.shape[0]), WIDE)
    for i in range(chunks):
        cut = slice(i * step, (i + 1) * step)
        grad = lax.dot_general(grad_ref[cut], weight_ref[...], NT, preferred_element_type=WIDE)
        grad = (grad * slope_ref[cut].astype(WIDE)).astype(LOW)
        out_ref[cut] = grad
        total = total + jnp.sum(grad.astype(WIDE), axis=0, keepdims=True)
    sum_ref[...] = total


def inner_grad(grad, weight, slope):
    tokens, model_width = grad.shape
    units = weight.shape[0]
    tile = 768
    return pl.pallas_call(
        functools.partial(inner_grad_kernel, chunks=2),
        grid=(units // tile,),
        in_specs=[
            pl.BlockSpec((tokens, model_width), lambda j: (0, 0)),
            pl.BlockSpec((tile, model_width), lambda j: (j, 0)),
            pl.BlockSpec((tokens, tile), lambda j: (0, j)),
        ],
        out_specs=[
            pl.BlockSpec((tokens, tile), lambda j: (0, j)),
            pl.BlockSpec((1, tile), lambda j: (0, j)),
        ],
        out_shape=[
            jax.ShapeDtypeStruct((tokens, units), LOW),
            jax.ShapeDtypeStruct((1, units), WIDE),
        ],
        cost_estimate=BRIEF,
        name="inner_grad",
    )(grad, weight, slope)


def standardise(value):
    centred = value - jnp.mean(value, axis=-1, keepdims=True)
    scale = lax.rsqrt(jnp.mean(centred * centred, axis=-1, keepdims=True) + EPS)
    return centred * scale, scale


def norm_back(grad, normal, scale, gain):
    grad_normal = grad * gain
    return scale * (
        grad_normal
        - jnp.mean(grad_normal, axis=-1, keepdims=True)
        - normal * jnp.mean(grad_normal * normal, axis=-1, keepdims=True)
    )


def add_sums(sum_ref, *values):
    sums = jnp.concatenate([jnp.sum(v, axis=0, keepdims=True) for v in values], axis=0)
    first = pl.program_id(0) == 0

    @pl.when(first)
    def _():
        sum_ref[...] = sums

    @pl.when(jnp.logical_not(first))
    def _():
        sum_ref[...] += sums


def first_kernel(
    context_ref, weight_ref, bias_ref, inputs_ref, gain_ref, shift_ref, sum_ref, low_ref
):
    branch = lax.dot_general(
        context_ref[...], weight_ref[...], NN, preferred_element_type=WIDE
    )
    total = inputs_ref[...].astype(WIDE) + (branch + bias_ref[...])
    sum_ref[...] = total
    low_ref[...] = (standardise(total)[0] * gain_ref[...] + shift_ref[...]).astype(LOW)


def first_norm(context, weight, bias, inputs, gain, shift):
    tokens, model_width = context.shape
    tile = 512
    block = pl.BlockSpec((tile, model_width), lambda i: (i, 0))
    line = pl.BlockSpec((1, model_width), lambda i: (0, 0))
    return pl.pallas_call(
        first_kernel,
        grid=(tokens // tile,),
        in_specs=[
            block,
            pl.BlockSpec((model_width, model_width), lambda i: (0, 0)),
            line,
            block,
            line,
            line,
        ],
        out_specs=[block, block],
        out_shape=[
            jax.ShapeDtypeStruct((tokens, model_width), WIDE),
            jax.ShapeDtypeStruct((tokens, model_width), LOW),
        ],
        cost_estimate=BRIEF,
        name="first_norm",
    )(context, weight, bias, inputs, gain, shift)


def second_kernel(
    active_ref,
    weight_ref,
    bias_ref,
    value_ref,
    first_gain_ref,
    first_shift_ref,
    gain_ref,
    shift_ref,
    cotangent_ref,
    out_ref,
    grad_ref,
    low_ref,
    sum_ref,
):
    ffn_out = bias_ref[...] + lax.dot_general(
        active_ref[...], weight_ref[...], NN, preferred_element_type=WIDE
    )
    hidden = standardise(value_ref[...])[0] * first_gain_ref[...] + first_shift_ref[...]
    normal, scale = standardise(hidden + ffn_out)
    out_ref[...] = (normal * gain_ref[...] + shift_ref[...]).astype(LOW)
    grad = cotangent_ref[...].astype(WIDE)
    total = norm_back(grad, normal, scale, gain_ref[...])
    low = total.astype(LOW)
    grad_ref[...] = total
    low_ref[...] = low
    add_sums(sum_ref, low.astype(WIDE), grad * normal, grad)


def second_norm(active, weight, bias, value, first_gain, first_shift, gain, shift, cotangent):
    tokens, units = active.shape
    model_width = weight.shape[1]
    tile = 256
    block = pl.BlockSpec((tile, model_width), lambda i: (i, 0))
    line = pl.BlockSpec((1, model_width), lambda i: (0, 0))
    return pl.pallas_call(
        second_kernel,
        grid=(tokens // tile,),
        in_specs=[
            pl.BlockSpec((tile, units), lambda i: (i, 0)),
            pl.BlockSpec((units, model_width), lambda i: (0, 0)),
            line,
            block,
            line,
            line,
            line,
            line,
            block,
        ],
        out_specs=[block, block, block, pl.BlockSpec((3, model_width), lambda i: (0, 0))],
        out_shape=[
            jax.ShapeDtypeStruct((tokens, model_width), LOW),
            jax.ShapeDtypeStruct((tokens, model_width), WIDE),
            jax.ShapeDtypeStruct((tokens, model_width), LOW),
            jax.ShapeDtypeStruct((3, model_width), WIDE),
        ],
        cost_estimate=BRIEF,
        name="second_norm",
    )(active, weight, bias, value, first_gain, first_shift, gain, shift, cotangent)


def first_back_kernel(
    inner_ref, weight_ref, second_ref, value_ref, gain_ref, grad_ref, low_ref, sum_ref
):
    grad = second_ref[...] + lax.dot_general(
        inner_ref[...], weight_ref[...], NT, preferred_element_type=WIDE
    )
    normal, scale = standardise(value_ref[...])
    total = norm_back(grad, normal, scale, gain_ref[...])
    low = total.astype(LOW)
    grad_ref[...] = total
    low_ref[...] = low
    add_sums(sum_ref, low.astype(WIDE), grad * normal, grad)


def first_back(grad_inner, weight, grad_second, value, gain):
    tokens, units = grad_inner.shape
    model_width = weight.shape[0]
    tile = 256
    wide = pl.BlockSpec((tile, model_width), lambda i: (i, 0))
    whole = lambda i: (0, 0)
    return pl.pallas_call(
        first_back_kernel,
        grid=(tokens // tile,),
        in_specs=[
            pl.BlockSpec((tile, units), lambda i: (i, 0)),
            pl.BlockSpec((model_width, units), whole),
            wide,
            wide,
            pl.BlockSpec((1, model_width), whole),
        ],
        out_specs=[wide, wide, pl.BlockSpec((3, model_width), whole)],
        out_shape=[
            jax.ShapeDtypeStruct((tokens, model_width), WIDE),
            jax.ShapeDtypeStruct((tokens, model_width), LOW),
            jax.ShapeDtypeStruct((3, model_width), WIDE),
        ],
        cost_estimate=BRIEF,
        name="first_back",
    )(grad_inner, weight, grad_second, value, gain)


class Wires:
    def __init__(self, fsdp_count):
        self.fsdp_count = fsdp_count
        self.total = 4 * fsdp_count
        self.shard = lax.axis_index("fsdp")
        rep = lax.axis_index("rep")
        self.x = rep >> 1
        self.core = rep & 1
        self.meta = jnp.stack([self.shard, self.x, self.core]).astype(jnp.int32)

    def swap(self, value, mask):
        return lax.ppermute(value, AXES, [(i, i ^ mask) for i in range(self.total)])

    def own_half(self, low, high):
        return jnp.where(self.core == 1, high, low)

    def other_half(self, low, high):
        return jnp.where(self.core == 1, low, high)

    def own_rows(self, value, axis=0):
        half = value.shape[axis] // 2
        low = lax.slice_in_dim(value, 0, half, axis=axis)
        high = lax.slice_in_dim(value, half, 2 * half, axis=axis)
        return jnp.where(self.x == 1, high, low), jnp.where(self.x == 1, low, high)

    def near(self, value):
        return [self.swap(value, 8 * k) for k in range(1, self.fsdp_count // 2)]

    def share(self, near):
        return near + [self.swap(v, 1) for v in near]


    def y_halves(self, held):
        held = held.reshape((held.shape[0] // 2, 2) + held.shape[1:])
        flag = (self.shard & 1) != 0
        return jnp.where(flag, held[:, 1], held[:, 0]), jnp.where(flag, held[:, 0], held[:, 1])

    def z_block(self, held, k):
        return lax.dynamic_index_in_dim(held, (self.shard >> 1) ^ k, 0, keepdims=False)

    def z_sends(self, held):
        if held.shape[0] > 4:
            return [held]
        return [self.z_block(held, k) for k in range(1, held.shape[0])]

    def z_swap(self, sends):
        if sends[0].ndim == 2:
            return [self.swap(v, 8 * (k + 1)) for k, v in enumerate(sends)]
        held, bit = sends[0], 2
        while bit < self.fsdp_count:
            held = held.reshape((held.shape[0] // 2, 2) + held.shape[1:])
            flag = (self.shard & bit) != 0
            got = self.swap(jnp.where(flag, held[:, 0], held[:, 1]), 4 * bit)
            held = add_low(jnp.where(flag, held[:, 1], held[:, 0]), got)
            bit *= 2
        return [held[0]]

    def z_sum(self, held, got):
        if held.shape[0] > 4:
            return got[0]
        return add_low(self.z_block(held, 0), *got)

    def by_x(self, own, other):
        return jnp.where(self.x == 1, other, own), jnp.where(self.x == 1, own, other)


def tie(*values):
    return lax.optimization_barrier(values)


def join(*parts):
    return jnp.concatenate(parts, axis=0)


def row(vector):
    return vector.reshape(1, -1).astype(WIDE)


def add_low(first, *others):
    total = first.astype(WIDE)
    for other in others:
        total = total + other.astype(WIDE)
    return total.astype(LOW)


def weight_copies(meta_ref, refs, out_ref, sem, parts, half_width):
    at = 0
    copies = []
    for width, start, by_x, offset, row in parts:
        for core, x, y in itertools.product(range(2), range(2 if by_x else 1), range(2)):
            piece = refs[at]
            at += 1
            col = (meta_ref[2] ^ core) * half_width + offset
            begin = start
            if by_x:
                col = col + (meta_ref[1] ^ x) * width
                begin = start[x]
            col = pl.multiple_of(col, LANES)
            rows = slice(row, row + piece.shape[1])
            for j in range(piece.shape[0]):
                copies.append(
                    pltpu.make_async_copy(
                        piece.at[j, :, pl.ds(begin, width)],
                        out_ref.at[meta_ref[0] ^ (2 * j + y), rows, pl.ds(col, width)],
                        sem,
                    )
                )
    return copies


def assemble_kernel(meta_ref, *refs, parts, half_width):
    copies = weight_copies(meta_ref, refs, refs[-2], refs[-1], parts, half_width)
    for copy in copies:
        copy.start()
    for copy in copies:
        copy.wait()


def project(inputs, weight_ref, query_ref, value_ref, out_ref, pairs):
    group = 3 * LANES
    step = 256
    for i, p in enumerate(pairs):
        cut = slice(i * group, (i + 1) * group)
        weight = weight_ref[..., cut].reshape(inputs.shape[1], group)
        bias = jnp.concatenate(
            [query_ref[p : p + 1], jnp.zeros((1, LANES), WIDE), value_ref[p : p + 1]], axis=1
        )
        for t in range(0, inputs.shape[0], step):
            out = lax.dot_general(inputs[t : t + step], weight, NN, preferred_element_type=WIDE)
            out_ref[t : t + step, cut] = (out + bias).astype(LOW)


def project_kernel(meta_ref, inputs_ref, query_ref, value_ref, *refs, parts, half_width, pairs):
    full_ref, out_ref, sem = refs[-3:]
    copies = weight_copies(meta_ref, refs, full_ref, sem, parts, half_width)
    for copy in copies:
        copy.start()
    for copy in copies:
        copy.wait()
    project(inputs_ref, full_ref, query_ref, value_ref, out_ref, pairs)


def project_whole_kernel(inputs_ref, query_ref, value_ref, full_ref, *refs, pairs):
    project(inputs_ref, full_ref, query_ref, value_ref, refs[-1], pairs)


def joint_project(wires, inputs, pieces, query_bias, value_bias, chunk, shard_rows, behind=()):
    tokens, model_width = inputs.shape
    half_width = chunk.count * 3 * LANES
    out_shape = jax.ShapeDtypeStruct((tokens, 2 * half_width), LOW)
    on_chip = pl.BlockSpec(memory_space=pltpu.VMEM)
    anywhere = pl.BlockSpec(memory_space=pl.ANY)
    cost = BRIEF
    if not isinstance(pieces, list):
        out = pl.pallas_call(
            functools.partial(project_whole_kernel, pairs=chunk.pairs),
            out_shape=out_shape,
            in_specs=[on_chip] * 4 + [anywhere] * len(behind),
            out_specs=on_chip,
            cost_estimate=cost,
            name="joint_project",
        )(inputs, query_bias, value_bias, pieces, *behind)
        return pieces, out
    full, out = pl.pallas_call(
        functools.partial(
            project_kernel,
            parts=[(half_width, 0, False, 0, 0)],
            half_width=half_width,
            pairs=chunk.pairs,
        ),
        out_shape=[
            jax.ShapeDtypeStruct((wires.fsdp_count, shard_rows, 2 * half_width), LOW),
            out_shape,
        ],
        in_specs=[pl.BlockSpec(memory_space=pltpu.SMEM)]
        + [on_chip] * 3
        + [anywhere] * (len(pieces) + len(behind)),
        out_specs=[on_chip] * 2,
        scratch_shapes=[pltpu.SemaphoreType.DMA],
        cost_estimate=cost,
        name="joint_project",
    )(wires.meta, inputs, query_bias, value_bias, *pieces, *behind)
    return full.reshape(model_width, 2 * half_width), out


def pack_kernel(*refs, chunks, wide):
    *vector_refs, out_ref = refs
    sum_refs, vector_refs = vector_refs[: len(chunks)], vector_refs[len(chunks) :]
    out_ref[...] = jnp.zeros_like(out_ref)
    for ref, chunk in zip(sum_refs, chunks):
        for i, p in enumerate(chunk.pairs):
            total = ref[0, i, 0:1]
            for r in range(1, ref.shape[0]):
                total = total + ref[r, i, 0:1]
            out_ref[0:1, p * LANES : (p + 1) * LANES] = total[:, :LANES]
            out_ref[1:2, p * LANES : (p + 1) * LANES] = total[:, 2 * LANES :]
    row = 2
    for ref in vector_refs:
        for r, start in itertools.product(range(ref.shape[0]), range(0, ref.shape[1], wide)):
            out_ref[row : row + 1] = ref[r : r + 1, start : start + wide]
            row += 1


def pack(sums, chunks, vectors, wide):
    rows = 2 + sum(v.shape[0] * v.shape[1] // wide for v in vectors)
    return pl.pallas_call(
        functools.partial(pack_kernel, chunks=chunks, wide=wide),
        out_shape=jax.ShapeDtypeStruct(((rows + 7) // 8 * 8, wide), WIDE),
        name="pack",
    )(*sums, *vectors)


def assemble(wires, shard_rows, half_width, parts):
    count = wires.fsdp_count
    operands, plan = [], []
    for pieces, *where in parts:
        plan.append(where)
        operands += pieces
    shape = (count, shard_rows, 2 * half_width)
    full = pl.pallas_call(
        functools.partial(assemble_kernel, parts=plan, half_width=half_width),
        out_shape=jax.ShapeDtypeStruct(shape, LOW),
        in_specs=[pl.BlockSpec(memory_space=pltpu.SMEM)]
        + [pl.BlockSpec(memory_space=pl.ANY)] * len(operands),
        out_specs=pl.BlockSpec(memory_space=pltpu.VMEM),
        scratch_shapes=[pltpu.SemaphoreType.DMA],
        cost_estimate=BRIEF,
        name="assemble",
    )(wires.meta, *operands)
    return full.reshape(count * shard_rows, 2 * half_width)


def pair_columns(array, pairs, model_width):
    return jnp.concatenate(
        [
            array[..., part * model_width + p * LANES : part * model_width + (p + 1) * LANES]
            for p in pairs
            for part in range(3)
        ],
        axis=-1,
    )


def natural_columns(pieces, chunks):
    where = {}
    for piece, chunk in zip(pieces, chunks):
        for i, p in enumerate(chunk.pairs):
            for part in range(3):
                place = (3 * i + part) * LANES
                where[(part, p)] = piece[..., place : place + LANES]
    return jnp.concatenate([where[key] for key in sorted(where)], axis=-1)


def body(
    fsdp_count,
    layer_input,
    segment_ids,
    joint_weight,
    query_bias,
    value_bias,
    close_weight,
    close_bias,
    first_gain,
    first_shift,
    expand_weight,
    expand_bias,
    shrink_weight,
    shrink_bias,
    second_gain,
    second_shift,
    cotangent,
):
    row_count, pos_count, model_width = layer_input.shape
    hidden_units = expand_bias.shape[0]
    tok_count = row_count * pos_count
    flat_input = layer_input.reshape(tok_count, model_width)
    wires = Wires(fsdp_count)
    half_pairs = model_width // LANES // 2
    chunks = (Chunk(0, 1, half_pairs), Chunk(1, half_pairs - 1, half_pairs))
    shard_rows = joint_weight.shape[0]

    joint_pieces = []
    for chunk in chunks:
        low, high = (
            pair_columns(joint_weight, chunk.pairs[c * chunk.count : (c + 1) * chunk.count], model_width)
            for c in range(2)
        )
        joint_pieces.append(wires.own_half(low, high))
    half_model, half_hidden = model_width // 2, hidden_units // 2
    unit = half_hidden // 3
    expand_half = wires.own_half(expand_weight[:, :half_hidden], expand_weight[:, half_hidden:])
    close_half = wires.own_half(close_weight[:, :half_model], close_weight[:, half_model:])
    shrink_half = wires.own_half(shrink_weight[:, :half_model], shrink_weight[:, half_model:])
    shrink_rows = shrink_half.shape[0] // 2
    aligned = fsdp_count == 8 and shard_rows % 32 == 0
    query_rows = query_bias.astype(WIDE).reshape(-1, LANES)
    value_rows = value_bias.astype(WIDE).reshape(-1, LANES)

    inputs_t = jnp.swapaxes(layer_input, 1, 2)
    lines = [
        row(v)
        for v in (
            close_bias,
            first_gain,
            first_shift,
            expand_bias,
            shrink_bias,
            second_gain,
            second_shift,
        )
    ]
    segments = segment_ids[:, :, None], segment_ids[:, None, :]

    def project_and_attend(place, shared, context):
        full, part = joint_project(
            wires, flat_input, shared, query_rows, value_rows, chunks[place], shard_rows
        )
        return full, part.reshape(row_count, pos_count, -1)

    if aligned:
        first, second = joint_pieces[0][None], joint_pieces[1][None]
        split = wires.by_x(expand_half[:, unit : 2 * unit], expand_half[:, 2 * unit :])[0]
        piece = jnp.concatenate([expand_half[:, :unit], close_half, split], axis=1)[None]
        shrink = shrink_half[None]
        first_near = wires.near(first)
        first = join(first, *first_near)
        first, second, inputs_t, *segments = tie(first, second, inputs_t, *segments)
        first_y = wires.swap(first, 4)
        second_near = wires.near(second)
        first, first_y, second_near[0], second_near[1], *lines = tie(
            first, first_y, second_near[0], second_near[1], *lines
        )
        first_shared = wires.share([first, first_y])
        *first_shared, piece, second, second_near[0], second_near[1], second_near[2] = tie(
            *first_shared, piece, second, *second_near
        )
        second = join(second, *second_near)
        second_y = wires.swap(second, 4)
        piece_near = wires.near(piece)
        full, part = project_and_attend(0, first_shared, None)
        joint_full, mixed = [full], [part]
        context, w, inv = attend(mixed[0], segments, chunks[0])
        weights, inverse = [w], [inv]
        context, second, second_y, piece_near[0], piece_near[1] = tie(
            context, second, second_y, piece_near[0], piece_near[1]
        )
        *second_shared, piece, shrink, piece_near[0], piece_near[1], piece_near[2] = tie(
            *wires.share([second, second_y]), piece, shrink, *piece_near
        )
        piece = join(piece, *piece_near)
        split = piece[..., unit + half_model :]
        piece, split = tie(piece, split)
        piece_y = wires.swap(piece, 4)
        split_x = wires.swap(split, 2)
        shrink_near = wires.near(shrink)
        full, part = project_and_attend(1, second_shared, context)
        joint_full.append(full)
        part, split, split_x = tie(part, split, split_x)
        mixed.append(part)
        context, w, inv = attend(mixed[1], segments, chunks[1], context)
        weights.append(w)
        inverse.append(inv)
        context, piece, piece_y, shrink, *shrink_near = tie(
            context, piece, piece_y, shrink, *shrink_near
        )
        plain_shared = wires.share([piece, piece_y])
        split_yx = wires.swap(piece_y[..., unit + half_model :], 2)
        shrink = join(shrink, *shrink_near)
        *plain_shared, shrink = tie(*plain_shared, shrink)
        shrink_y = wires.swap(shrink, 4)
        close_full = assemble(
            wires, shard_rows, half_model, [(plain_shared, half_model, unit, False, 0, 0)]
        )
    else:
        joint_full, mixed, weights, inverse = [], [], [], []
        context = None
        for place, chunk in enumerate(chunks):
            shared = lax.all_gather(
                pair_columns(joint_weight, chunk.pairs, model_width), "fsdp", axis=0, tiled=True
            )
            full, part = project_and_attend(place, shared, context)
            joint_full.append(full)
            mixed.append(part)
            context, w, inv = attend(part, segments, chunk, context)
            weights.append(w)
            inverse.append(inv)
        close_full, expand_full, shrink_full = (
            lax.all_gather(w, "fsdp", axis=0, tiled=True)
            for w in (close_weight, expand_weight, shrink_weight)
        )
    context_low = context.reshape(tok_count, model_width)

    first_sum, hidden_low = first_norm(
        context_low, close_full, lines[0], flat_input, lines[1], lines[2]
    )
    if aligned:
        own, other = plain_shared[:2], plain_shared[2:]
        hidden_low, split_x, split_yx = tie(hidden_low, split_x, split_yx)
        split_shared = wires.share([split_x, split_yx])
        expand_full = assemble(
            wires,
            shard_rows,
            half_hidden,
            [
                (plain_shared, unit, 0, False, 0, 0),
                (
                    [*own, *split_shared[:2], *other, *split_shared[2:]],
                    unit,
                    [unit + half_model, 0],
                    True,
                    unit,
                    0,
                ),
            ],
        )
    active_low, slope = expand_gelu(hidden_low, expand_full, lines[3])
    if aligned:
        active_low, shrink, shrink_y = tie(active_low, shrink, shrink_y)
        shrink_full = assemble(
            wires,
            shrink_weight.shape[0],
            half_model,
            [(wires.share([shrink, shrink_y]), half_model, 0, False, 0, 0)],
        )
    layer_output, grad_second, grad_ffn, second_sums = second_norm(
        active_low,
        shrink_full,
        lines[4],
        first_sum,
        lines[1],
        lines[2],
        lines[5],
        lines[6],
        cotangent.reshape(tok_count, model_width),
    )
    layer_output = layer_output.reshape(row_count, pos_count, model_width)

    def outgoing(left, right):
        half = right.shape[1] // 2
        send = wires.other_half(right[:, :half], right[:, half:])
        return jnp.einsum("tf,td->fd", left, send, preferred_element_type=WIDE).astype(LOW)

    def kept(left, right):
        half = right.shape[1] // 2
        keep = wires.own_half(right[:, :half], right[:, half:])
        return jnp.einsum("tf,td->fd", left, keep, preferred_element_type=WIDE)

    def by_shard(held):
        return held.reshape(fsdp_count, held.shape[0] // fsdp_count, held.shape[1])

    def staying(left, right, got):
        return by_shard(add_low(kept(left, right), got))

    def both_halves(mine):
        other = wires.swap(mine, 1)
        return wires.own_half(mine, other), wires.own_half(other, mine)

    shrink_send = outgoing(active_low, grad_ffn)
    active_low, shrink_send = tie(active_low, shrink_send)
    shrink_got = wires.swap(shrink_send, 1)
    shrink_keep = kept(active_low, grad_ffn)
    grad_ffn, shrink_keep, shrink_got = tie(grad_ffn, shrink_keep, shrink_got)
    shrink_held = by_shard(add_low(shrink_keep, shrink_got))
    top_keep, top_send = wires.y_halves(shrink_held[:, :shrink_rows])
    low_keep, low_send = wires.own_rows(shrink_held[:, shrink_rows:], axis=1)
    grad_ffn, top_keep, top_send, low_keep, low_send = tie(
        grad_ffn, top_keep, top_send, low_keep, low_send
    )
    top_got = wires.swap(top_send, 4)
    low_got = wires.swap(low_send, 2)
    grad_inner, inner_sum = inner_grad(grad_ffn, shrink_full, slope)
    grad_inner, top_keep, top_got, low_keep, low_got = tie(
        grad_inner, top_keep, top_got, low_keep, low_got
    )
    low_keep, low_send = wires.y_halves(add_low(low_keep, low_got))
    top_held = add_low(top_keep, top_got)
    hidden_low, low_keep, low_send = tie(hidden_low, low_keep, low_send)
    low_got = wires.swap(low_send, 4)
    expand_send = outgoing(hidden_low, grad_inner)
    hidden_low, expand_send = tie(hidden_low, expand_send)
    expand_got = wires.swap(expand_send, 1)
    expand_keep = kept(hidden_low, grad_inner)
    grad_inner, expand_keep, expand_got = tie(grad_inner, expand_keep, expand_got)
    expand_held = by_shard(add_low(expand_keep, expand_got))
    quarter = half_hidden // 2
    left_keep, left_send = wires.y_halves(expand_held[..., :quarter])
    right_keep, right_send = wires.by_x(
        expand_held[..., quarter : quarter + quarter // 2],
        expand_held[..., quarter + quarter // 2 :],
    )
    (
        grad_inner,
        left_keep,
        left_send,
        right_keep,
        right_send,
        low_keep,
        low_got,
        top_held,
        *top_sends,
    ) = tie(
        grad_inner,
        left_keep,
        left_send,
        right_keep,
        right_send,
        low_keep,
        low_got,
        top_held,
        *wires.z_sends(top_held),
    )
    top_got = wires.z_swap(top_sends)
    left_got = wires.swap(left_send, 4)
    right_got = wires.swap(right_send, 2)
    grad_first, grad_branch, first_sums = first_back(
        grad_inner, expand_full, grad_second, first_sum, lines[1]
    )
    grad_branch, left_keep, left_got, right_keep, right_got, top_held, *top_got = tie(
        grad_branch, left_keep, left_got, right_keep, right_got, top_held, *top_got
    )
    right_held = add_low(right_keep, right_got)
    top_mine = wires.z_sum(top_held, top_got)
    mid_held = jnp.concatenate([add_low(left_keep, left_got), add_low(low_keep, low_got)], axis=2)
    context_low, grad_branch = tie(context_low, grad_branch)
    close_send = outgoing(context_low, grad_branch)
    grad_branch, close_send = tie(grad_branch, close_send)
    close_got = wires.swap(close_send, 1)
    grad_context = jnp.einsum(
        "te,de->td", grad_branch, close_full, preferred_element_type=WIDE
    ).astype(LOW)
    context_low, grad_context, close_got = tie(context_low, grad_context, close_got)
    close_held = staying(context_low, grad_branch, close_got)
    grad_context = grad_context.reshape(row_count, pos_count, model_width)
    close_keep, close_send = wires.y_halves(jnp.concatenate([right_held, close_held], axis=2))
    (
        grad_context,
        close_keep,
        close_send,
        top_mine,
        mid_held,
        *mid_sends,
    ) = tie(
        grad_context,
        close_keep,
        close_send,
        top_mine,
        mid_held,
        *wires.z_sends(mid_held),
    )
    top_other = wires.swap(top_mine, 2)
    close_got = wires.swap(close_send, 4)
    mid_got = wires.z_swap(mid_sends)

    grad_mixed, bias_sums, joint_parts = {}, {}, {}
    grad_mixed[1], bias_sums[1], joint_parts[1] = attend_back(
        mixed[1], weights[1], context, inverse[1], grad_context, inputs_t, chunks[1]
    )
    grad_mixed[1] = grad_mixed[1].reshape(tok_count, -1)
    large, close_keep, close_got, top_mine, top_other, mid_held, *mid_got = tie(
        joint_parts[1], close_keep, close_got, top_mine, top_other, mid_held, *mid_got
    )
    large_got = wires.swap(wires.other_half(large[0], large[1]), 1)
    second_held = add_low(close_keep, close_got)
    large, large_got, second_held, *second_sends = tie(
        large, large_got, second_held, *wires.z_sends(second_held)
    )
    second_got = wires.z_swap(second_sends)
    large_keep, large_send = wires.own_rows(
        by_shard(add_low(wires.own_half(large[0], large[1]), large_got)), axis=1
    )
    grad_context, large_keep, large_send = tie(grad_context, large_keep, large_send)
    large_got = wires.swap(large_send, 2)
    grad_mixed[0], bias_sums[0], joint_parts[0] = attend_back(
        mixed[0], weights[0], context, inverse[0], grad_context, inputs_t, chunks[0]
    )
    grad_mixed[0] = grad_mixed[0].reshape(tok_count, -1)
    small, large_keep, large_got, second_held, *second_got = tie(
        joint_parts[0], large_keep, large_got, second_held, *second_got
    )
    small_got = wires.swap(wires.other_half(small[0], small[1]), 1)

    packed = pack(
        [bias_sums[0], bias_sums[1]],
        chunks,
        [
            first_sums,
            second_sums,
            inner_sum,
        ],
        model_width,
    )

    large_keep, large_send = wires.y_halves(add_low(large_keep, large_got))
    small, small_got, packed, large_keep, large_send = tie(
        small, small_got, packed, large_keep, large_send
    )
    large_got = wires.swap(large_send, 4)
    vector_got = wires.swap(packed, 1)
    small_keep, small_send = wires.y_halves(
        by_shard(add_low(wires.own_half(small[0], small[1]), small_got))
    )
    small_keep, small_send, packed, vector_got = tie(small_keep, small_send, packed, vector_got)
    small_got = wires.swap(small_send, 4)
    packed = packed + vector_got
    mine = jnp.concatenate(
        [wires.z_sum(mid_held, mid_got), wires.z_sum(second_held, second_got)], axis=1
    )
    grad_mixed[0], grad_mixed[1], packed, mine = tie(grad_mixed[0], grad_mixed[1], packed, mine)
    other = wires.swap(mine, 2)
    vector_got = wires.swap(packed, 2)
    input_grad = grad_first + jnp.einsum(
        "te,de->td", grad_mixed[0], joint_full[0], preferred_element_type=WIDE
    )
    input_grad, packed, vector_got = tie(input_grad, packed, vector_got)
    packed = packed + vector_got
    vector_got = wires.swap(packed, 4)
    input_grad = input_grad + jnp.einsum(
        "te,de->td", grad_mixed[1], joint_full[1], preferred_element_type=WIDE
    )
    input_grad, small_keep, small_got, large_keep, large_got, packed, vector_got, mine, other = tie(
        input_grad, small_keep, small_got, large_keep, large_got, packed, vector_got, mine, other
    )
    small_held = add_low(small_keep, small_got)
    half_rows = small_held.shape[1] // 2
    joint_held = jnp.concatenate(
        [small_held[:, :half_rows], small_held[:, half_rows:], add_low(large_keep, large_got)],
        axis=2,
    )
    packed = packed + vector_got
    packed, joint_held, *joint_sends = tie(packed, joint_held, *wires.z_sends(joint_held))
    joint_got = wires.z_swap(joint_sends)
    vector_got = wires.swap(packed, 8)
    joint_held, packed, vector_got, *joint_got = tie(
        joint_held, packed, vector_got, *joint_got
    )
    joint_mine, packed = tie(wires.z_sum(joint_held, joint_got), packed + vector_got)

    top_mine = add_low(top_mine, top_other)
    total = add_low(mine, other)
    cuts = [quarter, quarter + half_model, quarter + half_model + quarter // 2]
    left, _, _, close = jnp.split(total, cuts, axis=1)
    (_, low, right, _), (_, low_other, right_other, _) = (
        jnp.split(v, cuts, axis=1) for v in (mine, other)
    )
    shrink_mine = jnp.concatenate([top_mine, *wires.by_x(low, low_other)], axis=0)
    second_mine = jnp.concatenate([left, *wires.by_x(right, right_other), close], axis=1)
    joint_other = wires.swap(joint_mine, 2)
    vector_got = wires.swap(packed, 16)
    joint_mine, joint_other, packed, vector_got = tie(
        joint_mine, joint_other, packed, vector_got
    )
    small_width = small_held.shape[2]
    small_mine = add_low(joint_mine[:, : 2 * small_width], joint_other[:, : 2 * small_width])
    joint_mine = jnp.concatenate(
        [
            jnp.concatenate([small_mine[:, :small_width], small_mine[:, small_width:]], axis=0),
            jnp.concatenate(
                wires.by_x(joint_mine[:, 2 * small_width :], joint_other[:, 2 * small_width :]),
                axis=0,
            ),
        ],
        axis=1,
    )

    shrink_grad = jnp.concatenate(both_halves(shrink_mine), axis=1).astype(WIDE)
    low, high = both_halves(second_mine)
    cut = hidden_units // 2
    expand_grad = jnp.concatenate([low[:, :cut], high[:, :cut]], axis=1).astype(WIDE)
    close_grad = jnp.concatenate([low[:, cut:], high[:, cut:]], axis=1).astype(WIDE)
    joint_mine, summed = tie(joint_mine, packed + vector_got)
    low, high = both_halves(joint_mine)
    mask = 32
    while mask < wires.total:
        summed = summed + wires.swap(summed, mask)
        mask *= 2
    cut = chunks[0].count * 3 * LANES
    joint_grad = natural_columns(
        [
            jnp.concatenate([low[:, :cut], high[:, :cut]], axis=1),
            jnp.concatenate([low[:, cut:], high[:, cut:]], axis=1),
        ],
        chunks,
    ).astype(WIDE)
    (
        query_bias_grad,
        value_bias_grad,
        close_bias_grad,
        first_gain_grad,
        first_shift_grad,
        shrink_bias_grad,
        second_gain_grad,
        second_shift_grad,
    ) = (summed[i] for i in range(8))
    expand_bias_grad = summed[8 : 8 + hidden_units // model_width].reshape(hidden_units)
    return (
        layer_output,
        input_grad.reshape(row_count, pos_count, model_width),
        joint_grad,
        query_bias_grad,
        value_bias_grad,
        close_grad,
        close_bias_grad,
        first_gain_grad,
        first_shift_grad,
        expand_grad,
        expand_bias_grad,
        shrink_grad,
        shrink_bias_grad,
        second_gain_grad,
        second_shift_grad,
    )


def solution(mesh):
    rows = P(("fsdp", "rep"), None, None)
    sharded = P("fsdp", None)
    copied = P()
    return jax.shard_map(
        functools.partial(body, mesh.shape["fsdp"]),
        mesh=mesh,
        in_specs=(
            rows,
            P(("fsdp", "rep"), None),
            sharded,
            copied,
            copied,
            sharded,
            copied,
            copied,
            copied,
            sharded,
            copied,
            sharded,
            copied,
            copied,
            copied,
            rows,
        ),
        out_specs=(
            rows,
            rows,
            sharded,
            copied,
            copied,
            sharded,
            copied,
            copied,
            copied,
            sharded,
            copied,
            sharded,
            copied,
            copied,
            copied,
        ),
        check_vma=False,
    )
```

```python
import functools
import itertools
import math

import jax
import jax.numpy as jnp
from jax import lax
from jax.experimental import pallas as pl
from jax.experimental.pallas import tpu as pltpu
from jax.sharding import PartitionSpec as P

HEADS = 12
EPS = 1e-12
AXES = ("fsdp", "rep")
LANES = 128
NT = (((1,), (1,)), ((), ()))
NN = (((1,), (0,)), ((), ()))
LOW = jnp.bfloat16
WIDE = jnp.float32
BRIEF = pl.CostEstimate(flops=0, bytes_accessed=0, transcendentals=0)


def attend_kernel(mixed_ref, seg_col_ref, seg_row_ref, *refs):
    context_ref, weights_ref, inverse_ref = refs[-3:]
    pos = mixed_ref.shape[0]
    head = mixed_ref.shape[1] // 6
    same = seg_col_ref[...] == seg_row_ref[...]
    values_t = mixed_ref[:, 4 * head : 6 * head].T
    ones = jnp.ones((16, pos), LOW)
    outs, inverses = [], []
    for h in range(2):
        queries = mixed_ref[:, h * head : (h + 1) * head] * LOW(1.0 / math.sqrt(head))
        keys = mixed_ref[:, (2 + h) * head : (3 + h) * head]
        scores = lax.dot_general(keys, queries, NT, preferred_element_type=WIDE)
        scores = jnp.where(same, scores, -jnp.inf)
        raised = jnp.exp(scores - jnp.max(scores, axis=0, keepdims=True)).astype(LOW)
        weights_ref[h] = raised
        extended = jnp.concatenate([values_t[h * head : (h + 1) * head], ones], axis=0)
        out = lax.dot_general(extended, raised, NN, preferred_element_type=WIDE)
        inverse = 1.0 / out[head : head + 1]
        outs.append(out[:head] * inverse)
        inverses.append(jnp.broadcast_to(inverse, (head, pos)))
    context_ref[...] = jnp.concatenate(outs, axis=0).T.astype(LOW)
    inverse_ref[...] = jnp.concatenate(inverses, axis=0).T


def attend_back_kernel(
    mixed_ref,
    weights_ref,
    context_ref,
    inverse_ref,
    grad_ref,
    inputs_ref,
    out_ref,
    sum_ref,
    joint_ref,
    total_ref,
):
    row = pl.program_id(1)
    head = mixed_ref.shape[1] // 6
    scale = LOW(1.0 / math.sqrt(head))
    grad = grad_ref[...].astype(WIDE) * inverse_ref[...]
    product = (grad * context_ref[...].astype(WIDE)).astype(LOW)
    grad_low = grad.astype(LOW)
    queries = mixed_ref[:, : 2 * head] * scale
    keys_t = (mixed_ref[:, 2 * head : 4 * head] * scale).T
    ones = jnp.ones((8, head), LOW)
    grad_q, grad_k, grad_v = [], [], []
    for h in range(2):
        cut = slice(h * head, (h + 1) * head)
        values = mixed_ref[:, (4 + h) * head : (5 + h) * head]
        inner = lax.dot_general(ones, product[:, cut], NT, preferred_element_type=WIDE)[0:1]
        raised = weights_ref[h]
        grad_attn = lax.dot_general(values, grad_low[:, cut], NT, preferred_element_type=WIDE)
        grad_scores = raised * (grad_attn - inner).astype(LOW)
        grad_k.append(lax.dot_general(grad_scores, queries[:, cut], NN, preferred_element_type=WIDE))
        grad_v.append(lax.dot_general(raised, grad_low[:, cut], NN, preferred_element_type=WIDE))
        grad_q.append(lax.dot_general(keys_t[cut], grad_scores, NN, preferred_element_type=WIDE))
    out = jnp.concatenate([jnp.concatenate(grad_q, axis=0).T] + grad_k + grad_v, axis=1).astype(LOW)
    out_ref[...] = out
    sum_ref[...] = jnp.broadcast_to(
        jnp.sum(out.astype(WIDE), axis=0, keepdims=True), sum_ref.shape
    )
    part = lax.dot_general(inputs_ref[row], out, NN, preferred_element_type=WIDE)

    @pl.when(row == 0)
    def _():
        total_ref[...] = part

    @pl.when(row > 0)
    def _():
        total_ref[...] += part

    @pl.when(row == pl.num_programs(1) - 1)
    def _():
        joint_ref[...] = total_ref[...].astype(LOW)


class Chunk:
    def __init__(self, first, count, half):
        self.first, self.count, self.half = first, count, half
        self.pairs = [c * half + first + i for c in range(2) for i in range(count)]

    def block(self, place):
        return (place // self.count) * self.half + self.first + place % self.count


def attend(mixed, segments, chunk, context=None, behind=()):
    rows, pos, width = mixed.shape
    group = width // len(chunk.pairs)
    pair = group // 3
    count = len(chunk.pairs)
    total = 2 * chunk.half
    in_specs = [
        pl.BlockSpec((None, pos, group), lambda r, p: (r, 0, p)),
        pl.BlockSpec((None, pos, 1), lambda r, p: (r, 0, 0)),
        pl.BlockSpec((None, 1, pos), lambda r, p: (r, 0, 0)),
    ]
    operands = [mixed, *segments]
    aliases = {}
    if context is not None:
        in_specs.append(pl.BlockSpec(memory_space=pl.ANY))
        operands.append(context)
        aliases = {3: 0}
    in_specs += [pl.BlockSpec(memory_space=pl.ANY)] * len(behind)
    operands += behind
    return pl.pallas_call(
        attend_kernel,
        grid=(rows, count),
        in_specs=in_specs,
        out_specs=[
            pl.BlockSpec((None, pos, pair), lambda r, p: (r, 0, chunk.block(p))),
            pl.BlockSpec((None, None, 2, pos, pos), lambda r, p: (r, p, 0, 0, 0)),
            pl.BlockSpec((None, pos, pair), lambda r, p: (r, 0, p)),
        ],
        out_shape=[
            jax.ShapeDtypeStruct((rows, pos, total * pair), LOW),
            jax.ShapeDtypeStruct((rows, count, 2, pos, pos), LOW),
            jax.ShapeDtypeStruct((rows, pos, count * pair), WIDE),
        ],
        input_output_aliases=aliases,
        cost_estimate=BRIEF,
        name="attend",
    )(*operands)


def attend_back(mixed, weights, context, inverse, grad, inputs, chunk):
    rows, pos, width = mixed.shape
    model_width = inputs.shape[1]
    count = len(chunk.pairs)
    group = width // count
    pair = group // 3
    natural = pl.BlockSpec((None, pos, pair), lambda p, r: (r, 0, chunk.block(p)))
    return pl.pallas_call(
        attend_back_kernel,
        grid=(count, rows),
        in_specs=[
            pl.BlockSpec((None, pos, group), lambda p, r: (r, 0, p)),
            pl.BlockSpec((None, None, 2, pos, pos), lambda p, r: (r, p, 0, 0, 0)),
            natural,
            pl.BlockSpec((None, pos, pair), lambda p, r: (r, 0, p)),
            natural,
            pl.BlockSpec((rows, model_width, pos), lambda p, r: (0, 0, 0)),
        ],
        out_specs=[
            pl.BlockSpec((None, pos, group), lambda p, r: (r, 0, p)),
            pl.BlockSpec((None, None, 8, group), lambda p, r: (r, p, 0, 0)),
            pl.BlockSpec(
                (None, model_width, group),
                lambda p, r: (p // chunk.count, 0, p % chunk.count),
            ),
        ],
        out_shape=[
            jax.ShapeDtypeStruct((rows, pos, count * group), LOW),
            jax.ShapeDtypeStruct((rows, count, 8, group), WIDE),
            jax.ShapeDtypeStruct((2, model_width, chunk.count * group), LOW),
        ],
        scratch_shapes=[pltpu.VMEM((model_width, group), WIDE)],
        cost_estimate=BRIEF,
        name="attend_back",
    )(mixed, weights, context, inverse, grad, inputs)


def expand_kernel(hidden_ref, weight_ref, bias_ref, active_ref, slope_ref, *, chunks):
    step = hidden_ref.shape[0] // chunks
    for i in range(chunks):
        cut = slice(i * step, (i + 1) * step)
        inner = lax.dot_general(hidden_ref[cut], weight_ref[...], NN, preferred_element_type=WIDE)
        inner = inner + bias_ref[...]
        share = 0.5 + 0.5 * lax.erf(inner * math.sqrt(0.5))
        active_ref[cut] = (inner * share).astype(LOW)
        density = jnp.exp(-0.5 * inner * inner) * (1.0 / math.sqrt(2.0 * math.pi))
        slope_ref[cut] = (share + inner * density).astype(LOW)


def expand_gelu(hidden, weight, bias):
    tokens, model_width = hidden.shape
    units = weight.shape[1]
    tile = 768
    return pl.pallas_call(
        functools.partial(expand_kernel, chunks=8),
        grid=(units // tile,),
        in_specs=[
            pl.BlockSpec((tokens, model_width), lambda j: (0, 0)),
            pl.BlockSpec((model_width, tile), lambda j: (0, j)),
            pl.BlockSpec((1, tile), lambda j: (0, j)),
        ],
        out_specs=[pl.BlockSpec((tokens, tile), lambda j: (0, j))] * 2,
        out_shape=[jax.ShapeDtypeStruct((tokens, units), LOW)] * 2,
        cost_estimate=BRIEF,
        name="expand_gelu",
    )(hidden, weight, bias)


def inner_grad_kernel(grad_ref, weight_ref, slope_ref, out_ref, sum_ref, *, chunks):
    step = grad_ref.shape[0] // chunks
    total = jnp.zeros((1, weight_ref.shape[0]), WIDE)
    for i in range(chunks):
        cut = slice(i * step, (i + 1) * step)
        grad = lax.dot_general(grad_ref[cut], weight_ref[...], NT, preferred_element_type=WIDE)
        grad = (grad * slope_ref[cut].astype(WIDE)).astype(LOW)
        out_ref[cut] = grad
        total = total + jnp.sum(grad.astype(WIDE), axis=0, keepdims=True)
    sum_ref[...] = total


def inner_grad(grad, weight, slope):
    tokens, model_width = grad.shape
    units = weight.shape[0]
    tile = 768
    return pl.pallas_call(
        functools.partial(inner_grad_kernel, chunks=2),
        grid=(units // tile,),
        in_specs=[
            pl.BlockSpec((tokens, model_width), lambda j: (0, 0)),
            pl.BlockSpec((tile, model_width), lambda j: (j, 0)),
            pl.BlockSpec((tokens, tile), lambda j: (0, j)),
        ],
        out_specs=[
            pl.BlockSpec((tokens, tile), lambda j: (0, j)),
            pl.BlockSpec((1, tile), lambda j: (0, j)),
        ],
        out_shape=[
            jax.ShapeDtypeStruct((tokens, units), LOW),
            jax.ShapeDtypeStruct((1, units), WIDE),
        ],
        cost_estimate=BRIEF,
        name="inner_grad",
    )(grad, weight, slope)


def standardise(value):
    centred = value - jnp.mean(value, axis=-1, keepdims=True)
    scale = lax.rsqrt(jnp.mean(centred * centred, axis=-1, keepdims=True) + EPS)
    return centred * scale, scale


def norm_back(grad, normal, scale, gain):
    grad_normal = grad * gain
    return scale * (
        grad_normal
        - jnp.mean(grad_normal, axis=-1, keepdims=True)
        - normal * jnp.mean(grad_normal * normal, axis=-1, keepdims=True)
    )


def add_sums(sum_ref, *values):
    sums = jnp.concatenate([jnp.sum(v, axis=0, keepdims=True) for v in values], axis=0)
    first = pl.program_id(0) == 0

    @pl.when(first)
    def _():
        sum_ref[...] = sums

    @pl.when(jnp.logical_not(first))
    def _():
        sum_ref[...] += sums


def first_kernel(
    context_ref, weight_ref, bias_ref, inputs_ref, gain_ref, shift_ref, sum_ref, low_ref
):
    branch = lax.dot_general(
        context_ref[...], weight_ref[...], NN, preferred_element_type=WIDE
    )
    total = inputs_ref[...].astype(WIDE) + (branch + bias_ref[...])
    sum_ref[...] = total
    low_ref[...] = (standardise(total)[0] * gain_ref[...] + shift_ref[...]).astype(LOW)


def first_norm(context, weight, bias, inputs, gain, shift):
    tokens, model_width = context.shape
    tile = 512
    block = pl.BlockSpec((tile, model_width), lambda i: (i, 0))
    line = pl.BlockSpec((1, model_width), lambda i: (0, 0))
    return pl.pallas_call(
        first_kernel,
        grid=(tokens // tile,),
        in_specs=[
            block,
            pl.BlockSpec((model_width, model_width), lambda i: (0, 0)),
            line,
            block,
            line,
            line,
        ],
        out_specs=[block, block],
        out_shape=[
            jax.ShapeDtypeStruct((tokens, model_width), WIDE),
            jax.ShapeDtypeStruct((tokens, model_width), LOW),
        ],
        cost_estimate=BRIEF,
        name="first_norm",
    )(context, weight, bias, inputs, gain, shift)


def second_kernel(
    active_ref,
    weight_ref,
    bias_ref,
    value_ref,
    first_gain_ref,
    first_shift_ref,
    gain_ref,
    shift_ref,
    cotangent_ref,
    out_ref,
    grad_ref,
    low_ref,
    sum_ref,
):
    ffn_out = bias_ref[...] + lax.dot_general(
        active_ref[...], weight_ref[...], NN, preferred_element_type=WIDE
    )
    hidden = standardise(value_ref[...])[0] * first_gain_ref[...] + first_shift_ref[...]
    normal, scale = standardise(hidden + ffn_out)
    out_ref[...] = (normal * gain_ref[...] + shift_ref[...]).astype(LOW)
    grad = cotangent_ref[...].astype(WIDE)
    total = norm_back(grad, normal, scale, gain_ref[...])
    low = total.astype(LOW)
    grad_ref[...] = total
    low_ref[...] = low
    add_sums(sum_ref, low.astype(WIDE), grad * normal, grad)


def second_norm(active, weight, bias, value, first_gain, first_shift, gain, shift, cotangent):
    tokens, units = active.shape
    model_width = weight.shape[1]
    tile = 256
    block = pl.BlockSpec((tile, model_width), lambda i: (i, 0))
    line = pl.BlockSpec((1, model_width), lambda i: (0, 0))
    return pl.pallas_call(
        second_kernel,
        grid=(tokens // tile,),
        in_specs=[
            pl.BlockSpec((tile, units), lambda i: (i, 0)),
            pl.BlockSpec((units, model_width), lambda i: (0, 0)),
            line,
            block,
            line,
            line,
            line,
            line,
            block,
        ],
        out_specs=[block, block, block, pl.BlockSpec((3, model_width), lambda i: (0, 0))],
        out_shape=[
            jax.ShapeDtypeStruct((tokens, model_width), LOW),
            jax.ShapeDtypeStruct((tokens, model_width), WIDE),
            jax.ShapeDtypeStruct((tokens, model_width), LOW),
            jax.ShapeDtypeStruct((3, model_width), WIDE),
        ],
        cost_estimate=BRIEF,
        name="second_norm",
    )(active, weight, bias, value, first_gain, first_shift, gain, shift, cotangent)


def first_back_kernel(
    inner_ref, weight_ref, second_ref, value_ref, gain_ref, grad_ref, low_ref, sum_ref
):
    grad = second_ref[...] + lax.dot_general(
        inner_ref[...], weight_ref[...], NT, preferred_element_type=WIDE
    )
    normal, scale = standardise(value_ref[...])
    total = norm_back(grad, normal, scale, gain_ref[...])
    low = total.astype(LOW)
    grad_ref[...] = total
    low_ref[...] = low
    add_sums(sum_ref, low.astype(WIDE), grad * normal, grad)


def first_back(grad_inner, weight, grad_second, value, gain):
    tokens, units = grad_inner.shape
    model_width = weight.shape[0]
    tile = 256
    wide = pl.BlockSpec((tile, model_width), lambda i: (i, 0))
    whole = lambda i: (0, 0)
    return pl.pallas_call(
        first_back_kernel,
        grid=(tokens // tile,),
        in_specs=[
            pl.BlockSpec((tile, units), lambda i: (i, 0)),
            pl.BlockSpec((model_width, units), whole),
            wide,
            wide,
            pl.BlockSpec((1, model_width), whole),
        ],
        out_specs=[wide, wide, pl.BlockSpec((3, model_width), whole)],
        out_shape=[
            jax.ShapeDtypeStruct((tokens, model_width), WIDE),
            jax.ShapeDtypeStruct((tokens, model_width), LOW),
            jax.ShapeDtypeStruct((3, model_width), WIDE),
        ],
        cost_estimate=BRIEF,
        name="first_back",
    )(grad_inner, weight, grad_second, value, gain)


class Wires:
    def __init__(self, fsdp_count):
        self.fsdp_count = fsdp_count
        self.total = 4 * fsdp_count
        self.shard = lax.axis_index("fsdp")
        rep = lax.axis_index("rep")
        self.x = rep >> 1
        self.core = rep & 1
        self.meta = jnp.stack([self.shard, self.x, self.core]).astype(jnp.int32)

    def swap(self, value, mask):
        return lax.ppermute(value, AXES, [(i, i ^ mask) for i in range(self.total)])

    def own_half(self, low, high):
        return jnp.where(self.core == 1, high, low)

    def other_half(self, low, high):
        return jnp.where(self.core == 1, low, high)

    def own_rows(self, value, axis=0):
        half = value.shape[axis] // 2
        low = lax.slice_in_dim(value, 0, half, axis=axis)
        high = lax.slice_in_dim(value, half, 2 * half, axis=axis)
        return jnp.where(self.x == 1, high, low), jnp.where(self.x == 1, low, high)

    def near(self, value):
        return [self.swap(value, 8 * k) for k in range(1, self.fsdp_count // 2)]

    def share(self, near):
        return near + [self.swap(v, 1) for v in near]


    def y_halves(self, held):
        held = held.reshape((held.shape[0] // 2, 2) + held.shape[1:])
        flag = (self.shard & 1) != 0
        return jnp.where(flag, held[:, 1], held[:, 0]), jnp.where(flag, held[:, 0], held[:, 1])

    def z_block(self, held, k):
        return lax.dynamic_index_in_dim(held, (self.shard >> 1) ^ k, 0, keepdims=False)

    def z_sends(self, held):
        if held.shape[0] > 4:
            return [held]
        return [self.z_block(held, k) for k in range(1, held.shape[0])]

    def z_swap(self, sends):
        if sends[0].ndim == 2:
            return [self.swap(v, 8 * (k + 1)) for k, v in enumerate(sends)]
        held, bit = sends[0], 2
        while bit < self.fsdp_count:
            held = held.reshape((held.shape[0] // 2, 2) + held.shape[1:])
            flag = (self.shard & bit) != 0
            got = self.swap(jnp.where(flag, held[:, 0], held[:, 1]), 4 * bit)
            held = add_low(jnp.where(flag, held[:, 1], held[:, 0]), got)
            bit *= 2
        return [held[0]]

    def z_sum(self, held, got):
        if held.shape[0] > 4:
            return got[0]
        return add_low(self.z_block(held, 0), *got)

    def by_x(self, own, other):
        return jnp.where(self.x == 1, other, own), jnp.where(self.x == 1, own, other)


def tie(*values):
    return lax.optimization_barrier(values)


def join(*parts):
    return jnp.concatenate(parts, axis=0)


def row(vector):
    return vector.reshape(1, -1).astype(WIDE)


def add_low(first, *others):
    total = first.astype(WIDE)
    for other in others:
        total = total + other.astype(WIDE)
    return total.astype(LOW)


def weight_copies(meta_ref, refs, out_ref, sem, parts, half_width):
    at = 0
    copies = []
    for width, start, by_x, offset, row in parts:
        for core, x, y in itertools.product(range(2), range(2 if by_x else 1), range(2)):
            piece = refs[at]
            at += 1
            col = (meta_ref[2] ^ core) * half_width + offset
            begin = start
            if by_x:
                col = col + (meta_ref[1] ^ x) * width
                begin = start[x]
            col = pl.multiple_of(col, LANES)
            rows = slice(row, row + piece.shape[1])
            for j in range(piece.shape[0]):
                copies.append(
                    pltpu.make_async_copy(
                        piece.at[j, :, pl.ds(begin, width)],
                        out_ref.at[meta_ref[0] ^ (2 * j + y), rows, pl.ds(col, width)],
                        sem,
                    )
                )
    return copies


def assemble_kernel(meta_ref, *refs, parts, half_width):
    copies = weight_copies(meta_ref, refs, refs[-2], refs[-1], parts, half_width)
    for copy in copies:
        copy.start()
    for copy in copies:
        copy.wait()


def project(inputs, weight_ref, query_ref, value_ref, out_ref, pairs):
    group = 3 * LANES
    step = 256
    for i, p in enumerate(pairs):
        cut = slice(i * group, (i + 1) * group)
        weight = weight_ref[..., cut].reshape(inputs.shape[1], group)
        bias = jnp.concatenate(
            [query_ref[p : p + 1], jnp.zeros((1, LANES), WIDE), value_ref[p : p + 1]], axis=1
        )
        for t in range(0, inputs.shape[0], step):
            out = lax.dot_general(inputs[t : t + step], weight, NN, preferred_element_type=WIDE)
            out_ref[t : t + step, cut] = (out + bias).astype(LOW)


def project_kernel(meta_ref, inputs_ref, query_ref, value_ref, *refs, parts, half_width, pairs):
    full_ref, out_ref, sem = refs[-3:]
    copies = weight_copies(meta_ref, refs, full_ref, sem, parts, half_width)
    for copy in copies:
        copy.start()
    for copy in copies:
        copy.wait()
    project(inputs_ref, full_ref, query_ref, value_ref, out_ref, pairs)


def project_whole_kernel(inputs_ref, query_ref, value_ref, full_ref, *refs, pairs):
    project(inputs_ref, full_ref, query_ref, value_ref, refs[-1], pairs)


def joint_project(wires, inputs, pieces, query_bias, value_bias, chunk, shard_rows, behind=()):
    tokens, model_width = inputs.shape
    half_width = chunk.count * 3 * LANES
    out_shape = jax.ShapeDtypeStruct((tokens, 2 * half_width), LOW)
    on_chip = pl.BlockSpec(memory_space=pltpu.VMEM)
    anywhere = pl.BlockSpec(memory_space=pl.ANY)
    cost = BRIEF
    if not isinstance(pieces, list):
        out = pl.pallas_call(
            functools.partial(project_whole_kernel, pairs=chunk.pairs),
            out_shape=out_shape,
            in_specs=[on_chip] * 4 + [anywhere] * len(behind),
            out_specs=on_chip,
            cost_estimate=cost,
            name="joint_project",
        )(inputs, query_bias, value_bias, pieces, *behind)
        return pieces, out
    full, out = pl.pallas_call(
        functools.partial(
            project_kernel,
            parts=[(half_width, 0, False, 0, 0)],
            half_width=half_width,
            pairs=chunk.pairs,
        ),
        out_shape=[
            jax.ShapeDtypeStruct((wires.fsdp_count, shard_rows, 2 * half_width), LOW),
            out_shape,
        ],
        in_specs=[pl.BlockSpec(memory_space=pltpu.SMEM)]
        + [on_chip] * 3
        + [anywhere] * (len(pieces) + len(behind)),
        out_specs=[on_chip] * 2,
        scratch_shapes=[pltpu.SemaphoreType.DMA],
        cost_estimate=cost,
        name="joint_project",
    )(wires.meta, inputs, query_bias, value_bias, *pieces, *behind)
    return full.reshape(model_width, 2 * half_width), out


def pack_kernel(*refs, chunks, wide):
    *vector_refs, out_ref = refs
    sum_refs, vector_refs = vector_refs[: len(chunks)], vector_refs[len(chunks) :]
    out_ref[...] = jnp.zeros_like(out_ref)
    for ref, chunk in zip(sum_refs, chunks):
        for i, p in enumerate(chunk.pairs):
            total = ref[0, i, 0:1]
            for r in range(1, ref.shape[0]):
                total = total + ref[r, i, 0:1]
            out_ref[0:1, p * LANES : (p + 1) * LANES] = total[:, :LANES]
            out_ref[1:2, p * LANES : (p + 1) * LANES] = total[:, 2 * LANES :]
    row = 2
    for ref in vector_refs:
        for r, start in itertools.product(range(ref.shape[0]), range(0, ref.shape[1], wide)):
            out_ref[row : row + 1] = ref[r : r + 1, start : start + wide]
            row += 1


def pack(sums, chunks, vectors, wide):
    rows = 2 + sum(v.shape[0] * v.shape[1] // wide for v in vectors)
    return pl.pallas_call(
        functools.partial(pack_kernel, chunks=chunks, wide=wide),
        out_shape=jax.ShapeDtypeStruct(((rows + 7) // 8 * 8, wide), WIDE),
        name="pack",
    )(*sums, *vectors)


def assemble(wires, shard_rows, half_width, parts):
    count = wires.fsdp_count
    operands, plan = [], []
    for pieces, *where in parts:
        plan.append(where)
        operands += pieces
    shape = (count, shard_rows, 2 * half_width)
    full = pl.pallas_call(
        functools.partial(assemble_kernel, parts=plan, half_width=half_width),
        out_shape=jax.ShapeDtypeStruct(shape, LOW),
        in_specs=[pl.BlockSpec(memory_space=pltpu.SMEM)]
        + [pl.BlockSpec(memory_space=pl.ANY)] * len(operands),
        out_specs=pl.BlockSpec(memory_space=pltpu.VMEM),
        scratch_shapes=[pltpu.SemaphoreType.DMA],
        cost_estimate=BRIEF,
        name="assemble",
    )(wires.meta, *operands)
    return full.reshape(count * shard_rows, 2 * half_width)


def pieces_kernel(meta_ref, weight_ref, *out_refs, chunks):
    model_width = weight_ref.shape[1] // 3
    for chunk, out_ref in zip(chunks, out_refs):
        for i, part in itertools.product(range(chunk.count), range(3)):
            pair = meta_ref[2] * chunk.half + chunk.first + i
            col = pl.multiple_of(part * model_width + pair * LANES, LANES)
            place = (3 * i + part) * LANES
            out_ref[:, place : place + LANES] = weight_ref[:, pl.ds(col, LANES)]


def own_pairs(wires, weight, chunks):
    return pl.pallas_call(
        functools.partial(pieces_kernel, chunks=chunks),
        out_shape=[
            jax.ShapeDtypeStruct((weight.shape[0], c.count * 3 * LANES), LOW) for c in chunks
        ],
        in_specs=[
            pl.BlockSpec(memory_space=pltpu.SMEM),
            pl.BlockSpec(memory_space=pltpu.VMEM),
        ],
        out_specs=[pl.BlockSpec(memory_space=pltpu.VMEM)] * len(chunks),
        cost_estimate=BRIEF,
        name="own_pairs",
    )(wires.meta, weight)


def pair_columns(array, pairs, model_width):
    return jnp.concatenate(
        [
            array[..., part * model_width + p * LANES : part * model_width + (p + 1) * LANES]
            for p in pairs
            for part in range(3)
        ],
        axis=-1,
    )


def natural_columns(pieces, chunks):
    where = {}
    for piece, chunk in zip(pieces, chunks):
        for i, p in enumerate(chunk.pairs):
            for part in range(3):
                place = (3 * i + part) * LANES
                where[(part, p)] = piece[..., place : place + LANES]
    return jnp.concatenate([where[key] for key in sorted(where)], axis=-1)


def body(
    fsdp_count,
    layer_input,
    segment_ids,
    joint_weight,
    query_bias,
    value_bias,
    close_weight,
    close_bias,
    first_gain,
    first_shift,
    expand_weight,
    expand_bias,
    shrink_weight,
    shrink_bias,
    second_gain,
    second_shift,
    cotangent,
):
    row_count, pos_count, model_width = layer_input.shape
    hidden_units = expand_bias.shape[0]
    tok_count = row_count * pos_count
    flat_input = layer_input.reshape(tok_count, model_width)
    wires = Wires(fsdp_count)
    half_pairs = model_width // LANES // 2
    chunks = (Chunk(0, 1, half_pairs), Chunk(1, half_pairs - 1, half_pairs))
    shard_rows = joint_weight.shape[0]

    half_model, half_hidden = model_width // 2, hidden_units // 2
    unit = half_hidden // 3
    expand_half = wires.own_half(expand_weight[:, :half_hidden], expand_weight[:, half_hidden:])
    close_half = wires.own_half(close_weight[:, :half_model], close_weight[:, half_model:])
    shrink_half = wires.own_half(shrink_weight[:, :half_model], shrink_weight[:, half_model:])
    shrink_rows = shrink_half.shape[0] // 2
    aligned = fsdp_count == 8 and shard_rows % 32 == 0
    query_rows = query_bias.astype(WIDE).reshape(-1, LANES)
    value_rows = value_bias.astype(WIDE).reshape(-1, LANES)

    inputs_t = jnp.swapaxes(layer_input, 1, 2)
    lines = [
        row(v)
        for v in (
            close_bias,
            first_gain,
            first_shift,
            expand_bias,
            shrink_bias,
            second_gain,
            second_shift,
        )
    ]
    segments = segment_ids[:, :, None], segment_ids[:, None, :]

    def project_and_attend(place, shared, context):
        full, part = joint_project(
            wires, flat_input, shared, query_rows, value_rows, chunks[place], shard_rows
        )
        return full, part.reshape(row_count, pos_count, -1)

    if aligned:
        first, second = (v[None] for v in own_pairs(wires, joint_weight, chunks))
        split = wires.by_x(expand_half[:, unit : 2 * unit], expand_half[:, 2 * unit :])[0]
        piece = jnp.concatenate([expand_half[:, :unit], close_half, split], axis=1)[None]
        shrink = shrink_half[None]
        first_near = wires.near(first)
        ready = [inputs_t, query_rows, value_rows, *segments]
        first, first_near, ready = lax.optimization_barrier((first, first_near, ready))
        inputs_t, query_rows, value_rows, *segments = ready
        first = join(first, *first_near)
        first, second = tie(first, second)
        first_y = wires.swap(first, 4)
        second_near = wires.near(second)
        first, first_y, second_near[0], second_near[1] = tie(
            first, first_y, second_near[0], second_near[1]
        )
        first_shared = wires.share([first, first_y])
        first_shared, piece, second, second_near = lax.optimization_barrier(
            (first_shared, piece, second, second_near)
        )
        second = join(second, *second_near)
        second_y = wires.swap(second, 4)
        piece_near = wires.near(piece)
        full, part = project_and_attend(0, first_shared, None)
        joint_full, mixed = [full], [part]
        context, w, inv = attend(mixed[0], segments, chunks[0])
        weights, inverse = [w], [inv]
        context, second, second_y, piece_near[0], piece_near[1] = tie(
            context, second, second_y, piece_near[0], piece_near[1]
        )
        second_shared = wires.share([second, second_y])
        second_shared, piece, shrink, piece_near, lines = lax.optimization_barrier(
            (second_shared, piece, shrink, piece_near, lines)
        )
        piece = join(piece, *piece_near)
        split = piece[..., unit + half_model :]
        piece, split = tie(piece, split)
        piece_y = wires.swap(piece, 4)
        split_x = wires.swap(split, 2)
        shrink_near = wires.near(shrink)
        full, part = project_and_attend(1, second_shared, context)
        joint_full.append(full)
        part, split, split_x = tie(part, split, split_x)
        mixed.append(part)
        context, w, inv = attend(mixed[1], segments, chunks[1], context)
        weights.append(w)
        inverse.append(inv)
        context, piece, piece_y, shrink, *shrink_near = tie(
            context, piece, piece_y, shrink, *shrink_near
        )
        plain_shared = wires.share([piece, piece_y])
        split_yx = wires.swap(piece_y[..., unit + half_model :], 2)
        shrink = join(shrink, *shrink_near)
        *plain_shared, shrink = tie(*plain_shared, shrink)
        shrink_y = wires.swap(shrink, 4)
        close_full = assemble(
            wires, shard_rows, half_model, [(plain_shared, half_model, unit, False, 0, 0)]
        )
    else:
        joint_full, mixed, weights, inverse = [], [], [], []
        context = None
        for place, chunk in enumerate(chunks):
            shared = lax.all_gather(
                pair_columns(joint_weight, chunk.pairs, model_width), "fsdp", axis=0, tiled=True
            )
            full, part = project_and_attend(place, shared, context)
            joint_full.append(full)
            mixed.append(part)
            context, w, inv = attend(part, segments, chunk, context)
            weights.append(w)
            inverse.append(inv)
        close_full, expand_full, shrink_full = (
            lax.all_gather(w, "fsdp", axis=0, tiled=True)
            for w in (close_weight, expand_weight, shrink_weight)
        )
    context_low = context.reshape(tok_count, model_width)

    first_sum, hidden_low = first_norm(
        context_low, close_full, lines[0], flat_input, lines[1], lines[2]
    )
    if aligned:
        own, other = plain_shared[:2], plain_shared[2:]
        hidden_low, split_x, split_yx = tie(hidden_low, split_x, split_yx)
        split_shared = wires.share([split_x, split_yx])
        expand_full = assemble(
            wires,
            shard_rows,
            half_hidden,
            [
                (plain_shared, unit, 0, False, 0, 0),
                (
                    [*own, *split_shared[:2], *other, *split_shared[2:]],
                    unit,
                    [unit + half_model, 0],
                    True,
                    unit,
                    0,
                ),
            ],
        )
    active_low, slope = expand_gelu(hidden_low, expand_full, lines[3])
    if aligned:
        shrink_core = wires.swap(shrink, 1)
        active_low, shrink, shrink_y, shrink_core = tie(
            active_low, shrink, shrink_y, shrink_core
        )
        shrink_shared = [shrink, shrink_y, shrink_core, wires.swap(shrink_y, 1)]
        shrink_full = assemble(
            wires,
            shrink_weight.shape[0],
            half_model,
            [(shrink_shared, half_model, 0, False, 0, 0)],
        )
    layer_output, grad_second, grad_ffn, second_sums = second_norm(
        active_low,
        shrink_full,
        lines[4],
        first_sum,
        lines[1],
        lines[2],
        lines[5],
        lines[6],
        cotangent.reshape(tok_count, model_width),
    )
    layer_output = layer_output.reshape(row_count, pos_count, model_width)

    def outgoing(left, right):
        half = right.shape[1] // 2
        send = wires.other_half(right[:, :half], right[:, half:])
        return jnp.einsum("tf,td->fd", left, send, preferred_element_type=WIDE).astype(LOW)

    def kept(left, right):
        half = right.shape[1] // 2
        keep = wires.own_half(right[:, :half], right[:, half:])
        return jnp.einsum("tf,td->fd", left, keep, preferred_element_type=WIDE)

    def by_shard(held):
        return held.reshape(fsdp_count, held.shape[0] // fsdp_count, held.shape[1])

    def staying(left, right, got):
        return by_shard(add_low(kept(left, right), got))

    def both_halves(mine):
        other = wires.swap(mine, 1)
        return wires.own_half(mine, other), wires.own_half(other, mine)

    shrink_send = outgoing(active_low, grad_ffn)
    active_low, shrink_send = tie(active_low, shrink_send)
    shrink_got = wires.swap(shrink_send, 1)
    shrink_keep = kept(active_low, grad_ffn)
    grad_ffn, shrink_keep, shrink_got = tie(grad_ffn, shrink_keep, shrink_got)
    shrink_held = by_shard(add_low(shrink_keep, shrink_got))
    top_keep, top_send = wires.y_halves(shrink_held[:, :shrink_rows])
    low_keep, low_send = wires.own_rows(shrink_held[:, shrink_rows:], axis=1)
    grad_ffn, top_keep, top_send, low_keep, low_send = tie(
        grad_ffn, top_keep, top_send, low_keep, low_send
    )
    top_got = wires.swap(top_send, 4)
    low_got = wires.swap(low_send, 2)
    grad_inner, inner_sum = inner_grad(grad_ffn, shrink_full, slope)
    grad_inner, top_keep, top_got, low_keep, low_got = tie(
        grad_inner, top_keep, top_got, low_keep, low_got
    )
    low_keep, low_send = wires.y_halves(add_low(low_keep, low_got))
    top_held = add_low(top_keep, top_got)
    hidden_low, low_keep, low_send = tie(hidden_low, low_keep, low_send)
    low_got = wires.swap(low_send, 4)
    expand_send = outgoing(hidden_low, grad_inner)
    hidden_low, expand_send = tie(hidden_low, expand_send)
    expand_got = wires.swap(expand_send, 1)
    expand_keep = kept(hidden_low, grad_inner)
    grad_inner, expand_keep, expand_got = tie(grad_inner, expand_keep, expand_got)
    expand_held = by_shard(add_low(expand_keep, expand_got))
    quarter = half_hidden // 2
    left_keep, left_send = wires.y_halves(expand_held[..., :quarter])
    right_keep, right_send = wires.by_x(
        expand_held[..., quarter : quarter + quarter // 2],
        expand_held[..., quarter + quarter // 2 :],
    )
    (
        grad_inner,
        left_keep,
        left_send,
        right_keep,
        right_send,
        low_keep,
        low_got,
        top_held,
        *top_sends,
    ) = tie(
        grad_inner,
        left_keep,
        left_send,
        right_keep,
        right_send,
        low_keep,
        low_got,
        top_held,
        *wires.z_sends(top_held),
    )
    top_got = wires.z_swap(top_sends)
    left_got = wires.swap(left_send, 4)
    right_got = wires.swap(right_send, 2)
    grad_first, grad_branch, first_sums = first_back(
        grad_inner, expand_full, grad_second, first_sum, lines[1]
    )
    grad_branch, left_keep, left_got, right_keep, right_got, top_held, *top_got = tie(
        grad_branch, left_keep, left_got, right_keep, right_got, top_held, *top_got
    )
    right_held = add_low(right_keep, right_got)
    top_mine = wires.z_sum(top_held, top_got)
    mid_held = jnp.concatenate([add_low(left_keep, left_got), add_low(low_keep, low_got)], axis=2)
    context_low, grad_branch = tie(context_low, grad_branch)
    close_send = outgoing(context_low, grad_branch)
    grad_branch, close_send = tie(grad_branch, close_send)
    close_got = wires.swap(close_send, 1)
    grad_context = jnp.einsum(
        "te,de->td", grad_branch, close_full, preferred_element_type=WIDE
    ).astype(LOW)
    context_low, grad_context, close_got = tie(context_low, grad_context, close_got)
    close_held = staying(context_low, grad_branch, close_got)
    grad_context = grad_context.reshape(row_count, pos_count, model_width)
    close_keep, close_send = wires.y_halves(jnp.concatenate([right_held, close_held], axis=2))
    (
        grad_context,
        close_keep,
        close_send,
        top_mine,
        mid_held,
        *mid_sends,
    ) = tie(
        grad_context,
        close_keep,
        close_send,
        top_mine,
        mid_held,
        *wires.z_sends(mid_held),
    )
    top_other = wires.swap(top_mine, 2)
    close_got = wires.swap(close_send, 4)
    mid_got = wires.z_swap(mid_sends)

    grad_mixed, bias_sums, joint_parts = {}, {}, {}
    grad_mixed[1], bias_sums[1], joint_parts[1] = attend_back(
        mixed[1], weights[1], context, inverse[1], grad_context, inputs_t, chunks[1]
    )
    grad_mixed[1] = grad_mixed[1].reshape(tok_count, -1)
    large, close_keep, close_got, top_mine, top_other, mid_held, *mid_got = tie(
        joint_parts[1], close_keep, close_got, top_mine, top_other, mid_held, *mid_got
    )
    large_got = wires.swap(wires.other_half(large[0], large[1]), 1)
    second_held = add_low(close_keep, close_got)
    large, large_got, second_held, *second_sends = tie(
        large, large_got, second_held, *wires.z_sends(second_held)
    )
    second_got = wires.z_swap(second_sends)
    large_keep, large_send = wires.own_rows(
        by_shard(add_low(wires.own_half(large[0], large[1]), large_got)), axis=1
    )
    grad_context, large_keep, large_send = tie(grad_context, large_keep, large_send)
    large_got = wires.swap(large_send, 2)
    grad_mixed[0], bias_sums[0], joint_parts[0] = attend_back(
        mixed[0], weights[0], context, inverse[0], grad_context, inputs_t, chunks[0]
    )
    grad_mixed[0] = grad_mixed[0].reshape(tok_count, -1)
    small, large_keep, large_got, second_held, *second_got = tie(
        joint_parts[0], large_keep, large_got, second_held, *second_got
    )
    small_got = wires.swap(wires.other_half(small[0], small[1]), 1)

    packed = pack(
        [bias_sums[0], bias_sums[1]],
        chunks,
        [
            first_sums,
            second_sums,
            inner_sum,
        ],
        model_width,
    )

    large_keep, large_send = wires.y_halves(add_low(large_keep, large_got))
    small, small_got, packed, large_keep, large_send = tie(
        small, small_got, packed, large_keep, large_send
    )
    large_got = wires.swap(large_send, 4)
    vector_got = wires.swap(packed, 1)
    small_keep, small_send = wires.y_halves(
        by_shard(add_low(wires.own_half(small[0], small[1]), small_got))
    )
    small_keep, small_send, packed, vector_got = tie(small_keep, small_send, packed, vector_got)
    small_got = wires.swap(small_send, 4)
    packed = packed + vector_got
    mine = jnp.concatenate(
        [wires.z_sum(mid_held, mid_got), wires.z_sum(second_held, second_got)], axis=1
    )
    grad_mixed[0], grad_mixed[1], packed, mine = tie(grad_mixed[0], grad_mixed[1], packed, mine)
    other = wires.swap(mine, 2)
    vector_got = wires.swap(packed, 2)
    input_grad = grad_first + jnp.einsum(
        "te,de->td", grad_mixed[0], joint_full[0], preferred_element_type=WIDE
    )
    input_grad, packed, vector_got = tie(input_grad, packed, vector_got)
    packed = packed + vector_got
    vector_got = wires.swap(packed, 4)
    input_grad = input_grad + jnp.einsum(
        "te,de->td", grad_mixed[1], joint_full[1], preferred_element_type=WIDE
    )
    input_grad, small_keep, small_got, large_keep, large_got, packed, vector_got, mine, other = tie(
        input_grad, small_keep, small_got, large_keep, large_got, packed, vector_got, mine, other
    )
    small_held = add_low(small_keep, small_got)
    half_rows = small_held.shape[1] // 2
    joint_held = jnp.concatenate(
        [small_held[:, :half_rows], small_held[:, half_rows:], add_low(large_keep, large_got)],
        axis=2,
    )
    packed = packed + vector_got
    packed, joint_held, *joint_sends = tie(packed, joint_held, *wires.z_sends(joint_held))
    joint_got = wires.z_swap(joint_sends)
    vector_got = wires.swap(packed, 8)
    joint_held, packed, vector_got, *joint_got = tie(
        joint_held, packed, vector_got, *joint_got
    )
    joint_mine, packed = tie(wires.z_sum(joint_held, joint_got), packed + vector_got)

    top_mine = add_low(top_mine, top_other)
    total = add_low(mine, other)
    cuts = [quarter, quarter + half_model, quarter + half_model + quarter // 2]
    left, _, _, close = jnp.split(total, cuts, axis=1)
    (_, low, right, _), (_, low_other, right_other, _) = (
        jnp.split(v, cuts, axis=1) for v in (mine, other)
    )
    shrink_mine = jnp.concatenate([top_mine, *wires.by_x(low, low_other)], axis=0)
    second_mine = jnp.concatenate([left, *wires.by_x(right, right_other), close], axis=1)
    joint_other = wires.swap(joint_mine, 2)
    vector_got = wires.swap(packed, 16)
    joint_mine, joint_other, packed, vector_got = tie(
        joint_mine, joint_other, packed, vector_got
    )
    small_width = small_held.shape[2]
    small_mine = add_low(joint_mine[:, : 2 * small_width], joint_other[:, : 2 * small_width])
    joint_mine = jnp.concatenate(
        [
            jnp.concatenate([small_mine[:, :small_width], small_mine[:, small_width:]], axis=0),
            jnp.concatenate(
                wires.by_x(joint_mine[:, 2 * small_width :], joint_other[:, 2 * small_width :]),
                axis=0,
            ),
        ],
        axis=1,
    )

    shrink_grad = jnp.concatenate(both_halves(shrink_mine), axis=1).astype(WIDE)
    low, high = both_halves(second_mine)
    cut = hidden_units // 2
    expand_grad = jnp.concatenate([low[:, :cut], high[:, :cut]], axis=1).astype(WIDE)
    close_grad = jnp.concatenate([low[:, cut:], high[:, cut:]], axis=1).astype(WIDE)
    joint_mine, summed = tie(joint_mine, packed + vector_got)
    low, high = both_halves(joint_mine)
    mask = 32
    while mask < wires.total:
        summed = summed + wires.swap(summed, mask)
        mask *= 2
    cut = chunks[0].count * 3 * LANES
    joint_grad = natural_columns(
        [
            jnp.concatenate([low[:, :cut], high[:, :cut]], axis=1),
            jnp.concatenate([low[:, cut:], high[:, cut:]], axis=1),
        ],
        chunks,
    ).astype(WIDE)
    (
        query_bias_grad,
        value_bias_grad,
        close_bias_grad,
        first_gain_grad,
        first_shift_grad,
        shrink_bias_grad,
        second_gain_grad,
        second_shift_grad,
    ) = (summed[i] for i in range(8))
    expand_bias_grad = summed[8 : 8 + hidden_units // model_width].reshape(hidden_units)
    return (
        layer_output,
        input_grad.reshape(row_count, pos_count, model_width),
        joint_grad,
        query_bias_grad,
        value_bias_grad,
        close_grad,
        close_bias_grad,
        first_gain_grad,
        first_shift_grad,
        expand_grad,
        expand_bias_grad,
        shrink_grad,
        shrink_bias_grad,
        second_gain_grad,
        second_shift_grad,
    )


def solution(mesh):
    rows = P(("fsdp", "rep"), None, None)
    sharded = P("fsdp", None)
    copied = P()
    return jax.shard_map(
        functools.partial(body, mesh.shape["fsdp"]),
        mesh=mesh,
        in_specs=(
            rows,
            P(("fsdp", "rep"), None),
            sharded,
            copied,
            copied,
            sharded,
            copied,
            copied,
            copied,
            sharded,
            copied,
            sharded,
            copied,
            copied,
            copied,
            rows,
        ),
        out_specs=(
            rows,
            rows,
            sharded,
            copied,
            copied,
            sharded,
            copied,
            copied,
            copied,
            sharded,
            copied,
            sharded,
            copied,
            copied,
            copied,
        ),
        check_vma=False,
    )
```

```python
import functools
import itertools
import math

import jax
import jax.numpy as jnp
from jax import lax
from jax.experimental import pallas as pl
from jax.experimental.pallas import tpu as pltpu
from jax.sharding import PartitionSpec as P

HEADS = 12
EPS = 1e-12
AXES = ("fsdp", "rep")
LANES = 128
NT = (((1,), (1,)), ((), ()))
NN = (((1,), (0,)), ((), ()))
LOW = jnp.bfloat16
WIDE = jnp.float32
BRIEF = pl.CostEstimate(flops=0, bytes_accessed=0, transcendentals=0)


def attend_kernel(mixed_ref, seg_col_ref, seg_row_ref, *refs):
    context_ref, weights_ref, inverse_ref = refs[-3:]
    pos = mixed_ref.shape[0]
    head = mixed_ref.shape[1] // 6
    same = seg_col_ref[...] == seg_row_ref[...]
    values_t = mixed_ref[:, 4 * head : 6 * head].T
    ones = jnp.ones((16, pos), LOW)
    outs, inverses = [], []
    for h in range(2):
        queries = mixed_ref[:, h * head : (h + 1) * head] * LOW(1.0 / math.sqrt(head))
        keys = mixed_ref[:, (2 + h) * head : (3 + h) * head]
        scores = lax.dot_general(keys, queries, NT, preferred_element_type=WIDE)
        scores = jnp.where(same, scores, -jnp.inf)
        raised = jnp.exp(scores - jnp.max(scores, axis=0, keepdims=True)).astype(LOW)
        weights_ref[h] = raised
        extended = jnp.concatenate([values_t[h * head : (h + 1) * head], ones], axis=0)
        out = lax.dot_general(extended, raised, NN, preferred_element_type=WIDE)
        inverse = 1.0 / out[head : head + 1]
        outs.append(out[:head] * inverse)
        inverses.append(jnp.broadcast_to(inverse, (head, pos)))
    context_ref[...] = jnp.concatenate(outs, axis=0).T.astype(LOW)
    inverse_ref[...] = jnp.concatenate(inverses, axis=0).T


def attend_back_kernel(
    mixed_ref,
    weights_ref,
    context_ref,
    inverse_ref,
    grad_ref,
    inputs_ref,
    out_ref,
    sum_ref,
    joint_ref,
    total_ref,
):
    row = pl.program_id(1)
    head = mixed_ref.shape[1] // 6
    scale = LOW(1.0 / math.sqrt(head))
    grad = grad_ref[...].astype(WIDE) * inverse_ref[...]
    product = (grad * context_ref[...].astype(WIDE)).astype(LOW)
    grad_low = grad.astype(LOW)
    queries = mixed_ref[:, : 2 * head] * scale
    keys_t = (mixed_ref[:, 2 * head : 4 * head] * scale).T
    ones = jnp.ones((8, head), LOW)
    grad_q, grad_k, grad_v = [], [], []
    for h in range(2):
        cut = slice(h * head, (h + 1) * head)
        values = mixed_ref[:, (4 + h) * head : (5 + h) * head]
        inner = lax.dot_general(ones, product[:, cut], NT, preferred_element_type=WIDE)[0:1]
        raised = weights_ref[h]
        grad_attn = lax.dot_general(values, grad_low[:, cut], NT, preferred_element_type=WIDE)
        grad_scores = raised * (grad_attn - inner).astype(LOW)
        grad_k.append(lax.dot_general(grad_scores, queries[:, cut], NN, preferred_element_type=WIDE))
        grad_v.append(lax.dot_general(raised, grad_low[:, cut], NN, preferred_element_type=WIDE))
        grad_q.append(lax.dot_general(keys_t[cut], grad_scores, NN, preferred_element_type=WIDE))
    out = jnp.concatenate([jnp.concatenate(grad_q, axis=0).T] + grad_k + grad_v, axis=1).astype(LOW)
    out_ref[...] = out
    sum_ref[...] = jnp.broadcast_to(
        jnp.sum(out.astype(WIDE), axis=0, keepdims=True), sum_ref.shape
    )
    part = lax.dot_general(inputs_ref[row], out, NN, preferred_element_type=WIDE)

    @pl.when(row == 0)
    def _():
        total_ref[...] = part

    @pl.when(row > 0)
    def _():
        total_ref[...] += part

    @pl.when(row == pl.num_programs(1) - 1)
    def _():
        joint_ref[...] = total_ref[...].astype(LOW)


class Chunk:
    def __init__(self, first, count, half):
        self.first, self.count, self.half = first, count, half
        self.pairs = [c * half + first + i for c in range(2) for i in range(count)]

    def block(self, place):
        return (place // self.count) * self.half + self.first + place % self.count


def attend(mixed, segments, chunk, context=None, behind=()):
    rows, pos, width = mixed.shape
    group = width // len(chunk.pairs)
    pair = group // 3
    count = len(chunk.pairs)
    total = 2 * chunk.half
    in_specs = [
        pl.BlockSpec((None, pos, group), lambda r, p: (r, 0, p)),
        pl.BlockSpec((None, pos, 1), lambda r, p: (r, 0, 0)),
        pl.BlockSpec((None, 1, pos), lambda r, p: (r, 0, 0)),
    ]
    operands = [mixed, *segments]
    aliases = {}
    if context is not None:
        in_specs.append(pl.BlockSpec(memory_space=pl.ANY))
        operands.append(context)
        aliases = {3: 0}
    in_specs += [pl.BlockSpec(memory_space=pl.ANY)] * len(behind)
    operands += behind
    return pl.pallas_call(
        attend_kernel,
        grid=(rows, count),
        in_specs=in_specs,
        out_specs=[
            pl.BlockSpec((None, pos, pair), lambda r, p: (r, 0, chunk.block(p))),
            pl.BlockSpec((None, None, 2, pos, pos), lambda r, p: (r, p, 0, 0, 0)),
            pl.BlockSpec((None, pos, pair), lambda r, p: (r, 0, p)),
        ],
        out_shape=[
            jax.ShapeDtypeStruct((rows, pos, total * pair), LOW),
            jax.ShapeDtypeStruct((rows, count, 2, pos, pos), LOW),
            jax.ShapeDtypeStruct((rows, pos, count * pair), WIDE),
        ],
        input_output_aliases=aliases,
        cost_estimate=BRIEF,
        name="attend",
    )(*operands)


def attend_back(mixed, weights, context, inverse, grad, inputs, chunk):
    rows, pos, width = mixed.shape
    model_width = inputs.shape[1]
    count = len(chunk.pairs)
    group = width // count
    pair = group // 3
    natural = pl.BlockSpec((None, pos, pair), lambda p, r: (r, 0, chunk.block(p)))
    return pl.pallas_call(
        attend_back_kernel,
        grid=(count, rows),
        in_specs=[
            pl.BlockSpec((None, pos, group), lambda p, r: (r, 0, p)),
            pl.BlockSpec((None, None, 2, pos, pos), lambda p, r: (r, p, 0, 0, 0)),
            natural,
            pl.BlockSpec((None, pos, pair), lambda p, r: (r, 0, p)),
            natural,
            pl.BlockSpec((rows, model_width, pos), lambda p, r: (0, 0, 0)),
        ],
        out_specs=[
            pl.BlockSpec((None, pos, group), lambda p, r: (r, 0, p)),
            pl.BlockSpec((None, None, 8, group), lambda p, r: (r, p, 0, 0)),
            pl.BlockSpec(
                (None, model_width, group),
                lambda p, r: (p // chunk.count, 0, p % chunk.count),
            ),
        ],
        out_shape=[
            jax.ShapeDtypeStruct((rows, pos, count * group), LOW),
            jax.ShapeDtypeStruct((rows, count, 8, group), WIDE),
            jax.ShapeDtypeStruct((2, model_width, chunk.count * group), LOW),
        ],
        scratch_shapes=[pltpu.VMEM((model_width, group), WIDE)],
        cost_estimate=BRIEF,
        name="attend_back",
    )(mixed, weights, context, inverse, grad, inputs)


def expand_kernel(hidden_ref, weight_ref, bias_ref, active_ref, slope_ref, *, chunks):
    step = hidden_ref.shape[0] // chunks
    for i in range(chunks):
        cut = slice(i * step, (i + 1) * step)
        inner = lax.dot_general(hidden_ref[cut], weight_ref[...], NN, preferred_element_type=WIDE)
        inner = inner + bias_ref[...]
        share = 0.5 + 0.5 * lax.erf(inner * math.sqrt(0.5))
        active_ref[cut] = (inner * share).astype(LOW)
        density = jnp.exp(-0.5 * inner * inner) * (1.0 / math.sqrt(2.0 * math.pi))
        slope_ref[cut] = (share + inner * density).astype(LOW)


def expand_gelu(hidden, weight, bias):
    tokens, model_width = hidden.shape
    units = weight.shape[1]
    tile = 768
    return pl.pallas_call(
        functools.partial(expand_kernel, chunks=8),
        grid=(units // tile,),
        in_specs=[
            pl.BlockSpec((tokens, model_width), lambda j: (0, 0)),
            pl.BlockSpec((model_width, tile), lambda j: (0, j)),
            pl.BlockSpec((1, tile), lambda j: (0, j)),
        ],
        out_specs=[pl.BlockSpec((tokens, tile), lambda j: (0, j))] * 2,
        out_shape=[jax.ShapeDtypeStruct((tokens, units), LOW)] * 2,
        cost_estimate=BRIEF,
        name="expand_gelu",
    )(hidden, weight, bias)


def inner_grad_kernel(grad_ref, weight_ref, slope_ref, out_ref, sum_ref, *, chunks):
    step = grad_ref.shape[0] // chunks
    total = jnp.zeros((1, weight_ref.shape[0]), WIDE)
    for i in range(chunks):
        cut = slice(i * step, (i + 1) * step)
        grad = lax.dot_general(grad_ref[cut], weight_ref[...], NT, preferred_element_type=WIDE)
        grad = (grad * slope_ref[cut].astype(WIDE)).astype(LOW)
        out_ref[cut] = grad
        total = total + jnp.sum(grad.astype(WIDE), axis=0, keepdims=True)
    sum_ref[...] = total


def inner_grad(grad, weight, slope):
    tokens, model_width = grad.shape
    units = weight.shape[0]
    tile = 768
    return pl.pallas_call(
        functools.partial(inner_grad_kernel, chunks=2),
        grid=(units // tile,),
        in_specs=[
            pl.BlockSpec((tokens, model_width), lambda j: (0, 0)),
            pl.BlockSpec((tile, model_width), lambda j: (j, 0)),
            pl.BlockSpec((tokens, tile), lambda j: (0, j)),
        ],
        out_specs=[
            pl.BlockSpec((tokens, tile), lambda j: (0, j)),
            pl.BlockSpec((1, tile), lambda j: (0, j)),
        ],
        out_shape=[
            jax.ShapeDtypeStruct((tokens, units), LOW),
            jax.ShapeDtypeStruct((1, units), WIDE),
        ],
        cost_estimate=BRIEF,
        name="inner_grad",
    )(grad, weight, slope)


def standardise(value):
    centred = value - jnp.mean(value, axis=-1, keepdims=True)
    scale = lax.rsqrt(jnp.mean(centred * centred, axis=-1, keepdims=True) + EPS)
    return centred * scale, scale


def norm_back(grad, normal, scale, gain):
    grad_normal = grad * gain
    return scale * (
        grad_normal
        - jnp.mean(grad_normal, axis=-1, keepdims=True)
        - normal * jnp.mean(grad_normal * normal, axis=-1, keepdims=True)
    )


def add_sums(sum_ref, *values):
    sums = jnp.concatenate([jnp.sum(v, axis=0, keepdims=True) for v in values], axis=0)
    first = pl.program_id(0) == 0

    @pl.when(first)
    def _():
        sum_ref[...] = sums

    @pl.when(jnp.logical_not(first))
    def _():
        sum_ref[...] += sums


def first_kernel(
    context_ref, weight_ref, bias_ref, inputs_ref, gain_ref, shift_ref, sum_ref, low_ref
):
    branch = lax.dot_general(
        context_ref[...], weight_ref[...], NN, preferred_element_type=WIDE
    )
    total = inputs_ref[...].astype(WIDE) + (branch + bias_ref[...])
    sum_ref[...] = total
    low_ref[...] = (standardise(total)[0] * gain_ref[...] + shift_ref[...]).astype(LOW)


def first_norm(context, weight, bias, inputs, gain, shift):
    tokens, model_width = context.shape
    tile = 512
    block = pl.BlockSpec((tile, model_width), lambda i: (i, 0))
    line = pl.BlockSpec((1, model_width), lambda i: (0, 0))
    return pl.pallas_call(
        first_kernel,
        grid=(tokens // tile,),
        in_specs=[
            block,
            pl.BlockSpec((model_width, model_width), lambda i: (0, 0)),
            line,
            block,
            line,
            line,
        ],
        out_specs=[block, block],
        out_shape=[
            jax.ShapeDtypeStruct((tokens, model_width), WIDE),
            jax.ShapeDtypeStruct((tokens, model_width), LOW),
        ],
        cost_estimate=BRIEF,
        name="first_norm",
    )(context, weight, bias, inputs, gain, shift)


def second_kernel(
    active_ref,
    weight_ref,
    bias_ref,
    value_ref,
    first_gain_ref,
    first_shift_ref,
    gain_ref,
    shift_ref,
    cotangent_ref,
    out_ref,
    grad_ref,
    low_ref,
    sum_ref,
):
    ffn_out = bias_ref[...] + lax.dot_general(
        active_ref[...], weight_ref[...], NN, preferred_element_type=WIDE
    )
    hidden = standardise(value_ref[...])[0] * first_gain_ref[...] + first_shift_ref[...]
    normal, scale = standardise(hidden + ffn_out)
    out_ref[...] = (normal * gain_ref[...] + shift_ref[...]).astype(LOW)
    grad = cotangent_ref[...].astype(WIDE)
    total = norm_back(grad, normal, scale, gain_ref[...])
    low = total.astype(LOW)
    grad_ref[...] = total
    low_ref[...] = low
    add_sums(sum_ref, low.astype(WIDE), grad * normal, grad)


def second_norm(active, weight, bias, value, first_gain, first_shift, gain, shift, cotangent):
    tokens, units = active.shape
    model_width = weight.shape[1]
    tile = 256
    block = pl.BlockSpec((tile, model_width), lambda i: (i, 0))
    line = pl.BlockSpec((1, model_width), lambda i: (0, 0))
    return pl.pallas_call(
        second_kernel,
        grid=(tokens // tile,),
        in_specs=[
            pl.BlockSpec((tile, units), lambda i: (i, 0)),
            pl.BlockSpec((units, model_width), lambda i: (0, 0)),
            line,
            block,
            line,
            line,
            line,
            line,
            block,
        ],
        out_specs=[block, block, block, pl.BlockSpec((3, model_width), lambda i: (0, 0))],
        out_shape=[
            jax.ShapeDtypeStruct((tokens, model_width), LOW),
            jax.ShapeDtypeStruct((tokens, model_width), WIDE),
            jax.ShapeDtypeStruct((tokens, model_width), LOW),
            jax.ShapeDtypeStruct((3, model_width), WIDE),
        ],
        cost_estimate=BRIEF,
        name="second_norm",
    )(active, weight, bias, value, first_gain, first_shift, gain, shift, cotangent)


def first_back_kernel(
    inner_ref, weight_ref, second_ref, value_ref, gain_ref, grad_ref, low_ref, sum_ref
):
    grad = second_ref[...] + lax.dot_general(
        inner_ref[...], weight_ref[...], NT, preferred_element_type=WIDE
    )
    normal, scale = standardise(value_ref[...])
    total = norm_back(grad, normal, scale, gain_ref[...])
    low = total.astype(LOW)
    grad_ref[...] = total
    low_ref[...] = low
    add_sums(sum_ref, low.astype(WIDE), grad * normal, grad)


def first_back(grad_inner, weight, grad_second, value, gain):
    tokens, units = grad_inner.shape
    model_width = weight.shape[0]
    tile = 256
    wide = pl.BlockSpec((tile, model_width), lambda i: (i, 0))
    whole = lambda i: (0, 0)
    return pl.pallas_call(
        first_back_kernel,
        grid=(tokens // tile,),
        in_specs=[
            pl.BlockSpec((tile, units), lambda i: (i, 0)),
            pl.BlockSpec((model_width, units), whole),
            wide,
            wide,
            pl.BlockSpec((1, model_width), whole),
        ],
        out_specs=[wide, wide, pl.BlockSpec((3, model_width), whole)],
        out_shape=[
            jax.ShapeDtypeStruct((tokens, model_width), WIDE),
            jax.ShapeDtypeStruct((tokens, model_width), LOW),
            jax.ShapeDtypeStruct((3, model_width), WIDE),
        ],
        cost_estimate=BRIEF,
        name="first_back",
    )(grad_inner, weight, grad_second, value, gain)


class Wires:
    def __init__(self, fsdp_count):
        self.fsdp_count = fsdp_count
        self.total = 4 * fsdp_count
        self.shard = lax.axis_index("fsdp")
        rep = lax.axis_index("rep")
        self.x = rep >> 1
        self.core = rep & 1
        self.meta = jnp.stack([self.shard, self.x, self.core]).astype(jnp.int32)

    def swap(self, value, mask):
        return lax.ppermute(value, AXES, [(i, i ^ mask) for i in range(self.total)])

    def own_half(self, low, high):
        return jnp.where(self.core == 1, high, low)

    def other_half(self, low, high):
        return jnp.where(self.core == 1, low, high)

    def own_rows(self, value, axis=0):
        half = value.shape[axis] // 2
        low = lax.slice_in_dim(value, 0, half, axis=axis)
        high = lax.slice_in_dim(value, half, 2 * half, axis=axis)
        return jnp.where(self.x == 1, high, low), jnp.where(self.x == 1, low, high)

    def near(self, value):
        return [self.swap(value, 8 * k) for k in range(1, self.fsdp_count // 2)]

    def share(self, near):
        return near + [self.swap(v, 1) for v in near]


    def y_halves(self, held):
        held = held.reshape((held.shape[0] // 2, 2) + held.shape[1:])
        flag = (self.shard & 1) != 0
        return jnp.where(flag, held[:, 1], held[:, 0]), jnp.where(flag, held[:, 0], held[:, 1])

    def z_block(self, held, k):
        return lax.dynamic_index_in_dim(held, (self.shard >> 1) ^ k, 0, keepdims=False)

    def z_sends(self, held):
        if held.shape[0] > 4:
            return [held]
        return [self.z_block(held, k) for k in range(1, held.shape[0])]

    def z_swap(self, sends):
        if sends[0].ndim == 2:
            return [self.swap(v, 8 * (k + 1)) for k, v in enumerate(sends)]
        held, bit = sends[0], 2
        while bit < self.fsdp_count:
            held = held.reshape((held.shape[0] // 2, 2) + held.shape[1:])
            flag = (self.shard & bit) != 0
            got = self.swap(jnp.where(flag, held[:, 0], held[:, 1]), 4 * bit)
            held = add_low(jnp.where(flag, held[:, 1], held[:, 0]), got)
            bit *= 2
        return [held[0]]

    def z_sum(self, held, got):
        if held.shape[0] > 4:
            return got[0]
        return add_low(self.z_block(held, 0), *got)

    def by_x(self, own, other):
        return jnp.where(self.x == 1, other, own), jnp.where(self.x == 1, own, other)


def tie(*values):
    return lax.optimization_barrier(values)


def join(*parts):
    return jnp.concatenate(parts, axis=0)


def row(vector):
    return vector.reshape(1, -1).astype(WIDE)


def add_low(first, *others):
    total = first.astype(WIDE)
    for other in others:
        total = total + other.astype(WIDE)
    return total.astype(LOW)


def weight_copies(meta_ref, refs, out_ref, sem, parts, half_width):
    at = 0
    copies = []
    for width, start, by_x, offset, row in parts:
        for core, x, y in itertools.product(range(2), range(2 if by_x else 1), range(2)):
            piece = refs[at]
            at += 1
            col = (meta_ref[2] ^ core) * half_width + offset
            begin = start
            if by_x:
                col = col + (meta_ref[1] ^ x) * width
                begin = start[x]
            col = pl.multiple_of(col, LANES)
            rows = slice(row, row + piece.shape[1])
            for j in range(piece.shape[0]):
                copies.append(
                    pltpu.make_async_copy(
                        piece.at[j, :, pl.ds(begin, width)],
                        out_ref.at[meta_ref[0] ^ (2 * j + y), rows, pl.ds(col, width)],
                        sem,
                    )
                )
    return copies


def assemble_kernel(meta_ref, *refs, parts, half_width):
    copies = weight_copies(meta_ref, refs, refs[-2], refs[-1], parts, half_width)
    for copy in copies:
        copy.start()
    for copy in copies:
        copy.wait()


def project(inputs, weight_ref, query_ref, value_ref, out_ref, pairs):
    group = 3 * LANES
    step = 256
    for i, p in enumerate(pairs):
        cut = slice(i * group, (i + 1) * group)
        weight = weight_ref[..., cut].reshape(inputs.shape[1], group)
        bias = jnp.concatenate(
            [query_ref[p : p + 1], jnp.zeros((1, LANES), WIDE), value_ref[p : p + 1]], axis=1
        )
        for t in range(0, inputs.shape[0], step):
            out = lax.dot_general(inputs[t : t + step], weight, NN, preferred_element_type=WIDE)
            out_ref[t : t + step, cut] = (out + bias).astype(LOW)


def project_kernel(meta_ref, inputs_ref, query_ref, value_ref, *refs, parts, half_width, pairs):
    full_ref, out_ref, sem = refs[-3:]
    copies = weight_copies(meta_ref, refs, full_ref, sem, parts, half_width)
    for copy in copies:
        copy.start()
    for copy in copies:
        copy.wait()
    project(inputs_ref, full_ref, query_ref, value_ref, out_ref, pairs)


def project_whole_kernel(inputs_ref, query_ref, value_ref, full_ref, *refs, pairs):
    project(inputs_ref, full_ref, query_ref, value_ref, refs[-1], pairs)


def joint_project(wires, inputs, pieces, query_bias, value_bias, chunk, shard_rows, behind=()):
    tokens, model_width = inputs.shape
    half_width = chunk.count * 3 * LANES
    out_shape = jax.ShapeDtypeStruct((tokens, 2 * half_width), LOW)
    on_chip = pl.BlockSpec(memory_space=pltpu.VMEM)
    anywhere = pl.BlockSpec(memory_space=pl.ANY)
    cost = BRIEF
    if not isinstance(pieces, list):
        out = pl.pallas_call(
            functools.partial(project_whole_kernel, pairs=chunk.pairs),
            out_shape=out_shape,
            in_specs=[on_chip] * 4 + [anywhere] * len(behind),
            out_specs=on_chip,
            cost_estimate=cost,
            name="joint_project",
        )(inputs, query_bias, value_bias, pieces, *behind)
        return pieces, out
    full, out = pl.pallas_call(
        functools.partial(
            project_kernel,
            parts=[(half_width, 0, False, 0, 0)],
            half_width=half_width,
            pairs=chunk.pairs,
        ),
        out_shape=[
            jax.ShapeDtypeStruct((wires.fsdp_count, shard_rows, 2 * half_width), LOW),
            out_shape,
        ],
        in_specs=[pl.BlockSpec(memory_space=pltpu.SMEM)]
        + [on_chip] * 3
        + [anywhere] * (len(pieces) + len(behind)),
        out_specs=[on_chip] * 2,
        scratch_shapes=[pltpu.SemaphoreType.DMA],
        cost_estimate=cost,
        name="joint_project",
    )(wires.meta, inputs, query_bias, value_bias, *pieces, *behind)
    return full.reshape(model_width, 2 * half_width), out


def pack_kernel(*refs, chunks, wide):
    *vector_refs, out_ref = refs
    sum_refs, vector_refs = vector_refs[: len(chunks)], vector_refs[len(chunks) :]
    out_ref[...] = jnp.zeros_like(out_ref)
    for ref, chunk in zip(sum_refs, chunks):
        for i, p in enumerate(chunk.pairs):
            total = ref[0, i, 0:1]
            for r in range(1, ref.shape[0]):
                total = total + ref[r, i, 0:1]
            out_ref[0:1, p * LANES : (p + 1) * LANES] = total[:, :LANES]
            out_ref[1:2, p * LANES : (p + 1) * LANES] = total[:, 2 * LANES :]
    row = 2
    for ref in vector_refs:
        for r, start in itertools.product(range(ref.shape[0]), range(0, ref.shape[1], wide)):
            out_ref[row : row + 1] = ref[r : r + 1, start : start + wide]
            row += 1


def pack(sums, chunks, vectors, wide):
    rows = 2 + sum(v.shape[0] * v.shape[1] // wide for v in vectors)
    return pl.pallas_call(
        functools.partial(pack_kernel, chunks=chunks, wide=wide),
        out_shape=jax.ShapeDtypeStruct(((rows + 7) // 8 * 8, wide), WIDE),
        name="pack",
    )(*sums, *vectors)


def assemble(wires, shard_rows, half_width, parts):
    count = wires.fsdp_count
    operands, plan = [], []
    for pieces, *where in parts:
        plan.append(where)
        operands += pieces
    shape = (count, shard_rows, 2 * half_width)
    full = pl.pallas_call(
        functools.partial(assemble_kernel, parts=plan, half_width=half_width),
        out_shape=jax.ShapeDtypeStruct(shape, LOW),
        in_specs=[pl.BlockSpec(memory_space=pltpu.SMEM)]
        + [pl.BlockSpec(memory_space=pl.ANY)] * len(operands),
        out_specs=pl.BlockSpec(memory_space=pltpu.VMEM),
        scratch_shapes=[pltpu.SemaphoreType.DMA],
        cost_estimate=BRIEF,
        name="assemble",
    )(wires.meta, *operands)
    return full.reshape(count * shard_rows, 2 * half_width)


def pieces_kernel(meta_ref, weight_ref, *out_refs, chunks):
    model_width = weight_ref.shape[1] // 3
    for chunk, out_ref in zip(chunks, out_refs):
        for i, part in itertools.product(range(chunk.count), range(3)):
            pair = meta_ref[2] * chunk.half + chunk.first + i
            col = pl.multiple_of(part * model_width + pair * LANES, LANES)
            place = (3 * i + part) * LANES
            out_ref[:, place : place + LANES] = weight_ref[:, pl.ds(col, LANES)]


def own_pairs(wires, weight, chunks):
    return pl.pallas_call(
        functools.partial(pieces_kernel, chunks=chunks),
        out_shape=[
            jax.ShapeDtypeStruct((weight.shape[0], c.count * 3 * LANES), LOW) for c in chunks
        ],
        in_specs=[
            pl.BlockSpec(memory_space=pltpu.SMEM),
            pl.BlockSpec(memory_space=pltpu.VMEM),
        ],
        out_specs=[pl.BlockSpec(memory_space=pltpu.VMEM)] * len(chunks),
        cost_estimate=BRIEF,
        name="own_pairs",
    )(wires.meta, weight)


def pair_columns(array, pairs, model_width):
    return jnp.concatenate(
        [
            array[..., part * model_width + p * LANES : part * model_width + (p + 1) * LANES]
            for p in pairs
            for part in range(3)
        ],
        axis=-1,
    )


def natural_columns(pieces, chunks):
    where = {}
    for piece, chunk in zip(pieces, chunks):
        for i, p in enumerate(chunk.pairs):
            for part in range(3):
                place = (3 * i + part) * LANES
                where[(part, p)] = piece[..., place : place + LANES]
    return jnp.concatenate([where[key] for key in sorted(where)], axis=-1)


def body(
    fsdp_count,
    layer_input,
    segment_ids,
    joint_weight,
    query_bias,
    value_bias,
    close_weight,
    close_bias,
    first_gain,
    first_shift,
    expand_weight,
    expand_bias,
    shrink_weight,
    shrink_bias,
    second_gain,
    second_shift,
    cotangent,
):
    row_count, pos_count, model_width = layer_input.shape
    hidden_units = expand_bias.shape[0]
    tok_count = row_count * pos_count
    flat_input = layer_input.reshape(tok_count, model_width)
    wires = Wires(fsdp_count)
    half_pairs = model_width // LANES // 2
    chunks = (Chunk(0, 1, half_pairs), Chunk(1, half_pairs - 1, half_pairs))
    shard_rows = joint_weight.shape[0]

    half_model, half_hidden = model_width // 2, hidden_units // 2
    unit = half_hidden // 3
    expand_half = wires.own_half(expand_weight[:, :half_hidden], expand_weight[:, half_hidden:])
    close_half = wires.own_half(close_weight[:, :half_model], close_weight[:, half_model:])
    shrink_half = wires.own_half(shrink_weight[:, :half_model], shrink_weight[:, half_model:])
    shrink_rows = shrink_half.shape[0] // 2
    aligned = fsdp_count == 8 and shard_rows % 32 == 0
    query_rows = query_bias.astype(WIDE).reshape(-1, LANES)
    value_rows = value_bias.astype(WIDE).reshape(-1, LANES)

    inputs_t = jnp.swapaxes(layer_input, 1, 2)
    lines = [
        row(v)
        for v in (
            close_bias,
            first_gain,
            first_shift,
            expand_bias,
            shrink_bias,
            second_gain,
            second_shift,
        )
    ]
    segments = segment_ids[:, :, None], segment_ids[:, None, :]

    def project_and_attend(place, shared, context):
        full, part = joint_project(
            wires, flat_input, shared, query_rows, value_rows, chunks[place], shard_rows
        )
        return full, part.reshape(row_count, pos_count, -1)

    if aligned:
        first, second = (v[None] for v in own_pairs(wires, joint_weight, chunks))
        split = wires.by_x(expand_half[:, unit : 2 * unit], expand_half[:, 2 * unit :])[0]
        piece = jnp.concatenate([expand_half[:, :unit], close_half, split], axis=1)[None]
        shrink = shrink_half[None]
        first_near = wires.near(first)
        ready = [inputs_t, query_rows, value_rows, *segments]
        first, first_near, ready = lax.optimization_barrier((first, first_near, ready))
        inputs_t, query_rows, value_rows, *segments = ready
        first = join(first, *first_near)
        first, second = tie(first, second)
        first_y = wires.swap(first, 4)
        second_near = wires.near(second)
        first, first_y, second_near[0], second_near[1] = tie(
            first, first_y, second_near[0], second_near[1]
        )
        first_shared = wires.share([first, first_y])
        first_shared, piece, second, second_near = lax.optimization_barrier(
            (first_shared, piece, second, second_near)
        )
        second = join(second, *second_near)
        second_y = wires.swap(second, 4)
        piece_near = wires.near(piece)
        full, part = project_and_attend(0, first_shared, None)
        joint_full, mixed = [full], [part]
        context, w, inv = attend(mixed[0], segments, chunks[0])
        weights, inverse = [w], [inv]
        context, second, second_y, piece_near[0], piece_near[1] = tie(
            context, second, second_y, piece_near[0], piece_near[1]
        )
        second_shared = wires.share([second, second_y])
        second_shared, piece, shrink, piece_near, lines = lax.optimization_barrier(
            (second_shared, piece, shrink, piece_near, lines)
        )
        piece = join(piece, *piece_near)
        split = piece[..., unit + half_model :]
        piece, split = tie(piece, split)
        piece_y = wires.swap(piece, 4)
        split_x = wires.swap(split, 2)
        shrink_near = wires.near(shrink)
        full, part = project_and_attend(1, second_shared, context)
        joint_full.append(full)
        part, split, split_x = tie(part, split, split_x)
        mixed.append(part)
        context, w, inv = attend(mixed[1], segments, chunks[1], context)
        weights.append(w)
        inverse.append(inv)
        context, piece, piece_y, shrink, *shrink_near = tie(
            context, piece, piece_y, shrink, *shrink_near
        )
        plain_shared = wires.share([piece, piece_y])
        split_yx = wires.swap(piece_y[..., unit + half_model :], 2)
        shrink = join(shrink, *shrink_near)
        *plain_shared, shrink = tie(*plain_shared, shrink)
        shrink_y = wires.swap(shrink, 4)
        close_full = assemble(
            wires, shard_rows, half_model, [(plain_shared, half_model, unit, False, 0, 0)]
        )
    else:
        joint_full, mixed, weights, inverse = [], [], [], []
        context = None
        for place, chunk in enumerate(chunks):
            shared = lax.all_gather(
                pair_columns(joint_weight, chunk.pairs, model_width), "fsdp", axis=0, tiled=True
            )
            full, part = project_and_attend(place, shared, context)
            joint_full.append(full)
            mixed.append(part)
            context, w, inv = attend(part, segments, chunk, context)
            weights.append(w)
            inverse.append(inv)
        close_full, expand_full, shrink_full = (
            lax.all_gather(w, "fsdp", axis=0, tiled=True)
            for w in (close_weight, expand_weight, shrink_weight)
        )
    context_low = context.reshape(tok_count, model_width)

    first_sum, hidden_low = first_norm(
        context_low, close_full, lines[0], flat_input, lines[1], lines[2]
    )
    if aligned:
        own, other = plain_shared[:2], plain_shared[2:]
        hidden_low, split_x, split_yx = tie(hidden_low, split_x, split_yx)
        split_shared = wires.share([split_x, split_yx])
        expand_full = assemble(
            wires,
            shard_rows,
            half_hidden,
            [
                (plain_shared, unit, 0, False, 0, 0),
                (
                    [*own, *split_shared[:2], *other, *split_shared[2:]],
                    unit,
                    [unit + half_model, 0],
                    True,
                    unit,
                    0,
                ),
            ],
        )
    active_low, slope = expand_gelu(hidden_low, expand_full, lines[3])
    if aligned:
        shrink_core = wires.swap(shrink, 1)
        active_low, shrink, shrink_y, shrink_core = tie(
            active_low, shrink, shrink_y, shrink_core
        )
        shrink_shared = [shrink, shrink_y, shrink_core, wires.swap(shrink_y, 1)]
        shrink_full = assemble(
            wires,
            shrink_weight.shape[0],
            half_model,
            [(shrink_shared, half_model, 0, False, 0, 0)],
        )
    layer_output, grad_second, grad_ffn, second_sums = second_norm(
        active_low,
        shrink_full,
        lines[4],
        first_sum,
        lines[1],
        lines[2],
        lines[5],
        lines[6],
        cotangent.reshape(tok_count, model_width),
    )
    layer_output = layer_output.reshape(row_count, pos_count, model_width)

    def outgoing(left, right):
        half = right.shape[1] // 2
        send = wires.other_half(right[:, :half], right[:, half:])
        return jnp.einsum("tf,td->fd", left, send, preferred_element_type=WIDE).astype(LOW)

    def kept(left, right):
        half = right.shape[1] // 2
        keep = wires.own_half(right[:, :half], right[:, half:])
        return jnp.einsum("tf,td->fd", left, keep, preferred_element_type=WIDE)

    def by_shard(held):
        return held.reshape(fsdp_count, held.shape[0] // fsdp_count, held.shape[1])

    def staying(left, right, got):
        return by_shard(add_low(kept(left, right), got))

    def both_halves(mine):
        other = wires.swap(mine, 1)
        return wires.own_half(mine, other), wires.own_half(other, mine)

    shrink_send = outgoing(active_low, grad_ffn)
    active_low, shrink_send = tie(active_low, shrink_send)
    shrink_got = wires.swap(shrink_send, 1)
    shrink_keep = kept(active_low, grad_ffn)
    grad_ffn, shrink_keep, shrink_got = tie(grad_ffn, shrink_keep, shrink_got)
    shrink_held = by_shard(add_low(shrink_keep, shrink_got))
    top_keep, top_send = wires.y_halves(shrink_held[:, :shrink_rows])
    low_keep, low_send = wires.own_rows(shrink_held[:, shrink_rows:], axis=1)
    grad_ffn, top_keep, top_send, low_keep, low_send = tie(
        grad_ffn, top_keep, top_send, low_keep, low_send
    )
    top_got = wires.swap(top_send, 4)
    low_got = wires.swap(low_send, 2)
    grad_inner, inner_sum = inner_grad(grad_ffn, shrink_full, slope)
    grad_inner, top_keep, top_got, low_keep, low_got = tie(
        grad_inner, top_keep, top_got, low_keep, low_got
    )
    low_keep, low_send = wires.y_halves(add_low(low_keep, low_got))
    top_held = add_low(top_keep, top_got)
    hidden_low, low_keep, low_send = tie(hidden_low, low_keep, low_send)
    low_got = wires.swap(low_send, 4)
    expand_send = outgoing(hidden_low, grad_inner)
    hidden_low, expand_send = tie(hidden_low, expand_send)
    expand_got = wires.swap(expand_send, 1)
    expand_keep = kept(hidden_low, grad_inner)
    grad_inner, expand_keep, expand_got = tie(grad_inner, expand_keep, expand_got)
    expand_held = by_shard(add_low(expand_keep, expand_got))
    quarter = half_hidden // 2
    left_keep, left_send = wires.y_halves(expand_held[..., :quarter])
    right_keep, right_send = wires.by_x(
        expand_held[..., quarter : quarter + quarter // 2],
        expand_held[..., quarter + quarter // 2 :],
    )
    (
        grad_inner,
        left_keep,
        left_send,
        right_keep,
        right_send,
        low_keep,
        low_got,
        top_held,
        *top_sends,
    ) = tie(
        grad_inner,
        left_keep,
        left_send,
        right_keep,
        right_send,
        low_keep,
        low_got,
        top_held,
        *wires.z_sends(top_held),
    )
    top_got = wires.z_swap(top_sends)
    left_got = wires.swap(left_send, 4)
    right_got = wires.swap(right_send, 2)
    grad_first, grad_branch, first_sums = first_back(
        grad_inner, expand_full, grad_second, first_sum, lines[1]
    )
    grad_branch, left_keep, left_got, right_keep, right_got, top_held, *top_got = tie(
        grad_branch, left_keep, left_got, right_keep, right_got, top_held, *top_got
    )
    right_held = add_low(right_keep, right_got)
    top_mine = wires.z_sum(top_held, top_got)
    mid_held = jnp.concatenate([add_low(left_keep, left_got), add_low(low_keep, low_got)], axis=2)
    context_low, grad_branch = tie(context_low, grad_branch)
    close_send = outgoing(context_low, grad_branch)
    grad_branch, close_send = tie(grad_branch, close_send)
    close_got = wires.swap(close_send, 1)
    grad_context = jnp.einsum(
        "te,de->td", grad_branch, close_full, preferred_element_type=WIDE
    ).astype(LOW)
    context_low, grad_context, close_got = tie(context_low, grad_context, close_got)
    close_held = staying(context_low, grad_branch, close_got)
    grad_context = grad_context.reshape(row_count, pos_count, model_width)
    close_keep, close_send = wires.y_halves(jnp.concatenate([right_held, close_held], axis=2))
    (
        grad_context,
        close_keep,
        close_send,
        top_mine,
        mid_held,
        *mid_sends,
    ) = tie(
        grad_context,
        close_keep,
        close_send,
        top_mine,
        mid_held,
        *wires.z_sends(mid_held),
    )
    top_other = wires.swap(top_mine, 2)
    close_got = wires.swap(close_send, 4)
    mid_got = wires.z_swap(mid_sends)

    grad_mixed, bias_sums, joint_parts = {}, {}, {}
    grad_mixed[1], bias_sums[1], joint_parts[1] = attend_back(
        mixed[1], weights[1], context, inverse[1], grad_context, inputs_t, chunks[1]
    )
    grad_mixed[1] = grad_mixed[1].reshape(tok_count, -1)
    large, close_keep, close_got, top_mine, top_other, mid_held, *mid_got = tie(
        joint_parts[1], close_keep, close_got, top_mine, top_other, mid_held, *mid_got
    )
    large_got = wires.swap(wires.other_half(large[0], large[1]), 1)
    second_held = add_low(close_keep, close_got)
    large, large_got, second_held, *second_sends = tie(
        large, large_got, second_held, *wires.z_sends(second_held)
    )
    second_got = wires.z_swap(second_sends)
    large_keep, large_send = wires.own_rows(
        by_shard(add_low(wires.own_half(large[0], large[1]), large_got)), axis=1
    )
    grad_context, large_keep, large_send = tie(grad_context, large_keep, large_send)
    large_got = wires.swap(large_send, 2)
    grad_mixed[0], bias_sums[0], joint_parts[0] = attend_back(
        mixed[0], weights[0], context, inverse[0], grad_context, inputs_t, chunks[0]
    )
    grad_mixed[0] = grad_mixed[0].reshape(tok_count, -1)
    small, large_keep, large_got, second_held, *second_got = tie(
        joint_parts[0], large_keep, large_got, second_held, *second_got
    )
    small_got = wires.swap(wires.other_half(small[0], small[1]), 1)

    packed = pack(
        [bias_sums[0], bias_sums[1]],
        chunks,
        [
            first_sums,
            second_sums,
            inner_sum,
        ],
        model_width,
    )

    large_keep, large_send = wires.y_halves(add_low(large_keep, large_got))
    small, small_got, packed, large_keep, large_send = tie(
        small, small_got, packed, large_keep, large_send
    )
    large_got = wires.swap(large_send, 4)
    vector_got = wires.swap(packed, 1)
    small_keep, small_send = wires.y_halves(
        by_shard(add_low(wires.own_half(small[0], small[1]), small_got))
    )
    small_keep, small_send, packed, vector_got = tie(small_keep, small_send, packed, vector_got)
    small_got = wires.swap(small_send, 4)
    packed = packed + vector_got
    mine = jnp.concatenate(
        [wires.z_sum(mid_held, mid_got), wires.z_sum(second_held, second_got)], axis=1
    )
    grad_mixed[0], grad_mixed[1], packed, mine = tie(grad_mixed[0], grad_mixed[1], packed, mine)
    other = wires.swap(mine, 2)
    vector_got = wires.swap(packed, 8)
    input_grad = grad_first + jnp.einsum(
        "te,de->td", grad_mixed[0], joint_full[0], preferred_element_type=WIDE
    )
    input_grad, packed, vector_got = tie(input_grad, packed, vector_got)
    packed = packed + vector_got
    vector_got = wires.swap(packed, 16)
    input_grad = input_grad + jnp.einsum(
        "te,de->td", grad_mixed[1], joint_full[1], preferred_element_type=WIDE
    )
    input_grad, small_keep, small_got, large_keep, large_got, packed, vector_got, mine, other = tie(
        input_grad, small_keep, small_got, large_keep, large_got, packed, vector_got, mine, other
    )
    small_held = add_low(small_keep, small_got)
    half_rows = small_held.shape[1] // 2
    joint_held = jnp.concatenate(
        [small_held[:, :half_rows], small_held[:, half_rows:], add_low(large_keep, large_got)],
        axis=2,
    )
    packed = packed + vector_got
    packed, joint_held, *joint_sends = tie(packed, joint_held, *wires.z_sends(joint_held))
    joint_got = wires.z_swap(joint_sends)
    vector_got = wires.swap(packed, 4)
    top_mine = add_low(top_mine, top_other)
    total = add_low(mine, other)
    cuts = [quarter, quarter + half_model, quarter + half_model + quarter // 2]
    left, _, _, close = jnp.split(total, cuts, axis=1)
    (_, low, right, _), (_, low_other, right_other, _) = (
        jnp.split(v, cuts, axis=1) for v in (mine, other)
    )
    shrink_mine = jnp.concatenate([top_mine, *wires.by_x(low, low_other)], axis=0)
    second_mine = jnp.concatenate([left, *wires.by_x(right, right_other), close], axis=1)
    shrink_grad = jnp.concatenate(both_halves(shrink_mine), axis=1).astype(WIDE)
    low, high = both_halves(second_mine)
    cut = hidden_units // 2
    expand_grad = jnp.concatenate([low[:, :cut], high[:, :cut]], axis=1).astype(WIDE)
    close_grad = jnp.concatenate([low[:, cut:], high[:, cut:]], axis=1).astype(WIDE)
    joint_held, packed, vector_got, shrink_grad, expand_grad, close_grad, *joint_got = tie(
        joint_held, packed, vector_got, shrink_grad, expand_grad, close_grad, *joint_got
    )
    joint_mine, packed = tie(wires.z_sum(joint_held, joint_got), packed + vector_got)

    joint_other = wires.swap(joint_mine, 2)
    vector_got = wires.swap(packed, 2)
    joint_mine, joint_other, packed, vector_got = tie(
        joint_mine, joint_other, packed, vector_got
    )
    small_width = small_held.shape[2]
    small_mine = add_low(joint_mine[:, : 2 * small_width], joint_other[:, : 2 * small_width])
    joint_mine = jnp.concatenate(
        [
            jnp.concatenate([small_mine[:, :small_width], small_mine[:, small_width:]], axis=0),
            jnp.concatenate(
                wires.by_x(joint_mine[:, 2 * small_width :], joint_other[:, 2 * small_width :]),
                axis=0,
            ),
        ],
        axis=1,
    )

    joint_mine, summed = tie(joint_mine, packed + vector_got)
    low, high = both_halves(joint_mine)
    mask = 32
    while mask < wires.total:
        summed = summed + wires.swap(summed, mask)
        mask *= 2
    cut = chunks[0].count * 3 * LANES
    joint_grad = natural_columns(
        [
            jnp.concatenate([low[:, :cut], high[:, :cut]], axis=1),
            jnp.concatenate([low[:, cut:], high[:, cut:]], axis=1),
        ],
        chunks,
    ).astype(WIDE)
    (
        query_bias_grad,
        value_bias_grad,
        close_bias_grad,
        first_gain_grad,
        first_shift_grad,
        shrink_bias_grad,
        second_gain_grad,
        second_shift_grad,
    ) = (summed[i] for i in range(8))
    expand_bias_grad = summed[8 : 8 + hidden_units // model_width].reshape(hidden_units)
    return (
        layer_output,
        input_grad.reshape(row_count, pos_count, model_width),
        joint_grad,
        query_bias_grad,
        value_bias_grad,
        close_grad,
        close_bias_grad,
        first_gain_grad,
        first_shift_grad,
        expand_grad,
        expand_bias_grad,
        shrink_grad,
        shrink_bias_grad,
        second_gain_grad,
        second_shift_grad,
    )


def solution(mesh):
    rows = P(("fsdp", "rep"), None, None)
    sharded = P("fsdp", None)
    copied = P()
    return jax.shard_map(
        functools.partial(body, mesh.shape["fsdp"]),
        mesh=mesh,
        in_specs=(
            rows,
            P(("fsdp", "rep"), None),
            sharded,
            copied,
            copied,
            sharded,
            copied,
            copied,
            copied,
            sharded,
            copied,
            sharded,
            copied,
            copied,
            copied,
            rows,
        ),
        out_specs=(
            rows,
            rows,
            sharded,
            copied,
            copied,
            sharded,
            copied,
            copied,
            copied,
            sharded,
            copied,
            sharded,
            copied,
            copied,
            copied,
        ),
        check_vma=False,
    )
```
